512 devices in a mesh: dp: 32 (over z, x), seq: 8 (over y_hi, core), sect: 2 (over y_lo).
Axes of the slice: x: 4, y: 8 (y_hi: 4, y_lo: 2; y = y_hi * 2 + y_lo), z: 8, core: 2. Of those that a mesh axis runs over, the one named last changes fastest.
Arguments:
- bases: int32 [64, 2048], P(('dp', 'sect'), 'seq'), may hold values from 0 to 3
- embed: bfloat16 [5, 4, 384], replicated, may hold values from -2.5 to 2.5
- conv_w: bfloat16 [5, 384, 384], P(None, 'seq'), may hold values from -0.125 to 0.125
- w_in: bfloat16 [384, 768], P('seq', 'sect'), may hold values from -0.3125 to 0.3125
- w_out: bfloat16 [768, 384], P('sect', 'seq'), may hold values from -0.21875 to 0.21875
- cotangent: bfloat16 [64, 2048, 384], P(('dp', 'sect'), 'seq'), may hold values from -0.0390625 to 0.0390625
Outputs:
- output: bfloat16 [64, 2048, 384], P(('dp', 'sect'), 'seq')
- grad_embed: float32 [5, 4, 384], P(None, None, 'seq')
- grad_conv: float32 [5, 384, 384], P(None, 'seq')
- grad_in: float32 [384, 768], P('seq', 'sect')
- grad_out: float32 [768, 384], P('sect', 'seq')
The draws below stay inside these ranges and needn't reach their ends.
All inputs are finite; a program needn't handle non-finite values.
Results may differ from the reference program's by a relative error of at most 0.0088.
Values may be sent and summed in bfloat16 or wider, within the bound.
No kernel may reach another device: no remote copies, remote signals or barrier semaphores. Data moves between devices by JAX's collectives and lax.ppermute only.
A program may use at most 64 MiB of HBM per device.

```python
import jax
import jax.numpy as jnp
from jax import lax

C = 384
F = 768
TAPS = 5
BASES = 4
LENGTH = 2048
SAMPLES = 64


def set_ends(result, stream_key, smallest, largest):
    extent = result.shape
    place = [jax.random.randint(jax.random.fold_in(stream_key, axis), (), 0, extent[axis]) for axis in range(len(extent))]
    result = result.at[tuple(place)].set(smallest)
    longest = extent.index(max(extent))
    place[longest] = (place[longest] + 1) % extent[longest]
    return result.at[tuple(place)].set(largest)


def block_scale(key, shape, cuts, least, high):
    def one(position, parts):
        steps = jax.random.uniform(jax.random.fold_in(jax.random.fold_in(key, 6), position), (parts,), jnp.float32, least / len(cuts), high / len(cuts))
        return jnp.repeat(jnp.exp(steps), shape[position] // parts).reshape((-1,) + (1,) * (len(shape) - position - 1))

    level = one(*cuts[0])
    for cut in cuts[1:]:
        level = level * one(*cut)
    return level


def noise(rng, dims, width, limit, shards=(), kind=jnp.bfloat16):
    level = block_scale(rng, dims, shards, -0.22, 0.18) if shards else 1.0
    drawn = jax.random.normal(rng, dims, jnp.float32) * width * level
    return jnp.minimum(jnp.maximum(drawn, -limit), limit).astype(kind)


def setup_inputs(seed: int = 0) -> dict:
    key_list = jax.random.split(jax.random.key(seed), 7)
    bases = set_ends(jax.random.randint(key_list[0], (SAMPLES, LENGTH), 0, 4), jax.random.fold_in(key_list[0], 1), 0, 3).astype(jnp.int32)
    embed = noise(key_list[1], (TAPS, BASES, C), TAPS ** -0.5, 2.5)
    conv_w = noise(key_list[2], (TAPS, C, C), (TAPS * C) ** -0.5, 0.125, ((1, 8),))
    w_in = noise(key_list[3], (C, F), C ** -0.5, 0.3125, ((0, 8), (1, 2)))
    w_out = noise(key_list[4], (F, C), F ** -0.5, 0.21875, ((0, 2), (1, 8)))
    cotangent = noise(key_list[5], (SAMPLES, LENGTH, C), (1.0 / (LENGTH * SAMPLES) ** 0.5), 0.0390625, ((0, 64), (1, 8)))
    return dict(bases=bases, embed=embed, conv_w=conv_w, w_in=w_in, w_out=w_out, cotangent=cotangent)


def gelu_tanh(value):
    return jax.nn.gelu(value, approximate=True)

def gelu_back(value, grad):
    unused, pull = jax.vjp(gelu_tanh, value)
    return pull(grad)[0]

def contract_rows(left, right):
    return lax.dot_general(left, right, (((0,), (0,)), ((), ())), preferred_element_type=jnp.float32)

def contract_cols(left, right):
    return lax.dot_general(left, right, (((1,), (1,)), ((), ())), preferred_element_type=jnp.float32)

def one_sample(ids, embed, conv_w, w_in, w_out, cot):
    rows = ids.shape[0]
    chans = embed.shape[2]
    padded_ids = jnp.pad(ids + 1, 2)
    levels = jnp.arange(1, BASES + 1, dtype=jnp.int32)
    onehots = [(padded_ids[k:k + rows, None] == levels[None, :]).astype(jnp.bfloat16) for k in range(TAPS)]
    accum = jnp.zeros((rows, chans), jnp.float32)
    for k in range(TAPS):
        accum = accum + jnp.dot(onehots[k], embed[k], preferred_element_type=jnp.float32)
    h_zero = accum.astype(jnp.bfloat16)
    h_padded = jnp.pad(h_zero, ((2, 2), (0, 0)))
    pre_conv = jnp.zeros((rows, chans), jnp.float32)
    for k in range(TAPS):
        pre_conv = pre_conv + jnp.dot(h_padded[k:k + rows], conv_w[k], preferred_element_type=jnp.float32)
    h_one = lax.optimization_barrier((h_zero.astype(jnp.float32) + gelu_tanh(pre_conv)).astype(jnp.bfloat16))
    h_onef = h_one.astype(jnp.float32)
    pooled = lax.optimization_barrier((h_onef.reshape(rows // 2, 2, chans).sum(1) * 0.5).astype(jnp.bfloat16))
    pooledf = pooled.astype(jnp.float32)
    scale = lax.rsqrt(lax.optimization_barrier(jnp.mean(pooledf * pooledf, axis=-1, keepdims=True)) + 1e-06)
    normed = (pooledf * scale).astype(jnp.bfloat16)
    pre = jnp.dot(normed, w_in, preferred_element_type=jnp.float32)
    act = gelu_tanh(pre).astype(jnp.bfloat16)
    mixed = lax.optimization_barrier(jnp.dot(act, w_out, preferred_element_type=jnp.float32).astype(jnp.bfloat16))
    output = (h_onef + jnp.repeat(mixed.astype(jnp.float32), 2, axis=0)).astype(jnp.bfloat16)
    dout = cot.astype(jnp.float32)
    dmixed = dout.reshape(rows // 2, 2, chans).sum(1).astype(jnp.bfloat16)
    grad_out = contract_rows(act, dmixed)
    dact = contract_cols(dmixed, w_out)
    dpre = gelu_back(pre, dact).astype(jnp.bfloat16)
    grad_in = contract_rows(normed, dpre)
    dnormed = contract_cols(dpre, w_in)
    dpooled = scale * dnormed - pooledf * scale ** 3 * lax.optimization_barrier(jnp.mean(dnormed * pooledf, axis=-1, keepdims=True))
    dh_one = dout + jnp.repeat(dpooled * 0.5, 2, axis=0)
    dz_rows = gelu_back(pre_conv, dh_one).astype(jnp.bfloat16)
    dz_padded = jnp.pad(dz_rows, ((2, 2), (0, 0)))
    dh_zero = dh_one
    for k in range(TAPS):
        dh_zero = dh_zero + contract_cols(dz_padded[4 - k:4 - k + rows], conv_w[k])
    grad_conv = jnp.stack([contract_rows(h_padded[k:k + rows], dz_rows) for k in range(TAPS)])
    grad_embed = jnp.stack([lax.dot_general(onehots[k].astype(jnp.float32), dh_zero, (((0,), (0,)), ((), ())), precision=lax.Precision.HIGHEST, preferred_element_type=jnp.float32) for k in range(TAPS)])
    return (output, grad_embed, grad_conv, grad_in, grad_out)

def reference(bases, embed, conv_w, w_in, w_out, cotangent):

    def stepper(carry, item):
        ids, cot = item
        output, g_embed, g_conv, g_in, g_out = one_sample(ids, embed, conv_w, w_in, w_out, cot)
        carry = (carry[0] + g_embed, carry[1] + g_conv, carry[2] + g_in, carry[3] + g_out)
        return (carry, output)
    start = (jnp.zeros(embed.shape, jnp.float32), jnp.zeros(conv_w.shape, jnp.float32), jnp.zeros(w_in.shape, jnp.float32), jnp.zeros(w_out.shape, jnp.float32))
    totals, outputs = lax.scan(stepper, start, (bases, cotangent))
    return (outputs, totals[0], totals[1], totals[2], totals[3])
```

```python
import jax
import jax.numpy as jnp
from jax import lax
from jax.experimental import pallas as pl
from jax.experimental.pallas import tpu as pltpu
from jax.sharding import Mesh
from jax.sharding import PartitionSpec as P

Z, X, YH, CORE, YL = 8, 4, 4, 2, 2
TAPS = 5
BASES = 4
C = 384
F = 768
ROWS = 256
HALF = 128
LENGTH = 2048
SHARD = 48
PAIRS = TAPS * BASES
BF = jnp.bfloat16
F32 = jnp.float32
VMEM = pltpu.VMEM
LANES = [slice(128 * i, 128 * (i + 1)) for i in range(C // 128)]
GELU_C = 0.7978845608028654
GELU_A = 0.044715


def dot(a, b, dims):
    return lax.dot_general(a, b, (dims, ((), ())), preferred_element_type=F32)


def nn(a, b):
    return dot(a, b, ((1,), (0,)))


def nt(a, b):
    return dot(a, b, ((1,), (1,)))


def tn(a, b):
    return dot(a, b, ((0,), (0,)))


def iota(shape, dim):
    return lax.broadcasted_iota(jnp.int32, shape, dim)


def gelu_both(x):
    x2 = x * x
    t = jnp.tanh(GELU_C * (x + GELU_A * (x * x2)))
    half = 0.5 * (1.0 + t)
    slope = half + 0.5 * x * (1.0 - t * t) * (GELU_C * (1.0 + 3.0 * GELU_A * x2))
    return x * half, slope


def stack_embed(embed_ref, scratch, top):
    for j in range(TAPS):
        scratch[top + BASES * j : top + BASES * (j + 1), :] = embed_ref[j].astype(F32)


def picker(seq):
    return (iota((C, SHARD), 0) == iota((C, SHARD), 1) + seq * SHARD).astype(BF)


def pack_kernel(place, ids_ref, embed_ref, conv_ref, win_ref, wout_ref, out_ref, emb, esum):
    seq, yl = place[0], place[3]
    emb[...] = jnp.zeros_like(emb)
    esum[...] = jnp.zeros_like(esum)
    stack_embed(embed_ref, emb, 0)
    mine = nn(emb[...].astype(BF), picker(seq)).astype(BF)
    for k in range(TAPS):
        esum[PAIRS * k : PAIRS * (k + 1), :] = nn(mine, conv_ref[k])[:PAIRS]
    part = esum[pl.ds(pl.multiple_of(yl * 56, 8), 56), :]
    ids = ids_ref[...].astype(F32)
    ids = jnp.concatenate([ids, jnp.zeros((1, C - ROWS), F32)], axis=1)
    tail = jnp.concatenate([part, jnp.broadcast_to(ids, (8, C))], axis=0).astype(BF)
    for d in range(YH * YL):
        out_ref[d, 0:48, :] = win_ref[...]
        out_ref[d, 48:96, :] = wout_ref[...]
        out_ref[d, 96:160, :] = tail


def step_kernel(
    place, own, oth, ids_ref, embed_ref, cot_ref,
    out_ref, keep_ref, send_ref,
    win, wout, ebuf, embf, rows_f, grad_a, grad_b,
):
    seq, yh, core, yl = place[0], place[1], place[2], place[3]
    for h in range(YH):
        for side, ref in ((0, own), (1, oth)):
            which = core + side * (1 - 2 * core)
            top = pl.multiple_of((2 * h + which) * SHARD, SHARD)
            for half in range(YL):
                cols = slice(C * half, C * (half + 1))
                win[pl.ds(top, SHARD), cols] = ref[YL * h + half, 0:48, :]
                wout[pl.ds(top, SHARD), cols] = ref[YL * h + half, 48:96, :]
    ebuf[...] = jnp.zeros_like(ebuf)
    for half in range(YL):
        total = jnp.zeros((56, C), F32)
        for h in range(YH):
            for ref in (own, oth):
                total = total + ref[YL * h + half, 96:160, :].astype(F32)[:56]
        ebuf[56 * half : 56 * half + 56, :] = total
    embf[...] = jnp.zeros_like(embf)
    stack_embed(embed_ref, embf, TAPS * PAIRS)
    e_full = ebuf[...]
    e_hi = e_full.astype(BF)
    e_lo = (e_full - e_hi.astype(F32)).astype(BF)
    before = jnp.maximum(yh - (1 - core), 0)
    after = jnp.minimum(yh + core, YH - 1)
    id_prev = oth[YL * before + yl, 96:160, :].astype(F32)[56:64, 128:256]
    id_next = oth[YL * after + yl, 96:160, :].astype(F32)[56:64, 0:128]
    id_prev = jnp.where(seq == 0, -1.0, id_prev)
    id_next = jnp.where(seq == YH * CORE - 1, -1.0, id_next)
    id_mid = jnp.broadcast_to(ids_ref[...].astype(F32), (8, ROWS))
    line = jnp.concatenate([id_prev, id_mid, id_next], axis=1)
    m = iota((HALF, ROWS), 0)
    k = sum((m >= PAIRS * q).astype(jnp.int32) for q in range(1, TAPS + 1))
    rest = m - PAIRS * k
    k = jnp.where(m >= PAIRS * TAPS, 2, k)
    j = jnp.right_shift(rest, 2)
    base = jnp.bitwise_and(rest, 3)
    seen = jnp.full((HALF, ROWS), -2.0, F32)
    for o in range(2 * TAPS - 1):
        moved = pltpu.roll(line, (4 - o) % 512, 1)[:, 128 : 128 + ROWS]
        seen = jnp.where(k + j == o, jnp.concatenate([moved] * (HALF // 8), axis=0), seen)
    at = seq * ROWS + iota((HALF, ROWS), 1) + k - 2
    hit = (at >= 0) & (at < LENGTH) & (m < PAIRS * (TAPS + 1)) & (seen == base.astype(F32))
    onehot = jnp.where(hit, 1.0, 0.0).astype(BF)
    src = iota((ROWS, ROWS), 0)
    dst = iota((ROWS, ROWS), 1)
    order = jnp.where(dst < HALF, 2 * dst, 2 * dst - (ROWS - 1))
    onehot = nn(onehot, (src == order).astype(BF))
    onehot_t = onehot.T.astype(BF)
    onehot = onehot.astype(BF)
    z = nn(onehot_t, e_hi) + nn(onehot_t, e_lo)
    h_zero = nn(onehot_t, embf[...].astype(BF)).astype(BF).astype(F32)
    g_z, s_z = gelu_both(z)
    h_one = (h_zero + g_z).astype(BF).astype(F32)
    even, odd = h_one[:HALF], h_one[HALF:]
    pooled = ((even + odd) * 0.5).astype(BF).astype(F32)
    scale = lax.rsqrt(jnp.mean(pooled * pooled, axis=-1, keepdims=True) + 1e-06)
    normed = (pooled * scale).astype(BF)
    w_in = win[...]
    w_out = wout[...]
    pre = nn(normed, w_in)
    g_p, s_p = gelu_both(pre)
    act = g_p.astype(BF)
    mixed = nt(act, w_out).astype(BF).astype(F32)
    for lane in LANES:
        rows_f[pl.ds(0, HALF, stride=2), :] = (even + mixed)[:, lane]
        rows_f[pl.ds(1, HALF, stride=2), :] = (odd + mixed)[:, lane]
        out_ref[0, :, lane] = rows_f[...].astype(BF)
    d_even, d_odd = [], []
    for lane in LANES:
        rows_f[...] = cot_ref[0, :, lane].astype(F32)
        d_even.append(rows_f[pl.ds(0, HALF, stride=2), :])
        d_odd.append(rows_f[pl.ds(1, HALF, stride=2), :])
    d_even, d_odd = (jnp.concatenate(d, axis=1) for d in (d_even, d_odd))
    dmixed = (d_even + d_odd).astype(BF)
    dact = nn(dmixed, w_out)
    dpre = (dact * s_p).astype(BF)
    dnormed = nt(dpre, w_in)
    dpooled = scale * dnormed - pooled * (scale * scale * scale) * jnp.mean(
        dnormed * pooled, axis=-1, keepdims=True
    )
    add = dpooled * 0.5
    dh_one = jnp.concatenate([d_even + add, d_odd + add], axis=0)
    dz = (dh_one * s_z).astype(BF)
    d_hi = dh_one.astype(BF)
    d_lo = (dh_one - d_hi.astype(F32)).astype(BF)
    small = jnp.where(
        iota((HALF, C), 0) < TAPS * PAIRS, nn(onehot, dz), nn(onehot, d_hi) + nn(onehot, d_lo)
    )
    ebuf[...] = small
    grad_a[...] = tn(normed, dpre)
    grad_b[...] = tn(dmixed, act)
    for which, ref in ((core, keep_ref), (1 - core, send_ref)):
        for x in range(X):
            grad = grad_a if x < 2 else grad_b
            for half in range(YL):
                cols = slice(C * half, C * (half + 1))
                parts = []
                for h in range(YH):
                    top = pl.multiple_of((2 * h + which) * SHARD + 24 * (x % 2), 8)
                    parts.append(grad[pl.ds(top, 24), cols])
                parts.append(ebuf[32 * x : 32 * x + 32, :])
                ref[YL * x + half] = jnp.concatenate(parts, axis=0).astype(BF)


def middle_kernel(in_ref, out_ref):
    total = in_ref[0].astype(F32)
    for i in range(1, X * YL):
        total = total + in_ref[i].astype(F32)
    for z in range(Z):
        for h in range(YH):
            if z < 3:
                piece = total[24 * h + 8 * z : 24 * h + 8 * z + 8]
            elif z < 7:
                piece = total[96 + 8 * (z - 3) : 96 + 8 * (z - 3) + 8]
            else:
                piece = jnp.zeros((8, C), F32)
            out_ref[YH * z + h] = piece.astype(BF)


def last_kernel(in_ref, out_ref):
    total = in_ref[0].astype(F32)
    for i in range(1, Z * YH):
        total = total + in_ref[i].astype(F32)
    total = total.astype(BF)
    for i in range(Z * X):
        out_ref[i] = total


def grads_kernel(
    place, in_ref, embed_ref, conv_ref, gemb_ref, gconv_ref, gin_ref, gout_ref, sums, emb, left, back
):
    seq = place[0]
    for x in range(X):
        for z in range(3):
            piece = in_ref[X * z + x].astype(F32)
            top = 24 * (x % 2) + 8 * z
            (gin_ref if x < 2 else gout_ref)[top : top + 8, :] = piece
        for z in range(3, 7):
            top = 32 * x + 8 * (z - 3)
            sums[top : top + 8, :] = in_ref[X * z + x].astype(F32)
    emb[...] = jnp.zeros_like(emb)
    stack_embed(embed_ref, emb, 0)
    pick = picker(seq)
    mine = nn(emb[...].astype(BF), pick)
    small = sums[...].astype(BF)
    total = jnp.zeros((PAIRS, SHARD), F32)
    back[...] = nn(small, pick)
    total = total + back[TAPS * PAIRS : (TAPS + 1) * PAIRS, :]
    for k in range(TAPS):
        left[...] = jnp.zeros_like(left)
        left[PAIRS * k : PAIRS * (k + 1), :] = mine[:PAIRS]
        gconv_ref[k] = tn(left[...].astype(BF), small)
        back[...] = nt(small, conv_ref[k])
        total = total + back[PAIRS * k : PAIRS * (k + 1), :]
    back[0:PAIRS, :] = total
    for j in range(TAPS):
        gemb_ref[j] = back[BASES * j : BASES * (j + 1), :]


def call(body, outs, scratch, args, scalars=True, flops=0):
    specs = [pl.BlockSpec(memory_space=VMEM)] * len(args)
    if scalars:
        specs[0] = pl.BlockSpec(memory_space=pltpu.SMEM)
    many = isinstance(outs, list)
    spec = pl.BlockSpec(memory_space=VMEM)
    return pl.pallas_call(
        body,
        out_shape=outs,
        in_specs=specs,
        out_specs=[spec] * len(outs) if many else spec,
        scratch_shapes=scratch,
        compiler_params=pltpu.CompilerParams(vmem_limit_bytes=48 * 1024 * 1024),
        name=body.__name__,
    )(*args)


def array(*shape, dtype=BF):
    return jax.ShapeDtypeStruct(shape, dtype)


def exchange(pieces, axes):
    return lax.all_to_all(pieces, axes, 0, 0, tiled=True)


def local(bases, embed, conv_w, w_in, w_out, cotangent):
    yh, core, yl = lax.axis_index("yh"), lax.axis_index("core"), lax.axis_index("yl")
    place = jnp.stack([yh * CORE + core, yh, core, yl]).astype(jnp.int32)
    swap = [(0, 1), (1, 0)]
    packed = call(
        pack_kernel,
        array(YH * YL, 160, C),
        [VMEM((24, C), F32), VMEM((112, C), F32)],
        (place, bases, embed, conv_w, w_in, w_out.T),
    )
    own = exchange(packed, ("yh", "yl"))
    other = lax.ppermute(own, "core", swap)
    output, keep, send = call(
        step_kernel,
        [array(1, ROWS, C), array(X * YL, 128, C), array(X * YL, 128, C)],
        [
            VMEM((C, F), BF),
            VMEM((C, F), BF),
            VMEM((128, C), F32),
            VMEM((128, C), F32),
            VMEM((ROWS, 128), F32),
            VMEM((C, F), F32),
            VMEM((C, F), F32),
        ],
        (place, own, other, bases, embed, cotangent),
    )
    came = lax.ppermute(send, "core", swap)
    pairs = (keep.astype(F32) + came.astype(F32)).astype(BF)
    pieces = call(middle_kernel, array(Z * YH, 8, C), [], (exchange(pairs, ("x", "yl")),), scalars=False)
    copies = call(last_kernel, array(Z * X, 8, C), [], (exchange(pieces, ("z", "yh")),), scalars=False)
    gathered = exchange(copies, ("z", "x"))
    g_embed, g_conv, g_in, g_out = call(
        grads_kernel,
        [
            array(TAPS, BASES, SHARD, dtype=F32),
            array(TAPS, SHARD, C, dtype=F32),
            array(SHARD, C, dtype=F32),
            array(SHARD, C, dtype=F32),
        ],
        [VMEM((128, C), F32), VMEM((24, C), F32), VMEM((128, SHARD), F32), VMEM((128, SHARD), F32)],
        (place, gathered, embed, conv_w),
    )
    return output, g_embed, g_conv, g_in, g_out.T


def solution(mesh):
    mesh = Mesh(mesh.devices.reshape(Z, X, YH, CORE, YL), ("z", "x", "yh", "core", "yl"))
    seq = ("yh", "core")
    samples = ("z", "x", "yl")
    return jax.shard_map(
        local,
        mesh=mesh,
        in_specs=(
            P(samples, seq),
            P(),
            P(None, seq, None),
            P(seq, "yl"),
            P("yl", seq),
            P(samples, seq, None),
        ),
        out_specs=(
            P(samples, seq, None),
            P(None, None, seq),
            P(None, seq, None),
            P(seq, "yl"),
            P("yl", seq),
        ),
        check_vma=False,
    )
```

```python
import jax
import jax.numpy as jnp
from jax import lax
from jax.experimental import pallas as pl
from jax.experimental.pallas import tpu as pltpu
from jax.sharding import Mesh
from jax.sharding import PartitionSpec as P

Z, X, YH, CORE, YL = 8, 4, 4, 2, 2
TAPS = 5
BASES = 4
C = 384
F = 768
ROWS = 256
HALF = 128
LENGTH = 2048
SHARD = 48
PAIRS = TAPS * BASES
BF = jnp.bfloat16
F32 = jnp.float32
VMEM = pltpu.VMEM
LANES = [slice(128 * i, 128 * (i + 1)) for i in range(C // 128)]
GELU_C = 0.7978845608028654
GELU_A = 0.044715


def dot(a, b, dims):
    return lax.dot_general(a, b, (dims, ((), ())), preferred_element_type=F32)


def nn(a, b):
    return dot(a, b, ((1,), (0,)))


def nt(a, b):
    return dot(a, b, ((1,), (1,)))


def tn(a, b):
    return dot(a, b, ((0,), (0,)))


def iota(shape, dim):
    return lax.broadcasted_iota(jnp.int32, shape, dim)


def gelu_both(x):
    x2 = x * x
    t = jnp.tanh(GELU_C * (x + GELU_A * (x * x2)))
    half = 0.5 * (1.0 + t)
    slope = half + 0.5 * x * (1.0 - t * t) * (GELU_C * (1.0 + 3.0 * GELU_A * x2))
    return x * half, slope


def stack_embed(embed_ref, scratch, top):
    for j in range(TAPS):
        scratch[top + BASES * j : top + BASES * (j + 1), :] = embed_ref[j].astype(F32)


def picker(seq):
    return (iota((C, SHARD), 0) == iota((C, SHARD), 1) + seq * SHARD).astype(BF)


def pack_kernel(
    place, ids_hbm, embed_hbm, conv_hbm, win_hbm, wout_hbm, out_ref,
    ids_v, embed_v, conv_v, shard_v, sems, emb, esum, tail, shard_f,
):
    seq, yl, x = place[0], place[3], place[4]
    copies = [
        pltpu.make_async_copy(src, dst, sems.at[i])
        for i, (src, dst) in enumerate(
            (
                (embed_hbm, embed_v),
                (conv_hbm, conv_v),
                (win_hbm, shard_v.at[0]),
                (wout_hbm, shard_v.at[1]),
                (ids_hbm, ids_v),
            )
        )
    ]
    for copy in copies:
        copy.start()
    emb[...] = jnp.zeros_like(emb)
    esum[...] = jnp.zeros_like(esum)
    tail[...] = jnp.zeros_like(tail)
    copies[0].wait()
    stack_embed(embed_v, emb, 0)
    mine = nn(emb[...].astype(BF), picker(seq)).astype(BF)
    copies[1].wait()
    for k in range(TAPS):
        esum[PAIRS * k : PAIRS * (k + 1), :] = nn(mine, conv_v[k])[:PAIRS]
    for q in range(X * YL):
        tail[16 * q : 16 * q + 13, :] = esum[13 * q : 13 * q + 13, :]
    part = tail[pl.ds(pl.multiple_of((YL * x + yl) * 16, 16), 16), :]
    for copy in copies[2:]:
        copy.wait()
    ids = jnp.concatenate([ids_v[...].astype(F32), jnp.zeros((1, C - ROWS), F32)], axis=1)
    part = jnp.where(iota((16, C), 0) == 15, ids, part)
    shard_f[0:48, :] = shard_v[0].astype(F32)
    shard_f[48:96, :] = shard_v[1].astype(F32)
    piece = shard_f[pl.ds(pl.multiple_of(24 * x, 8), 24), :]
    piece = jnp.concatenate([piece, part], axis=0).astype(BF)
    for d in range(YH * YL):
        out_ref[d] = piece


def relay_kernel(place, in_ref, out_ref):
    yl = place[3]
    got = [in_ref[p].astype(F32) for p in range(YH * YL)]
    sums = [sum(got[YL * h + half][24:40] for h in range(YH)) for half in range(YL)]
    row = iota((16, C), 0)
    for h in range(YH):
        ids = in_ref[YL * h + yl].astype(F32)[39:40]
        sums[h // 2] = jnp.where(row == 13 + h % 2, ids, sums[h // 2])
    piece = jnp.concatenate([g[:24] for g in got] + sums, axis=0).astype(BF)
    for x in range(X):
        out_ref[x] = piece


def step_kernel(
    place, own, oth, ids_ref, embed_ref, cot_ref,
    out_ref, keep_ref, send_ref,
    win, wout, ebuf, embf, rows_f, grad_a, grad_b,
):
    seq, yh, core, x_mine = place[0], place[1], place[2], place[4]
    for side, got in ((core, own), (1 - core, oth)):
        for h in range(YH):
            top = pl.multiple_of((CORE * h + side) * SHARD, SHARD)
            for half in range(YL):
                cols = slice(C * half, C * (half + 1))
                p = 24 * (YL * h + half)
                for ref, first in ((win, 0), (wout, 2)):
                    ref[pl.ds(top, SHARD), cols] = jnp.concatenate(
                        [got[first, p : p + 24, :], got[first + 1, p : p + 24, :]], axis=0
                    )
    ebuf[...] = jnp.zeros_like(ebuf)
    for x in range(X):
        for half in range(YL):
            p = 192 + 16 * half
            total = own[x, p : p + 16, :].astype(F32) + oth[x, p : p + 16, :].astype(F32)
            q = YL * x + half
            ebuf[13 * q : 13 * q + 13, :] = total[:13]
    embf[...] = jnp.zeros_like(embf)
    stack_embed(embed_ref, embf, TAPS * PAIRS)
    e_full = ebuf[...]
    e_hi = e_full.astype(BF)
    e_lo = (e_full - e_hi.astype(F32)).astype(BF)
    before = jnp.maximum(yh - (1 - core), 0)
    after = jnp.minimum(yh + core, YH - 1)
    near = oth[x_mine, 192:224, :].astype(F32)[:, :ROWS]
    row = iota((32, ROWS), 0)

    def ids_of(h):
        at = 16 * jnp.right_shift(h, 1) + 13 + jnp.bitwise_and(h, 1)
        line = jnp.sum(jnp.where(row == at, near, 0.0), axis=0, keepdims=True)
        return jnp.broadcast_to(line, (8, ROWS))

    id_prev = jnp.where(seq == 0, -1.0, ids_of(before)[:, 128:])
    id_next = jnp.where(seq == YH * CORE - 1, -1.0, ids_of(after)[:, :128])
    id_mid = jnp.broadcast_to(ids_ref[...].astype(F32), (8, ROWS))
    line = jnp.concatenate([id_prev, id_mid, id_next], axis=1)
    m = iota((HALF, ROWS), 0)
    k = sum((m >= PAIRS * q).astype(jnp.int32) for q in range(1, TAPS + 1))
    rest = m - PAIRS * k
    k = jnp.where(m >= PAIRS * TAPS, 2, k)
    j = jnp.right_shift(rest, 2)
    base = jnp.bitwise_and(rest, 3)
    seen = jnp.full((HALF, ROWS), -2.0, F32)
    for o in range(2 * TAPS - 1):
        moved = pltpu.roll(line, (4 - o) % 512, 1)[:, 128 : 128 + ROWS]
        seen = jnp.where(k + j == o, jnp.concatenate([moved] * (HALF // 8), axis=0), seen)
    at = seq * ROWS + iota((HALF, ROWS), 1) + k - 2
    hit = (at >= 0) & (at < LENGTH) & (m < PAIRS * (TAPS + 1)) & (seen == base.astype(F32))
    onehot = jnp.where(hit, 1.0, 0.0).astype(BF)
    src = iota((ROWS, ROWS), 0)
    dst = iota((ROWS, ROWS), 1)
    order = jnp.where(dst < HALF, 2 * dst, 2 * dst - (ROWS - 1))
    onehot = nn(onehot, (src == order).astype(BF))
    onehot_t = onehot.T.astype(BF)
    onehot = onehot.astype(BF)
    z = nn(onehot_t, e_hi) + nn(onehot_t, e_lo)
    h_zero = nn(onehot_t, embf[...].astype(BF)).astype(BF).astype(F32)
    g_z, s_z = gelu_both(z)
    h_one = (h_zero + g_z).astype(BF).astype(F32)
    even, odd = h_one[:HALF], h_one[HALF:]
    pooled = ((even + odd) * 0.5).astype(BF).astype(F32)
    scale = lax.rsqrt(jnp.mean(pooled * pooled, axis=-1, keepdims=True) + 1e-06)
    normed = (pooled * scale).astype(BF)
    w_in = win[...]
    w_out = wout[...]
    pre = nn(normed, w_in)
    g_p, s_p = gelu_both(pre)
    act = g_p.astype(BF)
    mixed = nt(act, w_out).astype(BF).astype(F32)
    for lane in LANES:
        rows_f[pl.ds(0, HALF, stride=2), :] = (even + mixed)[:, lane]
        rows_f[pl.ds(1, HALF, stride=2), :] = (odd + mixed)[:, lane]
        out_ref[0, :, lane] = rows_f[...].astype(BF)
    d_even, d_odd = [], []
    for lane in LANES:
        rows_f[...] = cot_ref[0, :, lane].astype(F32)
        d_even.append(rows_f[pl.ds(0, HALF, stride=2), :])
        d_odd.append(rows_f[pl.ds(1, HALF, stride=2), :])
    d_even, d_odd = (jnp.concatenate(d, axis=1) for d in (d_even, d_odd))
    dmixed = (d_even + d_odd).astype(BF)
    dact = nn(dmixed, w_out)
    dpre = (dact * s_p).astype(BF)
    dnormed = nt(dpre, w_in)
    dpooled = scale * dnormed - pooled * (scale * scale * scale) * jnp.mean(
        dnormed * pooled, axis=-1, keepdims=True
    )
    add = dpooled * 0.5
    dh_one = jnp.concatenate([d_even + add, d_odd + add], axis=0)
    dz = (dh_one * s_z).astype(BF)
    d_hi = dh_one.astype(BF)
    d_lo = (dh_one - d_hi.astype(F32)).astype(BF)
    small = jnp.where(
        iota((HALF, C), 0) < TAPS * PAIRS, nn(onehot, dz), nn(onehot, d_hi) + nn(onehot, d_lo)
    )
    ebuf[...] = small
    grad_a[...] = tn(normed, dpre)
    grad_b[...] = tn(dmixed, act)
    for which, ref in ((core, keep_ref), (1 - core, send_ref)):
        for x in range(X):
            grad = grad_a if x < 2 else grad_b
            for half in range(YL):
                cols = slice(C * half, C * (half + 1))
                parts = []
                for h in range(YH):
                    top = pl.multiple_of((2 * h + which) * SHARD + 24 * (x % 2), 8)
                    parts.append(grad[pl.ds(top, 24), cols])
                parts.append(ebuf[32 * x : 32 * x + 32, :])
                ref[YL * x + half] = jnp.concatenate(parts, axis=0).astype(BF)


def middle_kernel(in_ref, out_ref):
    total = in_ref[0].astype(F32)
    for i in range(1, X * YL):
        total = total + in_ref[i].astype(F32)
    for z in range(Z):
        for h in range(YH):
            if z < 3:
                piece = total[24 * h + 8 * z : 24 * h + 8 * z + 8]
            elif z < 7:
                piece = total[96 + 8 * (z - 3) : 96 + 8 * (z - 3) + 8]
            else:
                piece = jnp.zeros((8, C), F32)
            out_ref[YH * z + h] = piece.astype(BF)


def last_kernel(in_ref, out_ref):
    total = in_ref[0].astype(F32)
    for i in range(1, Z * YH):
        total = total + in_ref[i].astype(F32)
    total = total.astype(BF)
    for i in range(Z * X):
        out_ref[i] = total


def grads_kernel(
    place, in_ref, embed_ref, conv_ref, gemb_ref, gconv_ref, gin_ref, gout_ref, sums, emb, left, back
):
    seq = place[0]
    for x in range(X):
        for z in range(3):
            piece = in_ref[X * z + x].astype(F32)
            top = 24 * (x % 2) + 8 * z
            (gin_ref if x < 2 else gout_ref)[top : top + 8, :] = piece
        for z in range(3, 7):
            top = 32 * x + 8 * (z - 3)
            sums[top : top + 8, :] = in_ref[X * z + x].astype(F32)
    emb[...] = jnp.zeros_like(emb)
    stack_embed(embed_ref, emb, 0)
    pick = picker(seq)
    mine = nn(emb[...].astype(BF), pick)
    small = sums[...].astype(BF)
    total = jnp.zeros((PAIRS, SHARD), F32)
    back[...] = nn(small, pick)
    total = total + back[TAPS * PAIRS : (TAPS + 1) * PAIRS, :]
    for k in range(TAPS):
        left[...] = jnp.zeros_like(left)
        left[PAIRS * k : PAIRS * (k + 1), :] = mine[:PAIRS]
        gconv_ref[k] = tn(left[...].astype(BF), small)
        back[...] = nt(small, conv_ref[k])
        total = total + back[PAIRS * k : PAIRS * (k + 1), :]
    back[0:PAIRS, :] = total
    for j in range(TAPS):
        gemb_ref[j] = back[BASES * j : BASES * (j + 1), :]


def call(body, outs, scratch, args, place=None, hbm=False):
    spec = pl.BlockSpec(memory_space=VMEM)
    specs = [pl.BlockSpec(memory_space=pltpu.HBM) if hbm else spec] * len(args)
    if hbm:
        args = tuple(pltpu.with_memory_space_constraint(a, pltpu.HBM) for a in args)
    if place is not None:
        args = (place,) + args
        specs = [pl.BlockSpec(memory_space=pltpu.SMEM)] + specs
    many = isinstance(outs, list)
    return pl.pallas_call(
        body,
        out_shape=outs,
        in_specs=specs,
        out_specs=[spec] * len(outs) if many else spec,
        scratch_shapes=scratch,
        compiler_params=pltpu.CompilerParams(vmem_limit_bytes=48 * 1024 * 1024),
        name=body.__name__,
    )(*args)


def array(*shape, dtype=BF):
    return jax.ShapeDtypeStruct(shape, dtype)


def exchange(pieces, axes):
    return lax.all_to_all(pieces, axes, 0, 0, tiled=True)


def local(bases, embed, conv_w, w_in, w_out, cotangent):
    x, yh, core, yl = (lax.axis_index(name) for name in ("x", "yh", "core", "yl"))
    place = jnp.stack([yh * CORE + core, yh, core, yl, x]).astype(jnp.int32)
    packed = call(
        pack_kernel,
        array(YH * YL, 40, C),
        [
            VMEM((1, ROWS), jnp.int32),
            VMEM((TAPS, BASES, C), BF),
            VMEM((TAPS, SHARD, C), BF),
            VMEM((2, SHARD, C), BF),
            pltpu.SemaphoreType.DMA((5,)),
            VMEM((24, C), F32),
            VMEM((104, C), F32),
            VMEM((128, C), F32),
            VMEM((96, C), F32),
        ],
        (bases, embed, conv_w, w_in, w_out.T),
        place,
        hbm=True,
    )
    quarters = call(relay_kernel, array(X, 224, C), [], (exchange(packed, ("yh", "yl")),), place)
    swap = [(0, 1), (1, 0)]
    mine = exchange(quarters, "x")
    other = lax.ppermute(mine, "core", swap)
    output, keep, send = call(
        step_kernel,
        [array(1, ROWS, C), array(X * YL, 128, C), array(X * YL, 128, C)],
        [
            VMEM((C, F), BF),
            VMEM((C, F), BF),
            VMEM((128, C), F32),
            VMEM((128, C), F32),
            VMEM((ROWS, 128), F32),
            VMEM((C, F), F32),
            VMEM((C, F), F32),
        ],
        (mine, other, bases, embed, cotangent),
        place,
    )
    came = lax.ppermute(send, "core", swap)
    pairs = (keep.astype(F32) + came.astype(F32)).astype(BF)
    pieces = call(middle_kernel, array(Z * YH, 8, C), [], (exchange(pairs, ("x", "yl")),))
    copies = call(last_kernel, array(Z * X, 8, C), [], (exchange(pieces, ("z", "yh")),))
    gathered = exchange(copies, ("z", "x"))
    g_embed, g_conv, g_in, g_out = call(
        grads_kernel,
        [
            array(TAPS, BASES, SHARD, dtype=F32),
            array(TAPS, SHARD, C, dtype=F32),
            array(SHARD, C, dtype=F32),
            array(SHARD, C, dtype=F32),
        ],
        [VMEM((128, C), F32), VMEM((24, C), F32), VMEM((128, SHARD), F32), VMEM((128, SHARD), F32)],
        (gathered, embed, conv_w),
        place,
    )
    return output, g_embed, g_conv, g_in, g_out.T


def solution(mesh):
    mesh = Mesh(mesh.devices.reshape(Z, X, YH, CORE, YL), ("z", "x", "yh", "core", "yl"))
    seq = ("yh", "core")
    samples = ("z", "x", "yl")
    return jax.shard_map(
        local,
        mesh=mesh,
        in_specs=(
            P(samples, seq),
            P(),
            P(None, seq, None),
            P(seq, "yl"),
            P("yl", seq),
            P(samples, seq, None),
        ),
        out_specs=(
            P(samples, seq, None),
            P(None, None, seq),
            P(None, seq, None),
            P(seq, "yl"),
            P("yl", seq),
        ),
        check_vma=False,
    )
```

```python
import jax
import jax.numpy as jnp
from jax import lax
from jax.experimental import pallas as pl
from jax.experimental.pallas import tpu as pltpu
from jax.sharding import Mesh
from jax.sharding import PartitionSpec as P

Z, X, YH, CORE, YL = 8, 4, 4, 2, 2
TAPS = 5
BASES = 4
C = 384
F = 768
ROWS = 256
HALF = 128
LENGTH = 2048
SHARD = 48
PAIRS = TAPS * BASES
BF = jnp.bfloat16
F32 = jnp.float32
VMEM = pltpu.VMEM
LANES = [slice(128 * i, 128 * (i + 1)) for i in range(C // 128)]
GELU_C = 0.7978845608028654
GELU_A = 0.044715


def dot(a, b, dims):
    return lax.dot_general(a, b, (dims, ((), ())), preferred_element_type=F32)


def nn(a, b):
    return dot(a, b, ((1,), (0,)))


def nt(a, b):
    return dot(a, b, ((1,), (1,)))


def tn(a, b):
    return dot(a, b, ((0,), (0,)))


def iota(shape, dim):
    return lax.broadcasted_iota(jnp.int32, shape, dim)


def gelu_both(x):
    x2 = x * x
    t = jnp.tanh(GELU_C * (x + GELU_A * (x * x2)))
    half = 0.5 * (1.0 + t)
    slope = half + 0.5 * x * (1.0 - t * t) * (GELU_C * (1.0 + 3.0 * GELU_A * x2))
    return x * half, slope


def stack_embed(embed_ref, scratch, top):
    for j in range(TAPS):
        scratch[top + BASES * j : top + BASES * (j + 1), :] = embed_ref[j].astype(F32)


def picker(seq):
    return (iota((C, SHARD), 0) == iota((C, SHARD), 1) + seq * SHARD).astype(BF)


def pack_kernel(
    place, ids_hbm, embed_hbm, conv_hbm, win_hbm, wout_hbm, out_ref,
    ids_v, embed_v, conv_v, shard_v, sems, emb, esum, tail, shard_f,
):
    seq, yl, x = place[0], place[3], place[4]
    copies = [
        pltpu.make_async_copy(src, dst, sems.at[i])
        for i, (src, dst) in enumerate(
            (
                (embed_hbm, embed_v),
                (conv_hbm, conv_v),
                (win_hbm, shard_v.at[0]),
                (wout_hbm, shard_v.at[1]),
                (ids_hbm, ids_v),
            )
        )
    ]
    for copy in copies:
        copy.start()
    emb[...] = jnp.zeros_like(emb)
    esum[...] = jnp.zeros_like(esum)
    tail[...] = jnp.zeros_like(tail)
    copies[0].wait()
    stack_embed(embed_v, emb, 0)
    mine = nn(emb[...].astype(BF), picker(seq)).astype(BF)
    copies[1].wait()
    for k in range(TAPS):
        esum[PAIRS * k : PAIRS * (k + 1), :] = nn(mine, conv_v[k])[:PAIRS]
    for q in range(X * YL):
        tail[16 * q : 16 * q + 13, :] = esum[13 * q : 13 * q + 13, :]
    part = tail[pl.ds(pl.multiple_of((YL * x + yl) * 16, 16), 16), :]
    for copy in copies[2:]:
        copy.wait()
    ids = jnp.concatenate([ids_v[...].astype(F32), jnp.zeros((1, C - ROWS), F32)], axis=1)
    part = jnp.where(iota((16, C), 0) == 15, ids, part)
    shard_f[0:48, :] = shard_v[0].astype(F32)
    shard_f[48:96, :] = shard_v[1].astype(F32)
    piece = shard_f[pl.ds(pl.multiple_of(24 * x, 8), 24), :]
    piece = jnp.concatenate([piece, part], axis=0).astype(BF)
    for d in range(YH * YL):
        out_ref[d] = piece


def relay_kernel(place, in_ref, out_ref):
    yl = place[3]
    got = [in_ref[p].astype(F32) for p in range(YH * YL)]
    sums = [sum(got[YL * h + half][24:40] for h in range(YH)) for half in range(YL)]
    row = iota((16, C), 0)
    for h in range(YH):
        ids = in_ref[YL * h + yl].astype(F32)[39:40]
        sums[h // 2] = jnp.where(row == 13 + h % 2, ids, sums[h // 2])
    piece = jnp.concatenate([g[:24] for g in got] + sums, axis=0).astype(BF)
    for x in range(X):
        out_ref[x] = piece


def step_kernel(
    place, own, oth, ids_ref, embed_ref, cot_ref,
    out_ref, keep_ref, send_ref,
    win, wout, ebuf, embf, rows_f, grad_a, grad_b,
):
    seq, yh, core, x_mine = place[0], place[1], place[2], place[4]
    for side, got in ((core, own), (1 - core, oth)):
        for h in range(YH):
            top = pl.multiple_of((CORE * h + side) * SHARD, SHARD)
            for half in range(YL):
                cols = slice(C * half, C * (half + 1))
                p = 24 * (YL * h + half)
                for ref, first in ((win, 0), (wout, 2)):
                    ref[pl.ds(top, SHARD), cols] = jnp.concatenate(
                        [got[first, p : p + 24, :], got[first + 1, p : p + 24, :]], axis=0
                    )
    ebuf[...] = jnp.zeros_like(ebuf)
    for x in range(X):
        for half in range(YL):
            p = 192 + 16 * half
            total = own[x, p : p + 16, :].astype(F32) + oth[x, p : p + 16, :].astype(F32)
            q = YL * x + half
            ebuf[13 * q : 13 * q + 13, :] = total[:13]
    embf[...] = jnp.zeros_like(embf)
    stack_embed(embed_ref, embf, TAPS * PAIRS)
    e_full = ebuf[...]
    e_hi = e_full.astype(BF)
    e_lo = (e_full - e_hi.astype(F32)).astype(BF)
    before = jnp.maximum(yh - (1 - core), 0)
    after = jnp.minimum(yh + core, YH - 1)
    near = oth[x_mine, 192:224, :].astype(F32)[:, :ROWS]
    row = iota((32, ROWS), 0)

    def ids_of(h):
        at = 16 * jnp.right_shift(h, 1) + 13 + jnp.bitwise_and(h, 1)
        line = jnp.sum(jnp.where(row == at, near, 0.0), axis=0, keepdims=True)
        return jnp.broadcast_to(line, (8, ROWS))

    id_prev = jnp.where(seq == 0, -1.0, ids_of(before)[:, 128:])
    id_next = jnp.where(seq == YH * CORE - 1, -1.0, ids_of(after)[:, :128])
    id_mid = jnp.broadcast_to(ids_ref[...].astype(F32), (8, ROWS))
    line = jnp.concatenate([id_prev, id_mid, id_next], axis=1)
    m = iota((HALF, ROWS), 0)
    k = sum((m >= PAIRS * q).astype(jnp.int32) for q in range(1, TAPS + 1))
    rest = m - PAIRS * k
    k = jnp.where(m >= PAIRS * TAPS, 2, k)
    j = jnp.right_shift(rest, 2)
    base = jnp.bitwise_and(rest, 3)
    seen = jnp.full((HALF, ROWS), -2.0, F32)
    for o in range(2 * TAPS - 1):
        moved = pltpu.roll(line, (4 - o) % 512, 1)[:, 128 : 128 + ROWS]
        seen = jnp.where(k + j == o, jnp.concatenate([moved] * (HALF // 8), axis=0), seen)
    at = seq * ROWS + iota((HALF, ROWS), 1) + k - 2
    hit = (at >= 0) & (at < LENGTH) & (m < PAIRS * (TAPS + 1)) & (seen == base.astype(F32))
    onehot = jnp.where(hit, 1.0, 0.0).astype(BF)
    src = iota((ROWS, ROWS), 0)
    dst = iota((ROWS, ROWS), 1)
    order = jnp.where(dst < HALF, 2 * dst, 2 * dst - (ROWS - 1))
    onehot = nn(onehot, (src == order).astype(BF))
    onehot_t = onehot.T.astype(BF)
    onehot = onehot.astype(BF)
    z = nn(onehot_t, e_hi) + nn(onehot_t, e_lo)
    h_zero = nn(onehot_t, embf[...].astype(BF)).astype(BF).astype(F32)
    g_z, s_z = gelu_both(z)
    h_one = (h_zero + g_z).astype(BF).astype(F32)
    even, odd = h_one[:HALF], h_one[HALF:]
    pooled = ((even + odd) * 0.5).astype(BF).astype(F32)
    scale = lax.rsqrt(jnp.mean(pooled * pooled, axis=-1, keepdims=True) + 1e-06)
    normed = (pooled * scale).astype(BF)
    w_in = win[...]
    w_out = wout[...]
    pre = nn(normed, w_in)
    g_p, s_p = gelu_both(pre)
    act = g_p.astype(BF)
    mixed = nt(act, w_out).astype(BF).astype(F32)
    for lane in LANES:
        rows_f[pl.ds(0, HALF, stride=2), :] = (even + mixed)[:, lane]
        rows_f[pl.ds(1, HALF, stride=2), :] = (odd + mixed)[:, lane]
        out_ref[0, :, lane] = rows_f[...].astype(BF)
    d_even, d_odd = [], []
    for lane in LANES:
        rows_f[...] = cot_ref[0, :, lane].astype(F32)
        d_even.append(rows_f[pl.ds(0, HALF, stride=2), :])
        d_odd.append(rows_f[pl.ds(1, HALF, stride=2), :])
    d_even, d_odd = (jnp.concatenate(d, axis=1) for d in (d_even, d_odd))
    dmixed = (d_even + d_odd).astype(BF)
    dact = nn(dmixed, w_out)
    dpre = (dact * s_p).astype(BF)
    dnormed = nt(dpre, w_in)
    dpooled = scale * dnormed - pooled * (scale * scale * scale) * jnp.mean(
        dnormed * pooled, axis=-1, keepdims=True
    )
    add = dpooled * 0.5
    dh_one = jnp.concatenate([d_even + add, d_odd + add], axis=0)
    dz = (dh_one * s_z).astype(BF)
    d_hi = dh_one.astype(BF)
    d_lo = (dh_one - d_hi.astype(F32)).astype(BF)
    small = jnp.where(
        iota((HALF, C), 0) < TAPS * PAIRS, nn(onehot, dz), nn(onehot, d_hi) + nn(onehot, d_lo)
    )
    ebuf[...] = small
    grad_a[...] = tn(normed, dpre)
    grad_b[...] = tn(dmixed, act)
    for which, ref in ((core, keep_ref), (1 - core, send_ref)):
        for x in range(X):
            grad = grad_a if x < 2 else grad_b
            parts = []
            for h in range(YH):
                top = pl.multiple_of((2 * h + which) * SHARD + 24 * (x % 2), 8)
                for half in range(YL):
                    parts.append(grad[pl.ds(top, 24), C * half : C * (half + 1)])
            parts.append(ebuf[32 * x : 32 * x + 32, :])
            ref[x] = jnp.concatenate(parts, axis=0).astype(BF)


def middle_kernel(in_ref, out_ref):
    total = in_ref[0].astype(F32)
    for i in range(1, X):
        total = total + in_ref[i].astype(F32)
    top = 24 * YH * YL
    for z in range(Z):
        for p in range(YH * YL):
            if z < 3:
                piece = total[24 * p + 8 * z : 24 * p + 8 * z + 8]
            elif z < 7:
                piece = total[top + 8 * (z - 3) : top + 8 * (z - 3) + 8]
            else:
                piece = jnp.zeros((8, C), F32)
            out_ref[YH * YL * z + p] = piece.astype(BF)


def last_kernel(in_ref, out_ref):
    total = in_ref[0].astype(F32)
    for i in range(1, Z * YH * YL):
        total = total + in_ref[i].astype(F32)
    total = total.astype(BF)
    for i in range(Z * X):
        out_ref[i] = total


def grads_kernel(
    place, in_ref, embed_ref, conv_ref, gemb_ref, gconv_ref, gin_ref, gout_ref, sums, emb, left, back
):
    seq = place[0]
    for x in range(X):
        for z in range(3):
            piece = in_ref[X * z + x].astype(F32)
            top = 24 * (x % 2) + 8 * z
            (gin_ref if x < 2 else gout_ref)[top : top + 8, :] = piece
        for z in range(3, 7):
            top = 32 * x + 8 * (z - 3)
            sums[top : top + 8, :] = in_ref[X * z + x].astype(F32)
    emb[...] = jnp.zeros_like(emb)
    stack_embed(embed_ref, emb, 0)
    pick = picker(seq)
    mine = nn(emb[...].astype(BF), pick)
    small = sums[...].astype(BF)
    total = jnp.zeros((PAIRS, SHARD), F32)
    back[...] = nn(small, pick)
    total = total + back[TAPS * PAIRS : (TAPS + 1) * PAIRS, :]
    for k in range(TAPS):
        left[...] = jnp.zeros_like(left)
        left[PAIRS * k : PAIRS * (k + 1), :] = mine[:PAIRS]
        gconv_ref[k] = tn(left[...].astype(BF), small)
        back[...] = nt(small, conv_ref[k])
        total = total + back[PAIRS * k : PAIRS * (k + 1), :]
    back[0:PAIRS, :] = total
    for j in range(TAPS):
        gemb_ref[j] = back[BASES * j : BASES * (j + 1), :]


def call(body, outs, scratch, args, place=None, hbm=False):
    spec = pl.BlockSpec(memory_space=VMEM)
    specs = [pl.BlockSpec(memory_space=pltpu.HBM) if hbm else spec] * len(args)
    if hbm:
        args = tuple(pltpu.with_memory_space_constraint(a, pltpu.HBM) for a in args)
    if place is not None:
        args = (place,) + args
        specs = [pl.BlockSpec(memory_space=pltpu.SMEM)] + specs
    many = isinstance(outs, list)
    return pl.pallas_call(
        body,
        out_shape=outs,
        in_specs=specs,
        out_specs=[spec] * len(outs) if many else spec,
        scratch_shapes=scratch,
        compiler_params=pltpu.CompilerParams(vmem_limit_bytes=48 * 1024 * 1024),
        name=body.__name__,
    )(*args)


def array(*shape, dtype=BF):
    return jax.ShapeDtypeStruct(shape, dtype)


def exchange(pieces, axes):
    return lax.all_to_all(pieces, axes, 0, 0, tiled=True)


def local(bases, embed, conv_w, w_in, w_out, cotangent):
    x, yh, core, yl = (lax.axis_index(name) for name in ("x", "yh", "core", "yl"))
    place = jnp.stack([yh * CORE + core, yh, core, yl, x]).astype(jnp.int32)
    packed = call(
        pack_kernel,
        array(YH * YL, 40, C),
        [
            VMEM((1, ROWS), jnp.int32),
            VMEM((TAPS, BASES, C), BF),
            VMEM((TAPS, SHARD, C), BF),
            VMEM((2, SHARD, C), BF),
            pltpu.SemaphoreType.DMA((5,)),
            VMEM((24, C), F32),
            VMEM((104, C), F32),
            VMEM((128, C), F32),
            VMEM((96, C), F32),
        ],
        (bases, embed, conv_w, w_in, w_out.T),
        place,
        hbm=True,
    )
    quarters = call(relay_kernel, array(X, 224, C), [], (exchange(packed, ("yh", "yl")),), place)
    swap = [(0, 1), (1, 0)]
    mine = exchange(quarters, "x")
    other = lax.ppermute(mine, "core", swap)
    output, keep, send = call(
        step_kernel,
        [array(1, ROWS, C), array(X, 224, C), array(X, 224, C)],
        [
            VMEM((C, F), BF),
            VMEM((C, F), BF),
            VMEM((128, C), F32),
            VMEM((128, C), F32),
            VMEM((ROWS, 128), F32),
            VMEM((C, F), F32),
            VMEM((C, F), F32),
        ],
        (mine, other, bases, embed, cotangent),
        place,
    )
    came = lax.ppermute(send, "core", swap)
    pairs = (keep.astype(F32) + came.astype(F32)).astype(BF)
    pieces = call(middle_kernel, array(Z * YH * YL, 8, C), [], (exchange(pairs, "x"),))
    copies = call(last_kernel, array(Z * X, 8, C), [], (exchange(pieces, ("z", "yh", "yl")),))
    gathered = exchange(copies, ("z", "x"))
    g_embed, g_conv, g_in, g_out = call(
        grads_kernel,
        [
            array(TAPS, BASES, SHARD, dtype=F32),
            array(TAPS, SHARD, C, dtype=F32),
            array(SHARD, C, dtype=F32),
            array(SHARD, C, dtype=F32),
        ],
        [VMEM((128, C), F32), VMEM((24, C), F32), VMEM((128, SHARD), F32), VMEM((128, SHARD), F32)],
        (gathered, embed, conv_w),
        place,
    )
    return output, g_embed, g_conv, g_in, g_out.T


def solution(mesh):
    mesh = Mesh(mesh.devices.reshape(Z, X, YH, CORE, YL), ("z", "x", "yh", "core", "yl"))
    seq = ("yh", "core")
    samples = ("z", "x", "yl")
    return jax.shard_map(
        local,
        mesh=mesh,
        in_specs=(
            P(samples, seq),
            P(),
            P(None, seq, None),
            P(seq, "yl"),
            P("yl", seq),
            P(samples, seq, None),
        ),
        out_specs=(
            P(samples, seq, None),
            P(None, None, seq),
            P(None, seq, None),
            P(seq, "yl"),
            P("yl", seq),
        ),
        check_vma=False,
    )
```

```python
import jax
import jax.numpy as jnp
from jax import lax
from jax.experimental import pallas as pl
from jax.experimental.pallas import tpu as pltpu
from jax.sharding import Mesh
from jax.sharding import PartitionSpec as P

Z, X, YH, CORE, YL = 8, 4, 4, 2, 2
TAPS = 5
BASES = 4
C = 384
F = 768
ROWS = 256
HALF = 128
LENGTH = 2048
SHARD = 48
PAIRS = TAPS * BASES
BF = jnp.bfloat16
F32 = jnp.float32
VMEM = pltpu.VMEM
LANES = [slice(128 * i, 128 * (i + 1)) for i in range(C // 128)]
GELU_C = 0.7978845608028654
GELU_A = 0.044715


def dot(a, b, dims):
    return lax.dot_general(a, b, (dims, ((), ())), preferred_element_type=F32)


def nn(a, b):
    return dot(a, b, ((1,), (0,)))


def nt(a, b):
    return dot(a, b, ((1,), (1,)))


def tn(a, b):
    return dot(a, b, ((0,), (0,)))


def iota(shape, dim):
    return lax.broadcasted_iota(jnp.int32, shape, dim)


def gelu_both(x):
    x2 = x * x
    t = jnp.tanh(GELU_C * (x + GELU_A * (x * x2)))
    half = 0.5 * (1.0 + t)
    slope = half + 0.5 * x * (1.0 - t * t) * (GELU_C * (1.0 + 3.0 * GELU_A * x2))
    return x * half, slope


def where_am_i():
    x, yh, core, yl = (lax.axis_index(name) for name in ("x", "yh", "core", "yl"))
    return x, yh, core, yl, yh * CORE + core


def stack_embed(embed_ref, scratch, top):
    for j in range(TAPS):
        scratch[top + BASES * j : top + BASES * (j + 1), :] = embed_ref[j].astype(F32)


def picker(seq):
    return (iota((C, SHARD), 0) == iota((C, SHARD), 1) + seq * SHARD).astype(BF)


def pack_kernel(
    ids_hbm, embed_hbm, conv_hbm, win_hbm, wout_hbm, out_ref,
    ids_v, embed_v, conv_v, shard_v, sems, emb, esum, tail, shard_f,
):
    x, yh, core, yl, seq = where_am_i()
    copies = [
        pltpu.make_async_copy(src, dst, sems.at[i])
        for i, (src, dst) in enumerate(
            (
                (embed_hbm, embed_v),
                (conv_hbm, conv_v),
                (win_hbm, shard_v.at[0]),
                (wout_hbm, shard_v.at[1]),
                (ids_hbm, ids_v),
            )
        )
    ]
    for copy in copies:
        copy.start()
    emb[...] = jnp.zeros_like(emb)
    esum[...] = jnp.zeros_like(esum)
    tail[...] = jnp.zeros_like(tail)
    copies[0].wait()
    stack_embed(embed_v, emb, 0)
    mine = nn(emb[...].astype(BF), picker(seq)).astype(BF)
    copies[1].wait()
    for k in range(TAPS):
        esum[PAIRS * k : PAIRS * (k + 1), :] = nn(mine, conv_v[k])[:PAIRS]
    for q in range(X * YL):
        tail[16 * q : 16 * q + 13, :] = esum[13 * q : 13 * q + 13, :]
    part = tail[pl.ds(pl.multiple_of((YL * x + yl) * 16, 16), 16), :]
    for copy in copies[2:]:
        copy.wait()
    ids = jnp.concatenate([ids_v[...].astype(F32), jnp.zeros((1, C - ROWS), F32)], axis=1)
    part = jnp.where(iota((16, C), 0) == 15, ids, part)
    shard_f[0:48, :] = shard_v[0].astype(F32)
    shard_f[48:96, :] = shard_v[1].astype(F32)
    piece = shard_f[pl.ds(pl.multiple_of(24 * x, 8), 24), :]
    piece = jnp.concatenate([piece, part], axis=0).astype(BF)
    for d in range(YH * YL):
        out_ref[d] = piece


def relay_kernel(in_ref, out_ref):
    yl = where_am_i()[3]
    got = [in_ref[p].astype(F32) for p in range(YH * YL)]
    sums = [sum(got[YL * h + half][24:40] for h in range(YH)) for half in range(YL)]
    row = iota((16, C), 0)
    for h in range(YH):
        ids = in_ref[YL * h + yl].astype(F32)[39:40]
        sums[h // 2] = jnp.where(row == 13 + h % 2, ids, sums[h // 2])
    piece = jnp.concatenate([g[:24] for g in got] + sums, axis=0).astype(BF)
    for x in range(X):
        out_ref[x] = piece


def fill_weights(core, got, win, wout):
    for h in range(YH):
        top = pl.multiple_of((CORE * h + core) * SHARD, SHARD)
        for half in range(YL):
            cols = slice(C * half, C * (half + 1))
            p = 24 * (YL * h + half)
            for ref, first in ((win, 0), (wout, 2)):
                ref[pl.ds(top, SHARD), cols] = jnp.concatenate(
                    [got[first, p : p + 24, :], got[first + 1, p : p + 24, :]], axis=0
                )


def add_e(got, ebuf):
    for x in range(X):
        for half in range(YL):
            p = 192 + 16 * half
            q = 13 * (YL * x + half)
            ebuf[q : q + 13, :] = ebuf[q : q + 13, :] + got[x, p : p + 16, :].astype(F32)[:13]


def own_kernel(own, embed_ref, cot_ref, win, wout, ebuf, stem, dout, dmixed, embf, rows_f):
    core = where_am_i()[2]
    fill_weights(core, own, win, wout)
    ebuf[...] = jnp.zeros_like(ebuf)
    add_e(own, ebuf)
    embf[...] = jnp.zeros_like(embf)
    stack_embed(embed_ref, embf, TAPS * PAIRS)
    stem[...] = embf[...].astype(BF)
    for lane in LANES:
        rows_f[...] = cot_ref[0, :, lane].astype(F32)
        even = rows_f[pl.ds(0, HALF, stride=2), :]
        odd = rows_f[pl.ds(1, HALF, stride=2), :]
        dout[:HALF, lane] = even
        dout[HALF:, lane] = odd
        dmixed[:, lane] = (even + odd).astype(BF)


def step_kernel(
    oth, ids_ref, win_in, wout_in, ebuf_in, stem, dout, dmixed_ref,
    keep_ref, send_ref, win, wout, ebuf, h_out, act_out,
    grad_a, grad_b,
):
    x_mine, yh, core, yl, seq = where_am_i()
    fill_weights(1 - core, oth, win, wout)
    add_e(oth, ebuf)
    e_full = ebuf[...]
    e_hi = e_full.astype(BF)
    e_lo = (e_full - e_hi.astype(F32)).astype(BF)
    before = jnp.maximum(yh - (1 - core), 0)
    after = jnp.minimum(yh + core, YH - 1)
    near = oth[x_mine, 192:224, :].astype(F32)[:, :ROWS]
    row = iota((32, ROWS), 0)

    def ids_of(h):
        at = 16 * jnp.right_shift(h, 1) + 13 + jnp.bitwise_and(h, 1)
        line = jnp.sum(jnp.where(row == at, near, 0.0), axis=0, keepdims=True)
        return jnp.broadcast_to(line, (8, ROWS))

    id_prev = jnp.where(seq == 0, -1.0, ids_of(before)[:, 128:])
    id_next = jnp.where(seq == YH * CORE - 1, -1.0, ids_of(after)[:, :128])
    id_mid = jnp.broadcast_to(ids_ref[...].astype(F32), (8, ROWS))
    line = jnp.concatenate([id_prev, id_mid, id_next], axis=1)
    m = iota((HALF, ROWS), 0)
    k = sum((m >= PAIRS * q).astype(jnp.int32) for q in range(1, TAPS + 1))
    rest = m - PAIRS * k
    k = jnp.where(m >= PAIRS * TAPS, 2, k)
    j = jnp.right_shift(rest, 2)
    base = jnp.bitwise_and(rest, 3)
    seen = jnp.full((HALF, ROWS), -2.0, F32)
    for o in range(2 * TAPS - 1):
        moved = pltpu.roll(line, (4 - o) % 512, 1)[:, 128 : 128 + ROWS]
        seen = jnp.where(k + j == o, jnp.concatenate([moved] * (HALF // 8), axis=0), seen)
    at = seq * ROWS + iota((HALF, ROWS), 1) + k - 2
    hit = (at >= 0) & (at < LENGTH) & (m < PAIRS * (TAPS + 1)) & (seen == base.astype(F32))
    onehot = jnp.where(hit, 1.0, 0.0).astype(BF)
    src = iota((ROWS, ROWS), 0)
    dst = iota((ROWS, ROWS), 1)
    order = jnp.where(dst < HALF, 2 * dst, 2 * dst - (ROWS - 1))
    onehot = nn(onehot, (src == order).astype(BF))
    onehot_t = onehot.T.astype(BF)
    onehot = onehot.astype(BF)
    z = nn(onehot_t, e_hi) + nn(onehot_t, e_lo)
    h_zero = nn(onehot_t, stem[...]).astype(BF).astype(F32)
    g_z, s_z = gelu_both(z)
    h_one = (h_zero + g_z).astype(BF).astype(F32)
    even, odd = h_one[:HALF], h_one[HALF:]
    pooled = ((even + odd) * 0.5).astype(BF).astype(F32)
    scale = lax.rsqrt(jnp.mean(pooled * pooled, axis=-1, keepdims=True) + 1e-06)
    normed = (pooled * scale).astype(BF)
    w_in = win[...]
    w_out = wout[...]
    pre = nn(normed, w_in)
    g_p, s_p = gelu_both(pre)
    act = g_p.astype(BF)
    h_out[...] = h_one
    act_out[...] = act
    dmixed = dmixed_ref[...]
    d_even, d_odd = dout[:HALF, :], dout[HALF:, :]
    dact = nn(dmixed, w_out)
    dpre = (dact * s_p).astype(BF)
    dnormed = nt(dpre, w_in)
    dpooled = scale * dnormed - pooled * (scale * scale * scale) * jnp.mean(
        dnormed * pooled, axis=-1, keepdims=True
    )
    add = dpooled * 0.5
    dh_one = jnp.concatenate([d_even + add, d_odd + add], axis=0)
    dz = (dh_one * s_z).astype(BF)
    d_hi = dh_one.astype(BF)
    d_lo = (dh_one - d_hi.astype(F32)).astype(BF)
    small = jnp.where(
        iota((HALF, C), 0) < TAPS * PAIRS, nn(onehot, dz), nn(onehot, d_hi) + nn(onehot, d_lo)
    )
    ebuf[...] = small
    grad_a[...] = tn(normed, dpre)
    grad_b[...] = tn(dmixed, act)
    for which, ref in ((core, keep_ref), (1 - core, send_ref)):
        for x in range(X):
            grad = grad_a if x < 2 else grad_b
            for half in range(YL):
                cols = slice(C * half, C * (half + 1))
                parts = []
                for h in range(YH):
                    top = pl.multiple_of((2 * h + which) * SHARD + 24 * (x % 2), 8)
                    parts.append(grad[pl.ds(top, 24), cols])
                parts.append(ebuf[32 * x : 32 * x + 32, :])
                ref[YL * x + half] = jnp.concatenate(parts, axis=0).astype(BF)


def output_kernel(h_one, act, wout, out_ref, rows_f):
    mixed = nt(act[...], wout[...]).astype(BF).astype(F32)
    for lane in LANES:
        rows_f[pl.ds(0, HALF, stride=2), :] = h_one[:HALF, lane] + mixed[:, lane]
        rows_f[pl.ds(1, HALF, stride=2), :] = h_one[HALF:, lane] + mixed[:, lane]
        out_ref[0, :, lane] = rows_f[...].astype(BF)


def middle_kernel(in_ref, out_ref):
    total = in_ref[0].astype(F32)
    for i in range(1, X * YL):
        total = total + in_ref[i].astype(F32)
    for z in range(Z):
        for h in range(YH):
            if z < 3:
                piece = total[24 * h + 8 * z : 24 * h + 8 * z + 8]
            elif z < 7:
                piece = total[96 + 8 * (z - 3) : 96 + 8 * (z - 3) + 8]
            else:
                piece = jnp.zeros((8, C), F32)
            out_ref[YH * z + h] = piece.astype(BF)


def last_kernel(in_ref, out_ref):
    total = in_ref[0].astype(F32)
    for i in range(1, Z * YH):
        total = total + in_ref[i].astype(F32)
    total = total.astype(BF)
    for i in range(Z * X):
        out_ref[i] = total


def grads_kernel(
    in_ref, embed_ref, conv_ref, gemb_ref, gconv_hbm, gin_hbm, gout_hbm,
    gin_v, gout_v, gconv_v, sums, emb, left, back, sems,
):
    seq = where_am_i()[4]
    for x in range(X):
        for z in range(3):
            top = 24 * (x % 2) + 8 * z
            (gin_v if x < 2 else gout_v)[top : top + 8, :] = in_ref[X * z + x].astype(F32)
    copies = [
        pltpu.make_async_copy(gin_v, gin_hbm, sems.at[0]),
        pltpu.make_async_copy(gout_v, gout_hbm, sems.at[1]),
        pltpu.make_async_copy(gconv_v, gconv_hbm, sems.at[2]),
    ]
    copies[0].start()
    copies[1].start()
    for x in range(X):
        for z in range(3, 7):
            top = 32 * x + 8 * (z - 3)
            sums[top : top + 8, :] = in_ref[X * z + x].astype(F32)
    emb[...] = jnp.zeros_like(emb)
    stack_embed(embed_ref, emb, 0)
    pick = picker(seq)
    mine = nn(emb[...].astype(BF), pick)
    small = sums[...].astype(BF)
    left[...] = jnp.zeros_like(left)
    for k in range(TAPS):
        left[k, PAIRS * k : PAIRS * (k + 1), :] = mine[:PAIRS]
    for k in range(TAPS):
        gconv_v[k] = tn(left[k].astype(BF), small)
    copies[2].start()
    back[...] = nn(small, pick)
    total = back[TAPS * PAIRS : (TAPS + 1) * PAIRS, :]
    for k in range(TAPS):
        back[...] = nt(small, conv_ref[k])
        total = total + back[PAIRS * k : PAIRS * (k + 1), :]
    back[0:PAIRS, :] = total
    for j in range(TAPS):
        gemb_ref[j] = back[BASES * j : BASES * (j + 1), :]
    for copy in copies:
        copy.wait()


def call(body, outs, scratch, args, hbm=False, out_hbm=(), alias={}, flops=0):
    spec = pl.BlockSpec(memory_space=VMEM)
    far = pl.BlockSpec(memory_space=pltpu.HBM)
    if hbm:
        args = tuple(pltpu.with_memory_space_constraint(a, pltpu.HBM) for a in args)
    many = isinstance(outs, list)
    moved = sum(a.size * a.dtype.itemsize for a in args)
    return pl.pallas_call(
        body,
        out_shape=outs,
        in_specs=[far if hbm else spec] * len(args),
        out_specs=[far if i in out_hbm else spec for i in range(len(outs))] if many else spec,
        scratch_shapes=scratch,
        input_output_aliases=alias,
        compiler_params=pltpu.CompilerParams(vmem_limit_bytes=48 * 1024 * 1024),
        cost_estimate=pl.CostEstimate(flops=flops, bytes_accessed=moved, transcendentals=0),
        name=body.__name__,
    )(*args)


def array(*shape, dtype=BF):
    return jax.ShapeDtypeStruct(shape, dtype)


def exchange(pieces, axes):
    return lax.all_to_all(pieces, axes, 0, 0, tiled=True)


def local(bases, embed, conv_w, w_in, w_out, cotangent):
    packed = call(
        pack_kernel,
        array(YH * YL, 40, C),
        [
            VMEM((1, ROWS), jnp.int32),
            VMEM((TAPS, BASES, C), BF),
            VMEM((TAPS, SHARD, C), BF),
            VMEM((2, SHARD, C), BF),
            pltpu.SemaphoreType.DMA((5,)),
            VMEM((24, C), F32),
            VMEM((104, C), F32),
            VMEM((128, C), F32),
            VMEM((96, C), F32),
        ],
        (bases, embed, conv_w, w_in, w_out.T),
        hbm=True,
    )
    quarters = call(relay_kernel, array(X, 224, C), [], (exchange(packed, ("yh", "yl")),))
    swap = [(0, 1), (1, 0)]
    mine = exchange(quarters, "x")
    other = lax.ppermute(mine, "core", swap)
    win, wout, e_own, stem, dout, dmixed = call(
        own_kernel,
        [
            array(C, F),
            array(C, F),
            array(128, C, dtype=F32),
            array(128, C),
            array(ROWS, C, dtype=F32),
            array(HALF, C),
        ],
        [VMEM((128, C), F32), VMEM((ROWS, 128), F32)],
        (mine, embed, cotangent),
        flops=10**8,
    )
    keep, send, win, wout, e_own, h_one, act = call(
        step_kernel,
        [
            array(X * YL, 128, C),
            array(X * YL, 128, C),
            array(C, F),
            array(C, F),
            array(128, C, dtype=F32),
            array(ROWS, C, dtype=F32),
            array(HALF, F),
        ],
        [VMEM((C, F), F32), VMEM((C, F), F32)],
        (other, bases, win, wout, e_own, stem, dout, dmixed),
        alias={2: 2, 3: 3, 4: 4},
        flops=10**9,
    )
    came = lax.ppermute(send, "core", swap)
    output = call(output_kernel, array(1, ROWS, C), [VMEM((ROWS, 128), F32)], (h_one, act, wout), flops=10**8)
    pairs = (keep.astype(F32) + came.astype(F32)).astype(BF)
    pieces = call(middle_kernel, array(Z * YH, 8, C), [], (exchange(pairs, ("x", "yl")),))
    copies = call(last_kernel, array(Z * X, 8, C), [], (exchange(pieces, ("z", "yh")),))
    gathered = exchange(copies, ("z", "x"))
    g_embed, g_conv, g_in, g_out = call(
        grads_kernel,
        [
            array(TAPS, BASES, SHARD, dtype=F32),
            array(TAPS, SHARD, C, dtype=F32),
            array(SHARD, C, dtype=F32),
            array(SHARD, C, dtype=F32),
        ],
        [
            VMEM((SHARD, C), F32),
            VMEM((SHARD, C), F32),
            VMEM((TAPS, SHARD, C), F32),
            VMEM((128, C), F32),
            VMEM((24, C), F32),
            VMEM((TAPS, 128, SHARD), F32),
            VMEM((128, SHARD), F32),
            pltpu.SemaphoreType.DMA((3,)),
        ],
        (gathered, embed, conv_w),
        out_hbm=(1, 2, 3),
    )
    return output, g_embed, g_conv, g_in, g_out.T


def solution(mesh):
    mesh = Mesh(mesh.devices.reshape(Z, X, YH, CORE, YL), ("z", "x", "yh", "core", "yl"))
    seq = ("yh", "core")
    samples = ("z", "x", "yl")
    return jax.shard_map(
        local,
        mesh=mesh,
        in_specs=(
            P(samples, seq),
            P(),
            P(None, seq, None),
            P(seq, "yl"),
            P("yl", seq),
            P(samples, seq, None),
        ),
        out_specs=(
            P(samples, seq, None),
            P(None, None, seq),
            P(None, seq, None),
            P(seq, "yl"),
            P("yl", seq),
        ),
        check_vma=False,
    )
```

```python
import jax
import jax.numpy as jnp
from jax import lax
from jax.experimental import pallas as pl
from jax.experimental.pallas import tpu as pltpu
from jax.sharding import Mesh
from jax.sharding import PartitionSpec as P

Z, X, YH, CORE, YL = 8, 4, 4, 2, 2
TAPS = 5
BASES = 4
C = 384
F = 768
ROWS = 256
HALF = 128
LENGTH = 2048
SHARD = 48
PAIRS = TAPS * BASES
BF = jnp.bfloat16
F32 = jnp.float32
VMEM = pltpu.VMEM
LANES = [slice(128 * i, 128 * (i + 1)) for i in range(C // 128)]
GELU_C = 0.7978845608028654
GELU_A = 0.044715


def dot(a, b, dims):
    return lax.dot_general(a, b, (dims, ((), ())), preferred_element_type=F32)


def nn(a, b):
    return dot(a, b, ((1,), (0,)))


def nt(a, b):
    return dot(a, b, ((1,), (1,)))


def tn(a, b):
    return dot(a, b, ((0,), (0,)))


def iota(shape, dim):
    return lax.broadcasted_iota(jnp.int32, shape, dim)


def gelu_both(x):
    x2 = x * x
    t = jnp.tanh(GELU_C * (x + GELU_A * (x * x2)))
    half = 0.5 * (1.0 + t)
    slope = half + 0.5 * x * (1.0 - t * t) * (GELU_C * (1.0 + 3.0 * GELU_A * x2))
    return x * half, slope


def where_am_i():
    x, yh, core, yl = (lax.axis_index(name) for name in ("x", "yh", "core", "yl"))
    return x, yh, core, yl, yh * CORE + core


def stack_embed(embed_ref, scratch, top):
    for j in range(TAPS):
        scratch[top + BASES * j : top + BASES * (j + 1), :] = embed_ref[j].astype(F32)


def picker(seq):
    return (iota((C, SHARD), 0) == iota((C, SHARD), 1) + seq * SHARD).astype(BF)


def pack_kernel(
    ids_hbm, embed_hbm, conv_hbm, win_hbm, wout_hbm, out_ref,
    ids_v, embed_v, conv_v, shard_v, sems, emb, esum, tail, shard_f,
):
    x, yh, core, yl, seq = where_am_i()
    copies = [
        pltpu.make_async_copy(src, dst, sems.at[i])
        for i, (src, dst) in enumerate(
            (
                (embed_hbm, embed_v),
                (conv_hbm, conv_v),
                (win_hbm, shard_v.at[0]),
                (wout_hbm, shard_v.at[1]),
                (ids_hbm, ids_v),
            )
        )
    ]
    for copy in copies:
        copy.start()
    emb[...] = jnp.zeros_like(emb)
    esum[...] = jnp.zeros_like(esum)
    tail[...] = jnp.zeros_like(tail)
    copies[0].wait()
    stack_embed(embed_v, emb, 0)
    mine = nn(emb[...].astype(BF), picker(seq)).astype(BF)
    copies[1].wait()
    for k in range(TAPS):
        esum[PAIRS * k : PAIRS * (k + 1), :] = nn(mine, conv_v[k])[:PAIRS]
    for q in range(X * YL):
        tail[16 * q : 16 * q + 13, :] = esum[13 * q : 13 * q + 13, :]
    part = tail[pl.ds(pl.multiple_of((YL * x + yl) * 16, 16), 16), :]
    for copy in copies[2:]:
        copy.wait()
    ids = jnp.concatenate([ids_v[...].astype(F32), jnp.zeros((1, C - ROWS), F32)], axis=1)
    part = jnp.where(iota((16, C), 0) == 15, ids, part)
    shard_f[0:48, :] = shard_v[0].astype(F32)
    shard_f[48:96, :] = shard_v[1].astype(F32)
    piece = shard_f[pl.ds(pl.multiple_of(24 * x, 8), 24), :]
    piece = jnp.concatenate([piece, part], axis=0).astype(BF)
    for d in range(YH * YL):
        out_ref[d] = piece


def relay_kernel(in_ref, out_ref):
    yl = where_am_i()[3]
    got = [in_ref[p].astype(F32) for p in range(YH * YL)]
    sums = [sum(got[YL * h + half][24:40] for h in range(YH)) for half in range(YL)]
    row = iota((16, C), 0)
    for h in range(YH):
        ids = in_ref[YL * h + yl].astype(F32)[39:40]
        sums[h // 2] = jnp.where(row == 13 + h % 2, ids, sums[h // 2])
    piece = jnp.concatenate([g[:24] for g in got] + sums, axis=0).astype(BF)
    for x in range(X):
        out_ref[x] = piece


def fill_weights(core, got, win, wout):
    for h in range(YH):
        top = pl.multiple_of((CORE * h + core) * SHARD, SHARD)
        for half in range(YL):
            cols = slice(C * half, C * (half + 1))
            p = 24 * (YL * h + half)
            for ref, first in ((win, 0), (wout, 2)):
                ref[pl.ds(top, SHARD), cols] = jnp.concatenate(
                    [got[first, p : p + 24, :], got[first + 1, p : p + 24, :]], axis=0
                )


def add_e(got, ebuf):
    for x in range(X):
        for half in range(YL):
            p = 192 + 16 * half
            q = 13 * (YL * x + half)
            ebuf[q : q + 13, :] = ebuf[q : q + 13, :] + got[x, p : p + 16, :].astype(F32)[:13]


def own_kernel(own, embed_ref, cot_ref, win, wout, ebuf, stem, dout, dmixed, embf, rows_f):
    core = where_am_i()[2]
    fill_weights(core, own, win, wout)
    ebuf[...] = jnp.zeros_like(ebuf)
    add_e(own, ebuf)
    embf[...] = jnp.zeros_like(embf)
    stack_embed(embed_ref, embf, TAPS * PAIRS)
    stem[...] = embf[...].astype(BF)
    for lane in LANES:
        rows_f[...] = cot_ref[0, :, lane].astype(F32)
        even = rows_f[pl.ds(0, HALF, stride=2), :]
        odd = rows_f[pl.ds(1, HALF, stride=2), :]
        dout[:HALF, lane] = even
        dout[HALF:, lane] = odd
        dmixed[:, lane] = (even + odd).astype(BF)


def step_kernel(
    oth, ids_ref, win_in, wout_in, ebuf_in, stem, dout, dmixed_ref,
    keep_ref, send_ref, win, wout, ebuf, h_out, act_out,
    grad_a, grad_b,
):
    x_mine, yh, core, yl, seq = where_am_i()
    fill_weights(1 - core, oth, win, wout)
    add_e(oth, ebuf)
    e_full = ebuf[...]
    e_hi = e_full.astype(BF)
    e_lo = (e_full - e_hi.astype(F32)).astype(BF)
    before = jnp.maximum(yh - (1 - core), 0)
    after = jnp.minimum(yh + core, YH - 1)
    near = oth[x_mine, 192:224, :].astype(F32)[:, :ROWS]
    row = iota((32, ROWS), 0)

    def ids_of(h):
        at = 16 * jnp.right_shift(h, 1) + 13 + jnp.bitwise_and(h, 1)
        line = jnp.sum(jnp.where(row == at, near, 0.0), axis=0, keepdims=True)
        return jnp.broadcast_to(line, (8, ROWS))

    id_prev = jnp.where(seq == 0, -1.0, ids_of(before)[:, 128:])
    id_next = jnp.where(seq == YH * CORE - 1, -1.0, ids_of(after)[:, :128])
    id_mid = jnp.broadcast_to(ids_ref[...].astype(F32), (8, ROWS))
    line = jnp.concatenate([id_prev, id_mid, id_next], axis=1)
    m = iota((HALF, ROWS), 0)
    k = sum((m >= PAIRS * q).astype(jnp.int32) for q in range(1, TAPS + 1))
    rest = m - PAIRS * k
    k = jnp.where(m >= PAIRS * TAPS, 2, k)
    j = jnp.right_shift(rest, 2)
    base = jnp.bitwise_and(rest, 3)
    seen = jnp.full((HALF, ROWS), -2.0, F32)
    for o in range(2 * TAPS - 1):
        moved = pltpu.roll(line, (4 - o) % 512, 1)[:, 128 : 128 + ROWS]
        seen = jnp.where(k + j == o, jnp.concatenate([moved] * (HALF // 8), axis=0), seen)
    at = seq * ROWS + iota((HALF, ROWS), 1) + k - 2
    hit = (at >= 0) & (at < LENGTH) & (m < PAIRS * (TAPS + 1)) & (seen == base.astype(F32))
    onehot = jnp.where(hit, 1.0, 0.0).astype(BF)
    src = iota((ROWS, ROWS), 0)
    dst = iota((ROWS, ROWS), 1)
    order = jnp.where(dst < HALF, 2 * dst, 2 * dst - (ROWS - 1))
    onehot = nn(onehot, (src == order).astype(BF))
    onehot_t = onehot.T.astype(BF)
    onehot = onehot.astype(BF)
    z = nn(onehot_t, e_hi) + nn(onehot_t, e_lo)
    h_zero = nn(onehot_t, stem[...]).astype(BF).astype(F32)
    g_z, s_z = gelu_both(z)
    h_one = (h_zero + g_z).astype(BF).astype(F32)
    even, odd = h_one[:HALF], h_one[HALF:]
    pooled = ((even + odd) * 0.5).astype(BF).astype(F32)
    scale = lax.rsqrt(jnp.mean(pooled * pooled, axis=-1, keepdims=True) + 1e-06)
    normed = (pooled * scale).astype(BF)
    w_in = win[...]
    w_out = wout[...]
    pre = nn(normed, w_in)
    g_p, s_p = gelu_both(pre)
    act = g_p.astype(BF)
    h_out[...] = h_one
    act_out[...] = act
    dmixed = dmixed_ref[...]
    d_even, d_odd = dout[:HALF, :], dout[HALF:, :]
    dact = nn(dmixed, w_out)
    dpre = (dact * s_p).astype(BF)
    dnormed = nt(dpre, w_in)
    dpooled = scale * dnormed - pooled * (scale * scale * scale) * jnp.mean(
        dnormed * pooled, axis=-1, keepdims=True
    )
    add = dpooled * 0.5
    dh_one = jnp.concatenate([d_even + add, d_odd + add], axis=0)
    dz = (dh_one * s_z).astype(BF)
    d_hi = dh_one.astype(BF)
    d_lo = (dh_one - d_hi.astype(F32)).astype(BF)
    small = jnp.where(
        iota((HALF, C), 0) < TAPS * PAIRS, nn(onehot, dz), nn(onehot, d_hi) + nn(onehot, d_lo)
    )
    ebuf[...] = small
    grad_a[...] = tn(normed, dpre)
    grad_b[...] = tn(dmixed, act)
    for which, ref in ((core, keep_ref), (1 - core, send_ref)):
        for x in range(X):
            grad = grad_a if x < 2 else grad_b
            for half in range(YL):
                cols = slice(C * half, C * (half + 1))
                parts = []
                for h in range(YH):
                    top = pl.multiple_of((2 * h + which) * SHARD + 24 * (x % 2), 8)
                    parts.append(grad[pl.ds(top, 24), cols])
                parts.append(ebuf[32 * x : 32 * x + 32, :])
                ref[YL * x + half] = jnp.concatenate(parts, axis=0).astype(BF)


def output_kernel(h_one, act, wout, out_ref, rows_f):
    mixed = nt(act[...], wout[...]).astype(BF).astype(F32)
    for lane in LANES:
        rows_f[pl.ds(0, HALF, stride=2), :] = h_one[:HALF, lane] + mixed[:, lane]
        rows_f[pl.ds(1, HALF, stride=2), :] = h_one[HALF:, lane] + mixed[:, lane]
        out_ref[0, :, lane] = rows_f[...].astype(BF)


def middle_kernel(in_ref, out_ref):
    total = in_ref[0].astype(F32)
    for i in range(1, X * YL):
        total = total + in_ref[i].astype(F32)
    for z in range(Z):
        for h in range(YH):
            if z < 3:
                piece = total[24 * h + 8 * z : 24 * h + 8 * z + 8]
            elif z < 7:
                piece = total[96 + 8 * (z - 3) : 96 + 8 * (z - 3) + 8]
            else:
                piece = jnp.zeros((8, C), F32)
            out_ref[YH * z + h] = piece.astype(BF)


def last_kernel(in_ref, out_ref):
    total = in_ref[0].astype(F32)
    for i in range(1, Z * YH):
        total = total + in_ref[i].astype(F32)
    total = total.astype(BF)
    for i in range(Z * X):
        out_ref[i] = total


def grads_kernel(
    in_ref, embed_ref, conv_ref, gemb_hbm, gconv_hbm, gin_hbm, gout_hbm,
    gemb_v, gin_v, gout_v, gconv_v, sums, emb, left, back, sems,
):
    seq = where_am_i()[4]
    emb[...] = jnp.zeros_like(emb)
    stack_embed(embed_ref, emb, 0)
    pick = picker(seq)
    mine = nn(emb[...].astype(BF), pick)
    left[...] = jnp.zeros_like(left)
    for k in range(TAPS):
        left[k, PAIRS * k : PAIRS * (k + 1), :] = mine[:PAIRS]
    for x in range(X):
        for z in range(3, 7):
            top = 32 * x + 8 * (z - 3)
            sums[top : top + 8, :] = in_ref[X * z + x].astype(F32)
    small = sums[...].astype(BF)
    for k in range(TAPS):
        gconv_v[k] = tn(left[k].astype(BF), small)
    copies = [
        pltpu.make_async_copy(src, dst, sems.at[i])
        for i, (src, dst) in enumerate(
            ((gconv_v, gconv_hbm), (gin_v, gin_hbm), (gout_v, gout_hbm), (gemb_v, gemb_hbm))
        )
    ]
    copies[0].start()
    for k in range(TAPS):
        back[k] = nt(small, conv_ref[k])
    back[TAPS] = nn(small, pick)
    total = sum(back[k, PAIRS * k : PAIRS * (k + 1), :] for k in range(TAPS + 1))
    for j in range(TAPS):
        gemb_v[j] = total[BASES * j : BASES * (j + 1)]
    copies[3].start()
    for x in range(X):
        for z in range(3):
            top = 24 * (x % 2) + 8 * z
            (gin_v if x < 2 else gout_v)[top : top + 8, :] = in_ref[X * z + x].astype(F32)
    copies[1].start()
    copies[2].start()
    for copy in copies:
        copy.wait()


def call(body, outs, scratch, args, hbm=False, out_hbm=(), alias={}, flops=0):
    spec = pl.BlockSpec(memory_space=VMEM)
    far = pl.BlockSpec(memory_space=pltpu.HBM)
    if hbm:
        args = tuple(pltpu.with_memory_space_constraint(a, pltpu.HBM) for a in args)
    many = isinstance(outs, list)
    moved = sum(a.size * a.dtype.itemsize for a in args)
    return pl.pallas_call(
        body,
        out_shape=outs,
        in_specs=[far if hbm else spec] * len(args),
        out_specs=[far if i in out_hbm else spec for i in range(len(outs))] if many else spec,
        scratch_shapes=scratch,
        input_output_aliases=alias,
        compiler_params=pltpu.CompilerParams(vmem_limit_bytes=48 * 1024 * 1024),
        cost_estimate=pl.CostEstimate(flops=flops, bytes_accessed=moved, transcendentals=0),
        name=body.__name__,
    )(*args)


def array(*shape, dtype=BF):
    return jax.ShapeDtypeStruct(shape, dtype)


def exchange(pieces, axes):
    return lax.all_to_all(pieces, axes, 0, 0, tiled=True)


def local(bases, embed, conv_w, w_in, w_out, cotangent):
    packed = call(
        pack_kernel,
        array(YH * YL, 40, C),
        [
            VMEM((1, ROWS), jnp.int32),
            VMEM((TAPS, BASES, C), BF),
            VMEM((TAPS, SHARD, C), BF),
            VMEM((2, SHARD, C), BF),
            pltpu.SemaphoreType.DMA((5,)),
            VMEM((24, C), F32),
            VMEM((104, C), F32),
            VMEM((128, C), F32),
            VMEM((96, C), F32),
        ],
        (bases, embed, conv_w, w_in, w_out.T),
        hbm=True,
    )
    quarters = call(relay_kernel, array(X, 224, C), [], (exchange(packed, ("yh", "yl")),))
    swap = [(0, 1), (1, 0)]
    mine = exchange(quarters, "x")
    other = lax.ppermute(mine, "core", swap)
    win, wout, e_own, stem, dout, dmixed = call(
        own_kernel,
        [
            array(C, F),
            array(C, F),
            array(128, C, dtype=F32),
            array(128, C),
            array(ROWS, C, dtype=F32),
            array(HALF, C),
        ],
        [VMEM((128, C), F32), VMEM((ROWS, 128), F32)],
        (mine, embed, cotangent),
        flops=10**8,
    )
    keep, send, win, wout, e_own, h_one, act = call(
        step_kernel,
        [
            array(X * YL, 128, C),
            array(X * YL, 128, C),
            array(C, F),
            array(C, F),
            array(128, C, dtype=F32),
            array(ROWS, C, dtype=F32),
            array(HALF, F),
        ],
        [VMEM((C, F), F32), VMEM((C, F), F32)],
        (other, bases, win, wout, e_own, stem, dout, dmixed),
        alias={2: 2, 3: 3, 4: 4},
        flops=10**9,
    )
    came = lax.ppermute(send, "core", swap)
    output = call(output_kernel, array(1, ROWS, C), [VMEM((ROWS, 128), F32)], (h_one, act, wout), flops=10**8)
    came, output = lax.optimization_barrier((came, output))
    pairs = (keep.astype(F32) + came.astype(F32)).astype(BF)
    pieces = call(middle_kernel, array(Z * YH, 8, C), [], (exchange(pairs, ("x", "yl")),))
    copies = call(last_kernel, array(Z * X, 8, C), [], (exchange(pieces, ("z", "yh")),))
    gathered = exchange(copies, ("z", "x"))
    g_embed, g_conv, g_in, g_out = call(
        grads_kernel,
        [
            array(TAPS, BASES, SHARD, dtype=F32),
            array(TAPS, SHARD, C, dtype=F32),
            array(SHARD, C, dtype=F32),
            array(SHARD, C, dtype=F32),
        ],
        [
            VMEM((TAPS, BASES, SHARD), F32),
            VMEM((SHARD, C), F32),
            VMEM((SHARD, C), F32),
            VMEM((TAPS, SHARD, C), F32),
            VMEM((128, C), F32),
            VMEM((24, C), F32),
            VMEM((TAPS, 128, SHARD), F32),
            VMEM((TAPS + 1, 128, SHARD), F32),
            pltpu.SemaphoreType.DMA((4,)),
        ],
        (gathered, embed, conv_w),
        out_hbm=(0, 1, 2, 3),
    )
    return output, g_embed, g_conv, g_in, g_out.T


def solution(mesh):
    mesh = Mesh(mesh.devices.reshape(Z, X, YH, CORE, YL), ("z", "x", "yh", "core", "yl"))
    seq = ("yh", "core")
    samples = ("z", "x", "yl")
    return jax.shard_map(
        local,
        mesh=mesh,
        in_specs=(
            P(samples, seq),
            P(),
            P(None, seq, None),
            P(seq, "yl"),
            P("yl", seq),
            P(samples, seq, None),
        ),
        out_specs=(
            P(samples, seq, None),
            P(None, None, seq),
            P(None, seq, None),
            P(seq, "yl"),
            P("yl", seq),
        ),
        check_vma=False,
    )
```

```python
import jax
import jax.numpy as jnp
from jax import lax
from jax.experimental import pallas as pl
from jax.experimental.pallas import tpu as pltpu
from jax.sharding import Mesh
from jax.sharding import PartitionSpec as P

Z, X, YH, CORE, YL = 8, 4, 4, 2, 2
TAPS = 5
BASES = 4
C = 384
F = 768
ROWS = 256
HALF = 128
LENGTH = 2048
SHARD = 48
PAIRS = TAPS * BASES
ENDS = [(0, 3), (0, 4), (1, 3), (1, 4), (3, 0), (3, 1), (4, 0), (4, 1)]
END_ROW = BASES * (2 * TAPS - 1)
STEM_ROW = END_ROW + BASES * len(ENDS)
SMALL = 96
BF = jnp.bfloat16
F32 = jnp.float32
VMEM = pltpu.VMEM
LANES = [slice(128 * i, 128 * (i + 1)) for i in range(C // 128)]
GELU_C = 0.7978845608028654
GELU_A = 0.044715


def dot(a, b, dims):
    return lax.dot_general(a, b, (dims, ((), ())), preferred_element_type=F32)


def nn(a, b):
    return dot(a, b, ((1,), (0,)))


def nt(a, b):
    return dot(a, b, ((1,), (1,)))


def tn(a, b):
    return dot(a, b, ((0,), (0,)))


def iota(shape, dim):
    return lax.broadcasted_iota(jnp.int32, shape, dim)


def gelu_both(x):
    x2 = x * x
    t = jnp.tanh(GELU_C * (x + GELU_A * (x * x2)))
    half = 0.5 * (1.0 + t)
    slope = half + 0.5 * x * (1.0 - t * t) * (GELU_C * (1.0 + 3.0 * GELU_A * x2))
    return x * half, slope


def where_am_i():
    x, yh, core, yl = (lax.axis_index(name) for name in ("x", "yh", "core", "yl"))
    return x, yh, core, yl, yh * CORE + core


def stack_embed(embed_ref, scratch, top):
    for j in range(TAPS):
        scratch[top + BASES * j : top + BASES * (j + 1), :] = embed_ref[j].astype(F32)


def picker(seq):
    return (iota((C, SHARD), 0) == iota((C, SHARD), 1) + seq * SHARD).astype(BF)


def pack_kernel(
    ids_hbm, embed_hbm, conv_hbm, win_hbm, wout_hbm, out_ref,
    ids_v, embed_v, conv_v, shard_v, sems, emb, esum, tail, shard_f,
):
    x, yh, core, yl, seq = where_am_i()
    copies = [
        pltpu.make_async_copy(src, dst, sems.at[i])
        for i, (src, dst) in enumerate(
            (
                (embed_hbm, embed_v),
                (conv_hbm, conv_v),
                (win_hbm, shard_v.at[0]),
                (wout_hbm, shard_v.at[1]),
                (ids_hbm, ids_v),
            )
        )
    ]
    for copy in copies:
        copy.start()
    emb[...] = jnp.zeros_like(emb)
    esum[...] = jnp.zeros_like(esum)
    tail[...] = jnp.zeros_like(tail)
    copies[0].wait()
    stack_embed(embed_v, emb, 0)
    mine = nn(emb[...].astype(BF), picker(seq)).astype(BF)
    copies[1].wait()
    for k in range(TAPS):
        esum[PAIRS * k : PAIRS * (k + 1), :] = nn(mine, conv_v[k])[:PAIRS]
    for q in range(X * YL):
        tail[16 * q : 16 * q + 13, :] = esum[13 * q : 13 * q + 13, :]
    part = tail[pl.ds(pl.multiple_of((YL * x + yl) * 16, 16), 16), :]
    for copy in copies[2:]:
        copy.wait()
    ids = jnp.concatenate([ids_v[...].astype(F32), jnp.zeros((1, C - ROWS), F32)], axis=1)
    part = jnp.where(iota((16, C), 0) == 15, ids, part)
    shard_f[0:48, :] = shard_v[0].astype(F32)
    shard_f[48:96, :] = shard_v[1].astype(F32)
    piece = shard_f[pl.ds(pl.multiple_of(24 * x, 8), 24), :]
    piece = jnp.concatenate([piece, part], axis=0).astype(BF)
    for d in range(YH * YL):
        out_ref[d] = piece


def relay_kernel(in_ref, out_ref):
    yl = where_am_i()[3]
    got = [in_ref[p].astype(F32) for p in range(YH * YL)]
    sums = [sum(got[YH * half + h][24:40] for h in range(YH)) for half in range(YL)]
    row = iota((16, C), 0)
    for h in range(YH):
        ids = in_ref[YH * yl + h].astype(F32)[39:40]
        sums[h // 2] = jnp.where(row == 13 + h % 2, ids, sums[h // 2])
    piece = jnp.concatenate([g[:24] for g in got] + sums, axis=0).astype(BF)
    for x in range(X):
        out_ref[x] = piece


def fill_weights(core, got, win, wout):
    for h in range(YH):
        top = pl.multiple_of((CORE * h + core) * SHARD, SHARD)
        for half in range(YL):
            cols = slice(C * half, C * (half + 1))
            p = 24 * (YH * half + h)
            for ref, first in ((win, 0), (wout, 2)):
                ref[pl.ds(top, SHARD), cols] = jnp.concatenate(
                    [got[first, p : p + 24, :], got[first + 1, p : p + 24, :]], axis=0
                )


def add_e(got, ebuf):
    for x in range(X):
        for half in range(YL):
            p = 192 + 16 * half
            q = 13 * (YL * x + half)
            ebuf[q : q + 13, :] = ebuf[q : q + 13, :] + got[x, p : p + 16, :].astype(F32)[:13]


def own_kernel(
    own, embed_ref, cot_ref, win, wout, ebuf, stem, dout, dmixed, left, pick_ref, embf, rows_f, emb, leftf
):
    x_mine, yh, core, yl, seq = where_am_i()
    pick = picker(seq)
    pick_ref[...] = pick
    emb[...] = jnp.zeros_like(emb)
    stack_embed(embed_ref, emb, 0)
    mine = nn(emb[...].astype(BF), pick)
    leftf[...] = jnp.zeros_like(leftf)
    for k in range(TAPS):
        leftf[k, BASES * k : BASES * k + PAIRS, :] = mine[:PAIRS]
    for q, (k, j) in enumerate(ENDS):
        leftf[k, END_ROW + BASES * q : END_ROW + BASES * (q + 1), :] = -mine[BASES * j : BASES * (j + 1)]
    left[...] = leftf[...].astype(BF)
    fill_weights(core, own, win, wout)
    ebuf[...] = jnp.zeros_like(ebuf)
    add_e(own, ebuf)
    embf[...] = jnp.zeros_like(embf)
    stack_embed(embed_ref, embf, TAPS * PAIRS)
    stem[...] = embf[...].astype(BF)
    for lane in LANES:
        rows_f[...] = cot_ref[0, :, lane].astype(F32)
        even = rows_f[pl.ds(0, HALF, stride=2), :]
        odd = rows_f[pl.ds(1, HALF, stride=2), :]
        dout[:HALF, lane] = even
        dout[HALF:, lane] = odd
        dmixed[:, lane] = (even + odd).astype(BF)


def step_kernel(
    oth, ids_ref, win_in, wout_in, ebuf_in, stem, dout, dmixed_ref,
    keep_ref, send_ref, win, wout, ebuf, h_out, act_out,
    grad_a, grad_b, small,
):
    x_mine, yh, core, yl, seq = where_am_i()
    fill_weights(1 - core, oth, win, wout)
    add_e(oth, ebuf)
    e_full = ebuf[...]
    e_hi = e_full.astype(BF)
    e_lo = (e_full - e_hi.astype(F32)).astype(BF)
    before = jnp.maximum(yh - (1 - core), 0)
    after = jnp.minimum(yh + core, YH - 1)
    near = oth[x_mine, 192:224, :].astype(F32)[:, :ROWS]
    row = iota((32, ROWS), 0)

    def ids_of(h):
        at = 16 * jnp.right_shift(h, 1) + 13 + jnp.bitwise_and(h, 1)
        line = jnp.sum(jnp.where(row == at, near, 0.0), axis=0, keepdims=True)
        return jnp.broadcast_to(line, (8, ROWS))

    id_prev = jnp.where(seq == 0, -1.0, ids_of(before)[:, 128:])
    id_next = jnp.where(seq == YH * CORE - 1, -1.0, ids_of(after)[:, :128])
    id_mid = jnp.broadcast_to(ids_ref[...].astype(F32), (8, ROWS))
    line = jnp.concatenate([id_prev, id_mid, id_next], axis=1)
    near_ids = [pltpu.roll(line, (4 - o) % 512, 1)[:, 128 : 128 + ROWS] for o in range(2 * TAPS - 1)]

    def matches(offset, base):
        rows = offset.shape[0]
        seen = jnp.full((rows, ROWS), -2.0, F32)
        for o in range(2 * TAPS - 1):
            seen = jnp.where(offset == o, jnp.concatenate([near_ids[o]] * (rows // 8), axis=0), seen)
        return seen == base.astype(F32)

    def outside(k):
        at = seq * ROWS + iota(k.shape, 1) + k - 2
        return (at < 0) | (at >= LENGTH)

    m = iota((HALF, ROWS), 0)
    k = sum((m >= PAIRS * q).astype(jnp.int32) for q in range(1, TAPS + 1))
    rest = m - PAIRS * k
    k = jnp.where(m >= PAIRS * TAPS, 2, k)
    hit = matches(k + jnp.right_shift(rest, 2), jnp.bitwise_and(rest, 3))
    hit = hit & jnp.logical_not(outside(k)) & (m < PAIRS * (TAPS + 1))
    onehot = jnp.where(hit, 1.0, 0.0).astype(BF)
    m = iota((SMALL, ROWS), 0)
    group = jnp.right_shift(m, 2)
    k = jnp.full((SMALL, ROWS), 2, jnp.int32)
    offset = jnp.where(m < END_ROW, group, group - STEM_ROW // BASES + 2)
    for q, (tap, j) in enumerate(ENDS):
        here = group == END_ROW // BASES + q
        k = jnp.where(here, tap, k)
        offset = jnp.where(here, tap + j, offset)
    ends = (m >= END_ROW) & (m < STEM_ROW)
    hit = matches(offset, jnp.bitwise_and(m, 3)) & (m < STEM_ROW + PAIRS)
    hit = hit & (jnp.logical_not(ends) | outside(k))
    small_hot = jnp.where(hit, 1.0, 0.0).astype(BF)
    src = iota((ROWS, ROWS), 0)
    dst = iota((ROWS, ROWS), 1)
    order = jnp.where(dst < HALF, 2 * dst, 2 * dst - (ROWS - 1))
    order = (src == order).astype(BF)
    onehot_t = nn(onehot, order).T.astype(BF)
    small_hot = nn(small_hot, order).astype(BF)
    z = nn(onehot_t, e_hi) + nn(onehot_t, e_lo)
    h_zero = nn(onehot_t, stem[...]).astype(BF).astype(F32)
    g_z, s_z = gelu_both(z)
    h_one = (h_zero + g_z).astype(BF).astype(F32)
    even, odd = h_one[:HALF], h_one[HALF:]
    pooled = ((even + odd) * 0.5).astype(BF).astype(F32)
    scale = lax.rsqrt(jnp.mean(pooled * pooled, axis=-1, keepdims=True) + 1e-06)
    normed = (pooled * scale).astype(BF)
    w_in = win[...]
    w_out = wout[...]
    pre = nn(normed, w_in)
    g_p, s_p = gelu_both(pre)
    act = g_p.astype(BF)
    h_out[...] = h_one
    act_out[...] = act
    dmixed = dmixed_ref[...]
    d_even, d_odd = dout[:HALF, :], dout[HALF:, :]
    dact = nn(dmixed, w_out)
    dpre = (dact * s_p).astype(BF)
    dnormed = nt(dpre, w_in)
    dpooled = scale * dnormed - pooled * (scale * scale * scale) * jnp.mean(
        dnormed * pooled, axis=-1, keepdims=True
    )
    add = dpooled * 0.5
    dh_one = jnp.concatenate([d_even + add, d_odd + add], axis=0)
    dz = (dh_one * s_z).astype(BF)
    d_hi = dh_one.astype(BF)
    d_lo = (dh_one - d_hi.astype(F32)).astype(BF)
    small[...] = jnp.where(
        iota((SMALL, C), 0) < STEM_ROW, nn(small_hot, dz), nn(small_hot, d_hi) + nn(small_hot, d_lo)
    )
    grad_a[...] = tn(normed, dpre)
    grad_b[...] = tn(dmixed, act)
    for which, ref in ((core, keep_ref), (1 - core, send_ref)):
        for x in range(X):
            grad = grad_a if x < 2 else grad_b
            for half in range(YL):
                cols = slice(C * half, C * (half + 1))
                parts = []
                for h in range(YH):
                    top = pl.multiple_of((2 * h + which) * SHARD + 24 * (x % 2), 8)
                    parts.append(grad[pl.ds(top, 24), cols])
                parts.append(small[24 * x : 24 * x + 24, :])
                ref[YL * x + half] = jnp.concatenate(parts, axis=0).astype(BF)


def output_kernel(h_one, act, wout, out_ref, rows_f):
    mixed = nt(act[...], wout[...]).astype(BF).astype(F32)
    for lane in LANES:
        rows_f[pl.ds(0, HALF, stride=2), :] = h_one[:HALF, lane] + mixed[:, lane]
        rows_f[pl.ds(1, HALF, stride=2), :] = h_one[HALF:, lane] + mixed[:, lane]
        out_ref[0, :, lane] = rows_f[...].astype(BF)


def middle_kernel(in_ref, out_ref):
    total = in_ref[0].astype(F32)
    for i in range(1, X * YL):
        total = total + in_ref[i].astype(F32)
    for z in range(Z):
        for h in range(YH):
            if z < 3:
                piece = total[24 * h + 8 * z : 24 * h + 8 * z + 8]
            elif z < 6:
                piece = total[96 + 8 * (z - 3) : 96 + 8 * (z - 3) + 8]
            else:
                piece = jnp.zeros((8, C), F32)
            out_ref[YH * z + h] = piece.astype(BF)


def last_kernel(in_ref, out_ref):
    total = in_ref[0].astype(F32)
    for i in range(1, Z * YH):
        total = total + in_ref[i].astype(F32)
    total = total.astype(BF)
    for i in range(Z * X):
        out_ref[i] = total


def grads_kernel(
    in_ref, left, pick, conv_ref, gemb_hbm, gconv_hbm, gin_hbm, gout_hbm,
    gemb_v, gin_v, gout_v, gconv_v, sums, back, sems,
):
    for x in range(X):
        for z in range(3, 6):
            top = 24 * x + 8 * (z - 3)
            sums[top : top + 8, :] = in_ref[X * z + x].astype(F32)
    small = sums[...].astype(BF)
    for k in range(TAPS):
        gconv_v[k] = tn(left[k], small)
    copies = [
        pltpu.make_async_copy(src, dst, sems.at[i])
        for i, (src, dst) in enumerate(
            ((gconv_v, gconv_hbm), (gin_v, gin_hbm), (gout_v, gout_hbm), (gemb_v, gemb_hbm))
        )
    ]
    copies[0].start()
    for k in range(TAPS):
        back[k] = nt(small, conv_ref[k])
    back[TAPS] = nn(small, pick[...])
    back[TAPS, 0:PAIRS, :] = back[TAPS, STEM_ROW : STEM_ROW + PAIRS, :] + sum(
        back[k, BASES * k : BASES * k + PAIRS, :] for k in range(TAPS)
    )
    for j in range(TAPS):
        rows = back[TAPS, BASES * j : BASES * (j + 1), :]
        for q, (k, tap) in enumerate(ENDS):
            if tap == j:
                rows = rows - back[k, END_ROW + BASES * q : END_ROW + BASES * (q + 1), :]
        gemb_v[j] = rows
    copies[3].start()
    for x in range(X):
        for z in range(3):
            top = 24 * (x % 2) + 8 * z
            (gin_v if x < 2 else gout_v)[top : top + 8, :] = in_ref[X * z + x].astype(F32)
    copies[1].start()
    copies[2].start()
    for copy in copies:
        copy.wait()


def call(body, outs, scratch, args, hbm=False, out_hbm=(), alias={}, flops=0):
    spec = pl.BlockSpec(memory_space=VMEM)
    far = pl.BlockSpec(memory_space=pltpu.HBM)
    if hbm:
        args = tuple(pltpu.with_memory_space_constraint(a, pltpu.HBM) for a in args)
    many = isinstance(outs, list)
    moved = sum(a.size * a.dtype.itemsize for a in args)
    return pl.pallas_call(
        body,
        out_shape=outs,
        in_specs=[far if hbm else spec] * len(args),
        out_specs=[far if i in out_hbm else spec for i in range(len(outs))] if many else spec,
        scratch_shapes=scratch,
        input_output_aliases=alias,
        compiler_params=pltpu.CompilerParams(vmem_limit_bytes=48 * 1024 * 1024),
        cost_estimate=pl.CostEstimate(flops=flops, bytes_accessed=moved, transcendentals=0),
        name=body.__name__,
    )(*args)


def array(*shape, dtype=BF):
    return jax.ShapeDtypeStruct(shape, dtype)


def exchange(pieces, axes):
    return lax.all_to_all(pieces, axes, 0, 0, tiled=True)


def local(bases, embed, conv_w, w_in, w_out, cotangent):
    packed = call(
        pack_kernel,
        array(YH * YL, 40, C),
        [
            VMEM((1, ROWS), jnp.int32),
            VMEM((TAPS, BASES, C), BF),
            VMEM((TAPS, SHARD, C), BF),
            VMEM((2, SHARD, C), BF),
            pltpu.SemaphoreType.DMA((5,)),
            VMEM((24, C), F32),
            VMEM((104, C), F32),
            VMEM((128, C), F32),
            VMEM((96, C), F32),
        ],
        (bases, embed, conv_w, w_in, w_out.T),
        hbm=True,
    )
    quarters = call(relay_kernel, array(X, 224, C), [], (exchange(packed, ("yl", "yh")),))
    swap = [(0, 1), (1, 0)]
    mine = exchange(quarters, "x")
    other = lax.ppermute(mine, "core", swap)
    win, wout, e_own, stem, dout, dmixed, left, pick = call(
        own_kernel,
        [
            array(C, F),
            array(C, F),
            array(128, C, dtype=F32),
            array(128, C),
            array(ROWS, C, dtype=F32),
            array(HALF, C),
            array(TAPS, SMALL, SHARD),
            array(C, SHARD),
        ],
        [VMEM((128, C), F32), VMEM((ROWS, 128), F32), VMEM((24, C), F32), VMEM((TAPS, SMALL, SHARD), F32)],
        (mine, embed, cotangent),
        flops=10**8,
    )
    keep, send, win, wout, e_own, h_one, act = call(
        step_kernel,
        [
            array(X * YL, 120, C),
            array(X * YL, 120, C),
            array(C, F),
            array(C, F),
            array(128, C, dtype=F32),
            array(ROWS, C, dtype=F32),
            array(HALF, F),
        ],
        [VMEM((C, F), F32), VMEM((C, F), F32), VMEM((SMALL, C), F32)],
        (other, bases, win, wout, e_own, stem, dout, dmixed),
        alias={2: 2, 3: 3, 4: 4},
        flops=10**9,
    )
    came = lax.ppermute(send, "core", swap)
    output = call(output_kernel, array(1, ROWS, C), [VMEM((ROWS, 128), F32)], (h_one, act, wout), flops=10**8)
    came, output = lax.optimization_barrier((came, output))
    pairs = (keep.astype(F32) + came.astype(F32)).astype(BF)
    pieces = call(middle_kernel, array(Z * YH, 8, C), [], (exchange(pairs, ("x", "yl")),))
    copies = call(last_kernel, array(Z * X, 8, C), [], (exchange(pieces, ("z", "yh")),))
    gathered = exchange(copies, ("z", "x"))
    g_embed, g_conv, g_in, g_out = call(
        grads_kernel,
        [
            array(TAPS, BASES, SHARD, dtype=F32),
            array(TAPS, SHARD, C, dtype=F32),
            array(SHARD, C, dtype=F32),
            array(SHARD, C, dtype=F32),
        ],
        [
            VMEM((TAPS, BASES, SHARD), F32),
            VMEM((SHARD, C), F32),
            VMEM((SHARD, C), F32),
            VMEM((TAPS, SHARD, C), F32),
            VMEM((SMALL, C), F32),
            VMEM((TAPS + 1, SMALL, SHARD), F32),
            pltpu.SemaphoreType.DMA((4,)),
        ],
        (gathered, left, pick, conv_w),
        out_hbm=(0, 1, 2, 3),
    )
    return output, g_embed, g_conv, g_in, g_out.T


def solution(mesh):
    mesh = Mesh(mesh.devices.reshape(Z, X, YH, CORE, YL), ("z", "x", "yh", "core", "yl"))
    seq = ("yh", "core")
    samples = ("z", "x", "yl")
    return jax.shard_map(
        local,
        mesh=mesh,
        in_specs=(
            P(samples, seq),
            P(),
            P(None, seq, None),
            P(seq, "yl"),
            P("yl", seq),
            P(samples, seq, None),
        ),
        out_specs=(
            P(samples, seq, None),
            P(None, None, seq),
            P(None, seq, None),
            P(seq, "yl"),
            P("yl", seq),
        ),
        check_vma=False,
    )
```

```python
import jax
import jax.numpy as jnp
from jax import lax
from jax.experimental import pallas as pl
from jax.experimental.pallas import tpu as pltpu
from jax.sharding import Mesh
from jax.sharding import PartitionSpec as P

Z, X, YH, CORE, YL = 8, 4, 4, 2, 2
TAPS = 5
BASES = 4
C = 384
F = 768
ROWS = 256
HALF = 128
LENGTH = 2048
SHARD = 48
PAIRS = TAPS * BASES
ENDS = [(0, 3), (0, 4), (1, 3), (1, 4), (3, 0), (3, 1), (4, 0), (4, 1)]
END_ROW = BASES * (2 * TAPS - 1)
STEM_ROW = END_ROW + BASES * len(ENDS)
SMALL = 96
BF = jnp.bfloat16
F32 = jnp.float32
VMEM = pltpu.VMEM
LANES = [slice(128 * i, 128 * (i + 1)) for i in range(C // 128)]
GELU_C = 0.7978845608028654
GELU_A = 0.044715


def dot(a, b, dims):
    return lax.dot_general(a, b, (dims, ((), ())), preferred_element_type=F32)


def nn(a, b):
    return dot(a, b, ((1,), (0,)))


def nt(a, b):
    return dot(a, b, ((1,), (1,)))


def tn(a, b):
    return dot(a, b, ((0,), (0,)))


def iota(shape, dim):
    return lax.broadcasted_iota(jnp.int32, shape, dim)


def gelu_both(x):
    x2 = x * x
    t = jnp.tanh(GELU_C * (x + GELU_A * (x * x2)))
    half = 0.5 * (1.0 + t)
    slope = half + 0.5 * x * (1.0 - t * t) * (GELU_C * (1.0 + 3.0 * GELU_A * x2))
    return x * half, slope


def where_am_i():
    x, yh, core, yl = (lax.axis_index(name) for name in ("x", "yh", "core", "yl"))
    return x, yh, core, yl, yh * CORE + core


def stack_embed(embed_ref, scratch, top):
    for j in range(TAPS):
        scratch[top + BASES * j : top + BASES * (j + 1), :] = embed_ref[j].astype(F32)


def picker(seq):
    return (iota((C, SHARD), 0) == iota((C, SHARD), 1) + seq * SHARD).astype(BF)


def pack_kernel(
    ids_hbm, embed_hbm, conv_hbm, win_hbm, wout_hbm, out_ref,
    ids_v, embed_v, conv_v, shard_v, sems, emb, esum, tail, shard_f,
):
    x, yh, core, yl, seq = where_am_i()
    copies = [
        pltpu.make_async_copy(src, dst, sems.at[i])
        for i, (src, dst) in enumerate(
            (
                (embed_hbm, embed_v),
                (conv_hbm, conv_v),
                (win_hbm, shard_v.at[0]),
                (wout_hbm, shard_v.at[1]),
                (ids_hbm, ids_v),
            )
        )
    ]
    for copy in copies:
        copy.start()
    emb[...] = jnp.zeros_like(emb)
    esum[...] = jnp.zeros_like(esum)
    tail[...] = jnp.zeros_like(tail)
    copies[0].wait()
    stack_embed(embed_v, emb, 0)
    mine = nn(emb[...].astype(BF), picker(seq)).astype(BF)
    copies[1].wait()
    for k in range(TAPS):
        esum[PAIRS * k : PAIRS * (k + 1), :] = nn(mine, conv_v[k])[:PAIRS]
    for q in range(X * YL):
        tail[16 * q : 16 * q + 13, :] = esum[13 * q : 13 * q + 13, :]
    part = tail[pl.ds(pl.multiple_of((YL * x + yl) * 16, 16), 16), :]
    for copy in copies[2:]:
        copy.wait()
    ids = jnp.concatenate([ids_v[...].astype(F32), jnp.zeros((1, C - ROWS), F32)], axis=1)
    part = jnp.where(iota((16, C), 0) == 15, ids, part)
    shard_f[0:48, :] = shard_v[0].astype(F32)
    shard_f[48:96, :] = shard_v[1].astype(F32)
    piece = shard_f[pl.ds(pl.multiple_of(24 * x, 8), 24), :]
    piece = jnp.concatenate([piece, part], axis=0).astype(BF)
    for d in range(YH * YL):
        out_ref[d] = piece


def relay_kernel(in_ref, out_ref):
    yl = where_am_i()[3]
    got = [in_ref[p].astype(F32) for p in range(YH * YL)]
    sums = [sum(got[YL * h + half][24:40] for h in range(YH)) for half in range(YL)]
    row = iota((16, C), 0)
    for h in range(YH):
        ids = in_ref[YL * h + yl].astype(F32)[39:40]
        sums[h // 2] = jnp.where(row == 13 + h % 2, ids, sums[h // 2])
    piece = jnp.concatenate([g[:24] for g in got] + sums, axis=0).astype(BF)
    for x in range(X):
        out_ref[x] = piece


def fill_weights(core, got, win, wout):
    for h in range(YH):
        top = pl.multiple_of((CORE * h + core) * SHARD, SHARD)
        for half in range(YL):
            cols = slice(C * half, C * (half + 1))
            p = 24 * (YL * h + half)
            for ref, first in ((win, 0), (wout, 2)):
                ref[pl.ds(top, SHARD), cols] = jnp.concatenate(
                    [got[first, p : p + 24, :], got[first + 1, p : p + 24, :]], axis=0
                )


def add_e(got, ebuf):
    for x in range(X):
        for half in range(YL):
            p = 192 + 16 * half
            q = 13 * (YL * x + half)
            ebuf[q : q + 13, :] = ebuf[q : q + 13, :] + got[x, p : p + 16, :].astype(F32)[:13]


def own_kernel(
    own, embed_ref, cot_ref, win, wout, ebuf, stem, dout, dmixed, left, pick_ref, embf, rows_f, emb, leftf
):
    x_mine, yh, core, yl, seq = where_am_i()
    pick = picker(seq)
    pick_ref[...] = pick
    emb[...] = jnp.zeros_like(emb)
    stack_embed(embed_ref, emb, 0)
    mine = nn(emb[...].astype(BF), pick)
    leftf[...] = jnp.zeros_like(leftf)
    for k in range(TAPS):
        leftf[k, BASES * k : BASES * k + PAIRS, :] = mine[:PAIRS]
    for q, (k, j) in enumerate(ENDS):
        leftf[k, END_ROW + BASES * q : END_ROW + BASES * (q + 1), :] = -mine[BASES * j : BASES * (j + 1)]
    left[...] = leftf[...].astype(BF)
    fill_weights(core, own, win, wout)
    ebuf[...] = jnp.zeros_like(ebuf)
    add_e(own, ebuf)
    embf[...] = jnp.zeros_like(embf)
    stack_embed(embed_ref, embf, TAPS * PAIRS)
    stem[...] = embf[...].astype(BF)
    for lane in LANES:
        rows_f[...] = cot_ref[0, :, lane].astype(F32)
        even = rows_f[pl.ds(0, HALF, stride=2), :]
        odd = rows_f[pl.ds(1, HALF, stride=2), :]
        dout[:HALF, lane] = even
        dout[HALF:, lane] = odd
        dmixed[:, lane] = (even + odd).astype(BF)


def step_kernel(
    oth, ids_ref, win_in, wout_in, ebuf_in, stem, dout, dmixed_ref,
    keep_ref, send_ref, win, wout, ebuf, h_out, act_out,
    grad_a, grad_b, small,
):
    x_mine, yh, core, yl, seq = where_am_i()
    fill_weights(1 - core, oth, win, wout)
    add_e(oth, ebuf)
    e_full = ebuf[...]
    e_hi = e_full.astype(BF)
    e_lo = (e_full - e_hi.astype(F32)).astype(BF)
    before = jnp.maximum(yh - (1 - core), 0)
    after = jnp.minimum(yh + core, YH - 1)
    near = oth[x_mine, 192:224, :].astype(F32)[:, :ROWS]
    row = iota((32, ROWS), 0)

    def ids_of(h):
        at = 16 * jnp.right_shift(h, 1) + 13 + jnp.bitwise_and(h, 1)
        line = jnp.sum(jnp.where(row == at, near, 0.0), axis=0, keepdims=True)
        return jnp.broadcast_to(line, (8, ROWS))

    id_prev = jnp.where(seq == 0, -1.0, ids_of(before)[:, 128:])
    id_next = jnp.where(seq == YH * CORE - 1, -1.0, ids_of(after)[:, :128])
    id_mid = jnp.broadcast_to(ids_ref[...].astype(F32), (8, ROWS))
    line = jnp.concatenate([id_prev, id_mid, id_next], axis=1)
    near_ids = [pltpu.roll(line, (4 - o) % 512, 1)[:, 128 : 128 + ROWS] for o in range(2 * TAPS - 1)]

    def matches(offset, base):
        rows = offset.shape[0]
        seen = jnp.full((rows, ROWS), -2.0, F32)
        for o in range(2 * TAPS - 1):
            seen = jnp.where(offset == o, jnp.concatenate([near_ids[o]] * (rows // 8), axis=0), seen)
        return seen == base.astype(F32)

    def outside(k):
        at = seq * ROWS + iota(k.shape, 1) + k - 2
        return (at < 0) | (at >= LENGTH)

    m = iota((HALF, ROWS), 0)
    k = sum((m >= PAIRS * q).astype(jnp.int32) for q in range(1, TAPS + 1))
    rest = m - PAIRS * k
    k = jnp.where(m >= PAIRS * TAPS, 2, k)
    hit = matches(k + jnp.right_shift(rest, 2), jnp.bitwise_and(rest, 3))
    hit = hit & jnp.logical_not(outside(k)) & (m < PAIRS * (TAPS + 1))
    onehot = jnp.where(hit, 1.0, 0.0).astype(BF)
    m = iota((SMALL, ROWS), 0)
    group = jnp.right_shift(m, 2)
    k = jnp.full((SMALL, ROWS), 2, jnp.int32)
    offset = jnp.where(m < END_ROW, group, group - STEM_ROW // BASES + 2)
    for q, (tap, j) in enumerate(ENDS):
        here = group == END_ROW // BASES + q
        k = jnp.where(here, tap, k)
        offset = jnp.where(here, tap + j, offset)
    ends = (m >= END_ROW) & (m < STEM_ROW)
    hit = matches(offset, jnp.bitwise_and(m, 3)) & (m < STEM_ROW + PAIRS)
    hit = hit & (jnp.logical_not(ends) | outside(k))
    small_hot = jnp.where(hit, 1.0, 0.0).astype(BF)
    src = iota((ROWS, ROWS), 0)
    dst = iota((ROWS, ROWS), 1)
    order = jnp.where(dst < HALF, 2 * dst, 2 * dst - (ROWS - 1))
    order = (src == order).astype(BF)
    onehot_t = nn(onehot, order).T.astype(BF)
    small_hot = nn(small_hot, order).astype(BF)
    z = nn(onehot_t, e_hi) + nn(onehot_t, e_lo)
    h_zero = nn(onehot_t, stem[...]).astype(BF).astype(F32)
    g_z, s_z = gelu_both(z)
    h_one = (h_zero + g_z).astype(BF).astype(F32)
    even, odd = h_one[:HALF], h_one[HALF:]
    pooled = ((even + odd) * 0.5).astype(BF).astype(F32)
    scale = lax.rsqrt(jnp.mean(pooled * pooled, axis=-1, keepdims=True) + 1e-06)
    normed = (pooled * scale).astype(BF)
    w_in = win[...]
    w_out = wout[...]
    pre = nn(normed, w_in)
    g_p, s_p = gelu_both(pre)
    act = g_p.astype(BF)
    h_out[...] = h_one
    act_out[...] = act
    dmixed = dmixed_ref[...]
    d_even, d_odd = dout[:HALF, :], dout[HALF:, :]
    dact = nn(dmixed, w_out)
    dpre = (dact * s_p).astype(BF)
    dnormed = nt(dpre, w_in)
    dpooled = scale * dnormed - pooled * (scale * scale * scale) * jnp.mean(
        dnormed * pooled, axis=-1, keepdims=True
    )
    add = dpooled * 0.5
    dh_one = jnp.concatenate([d_even + add, d_odd + add], axis=0)
    dz = (dh_one * s_z).astype(BF)
    d_hi = dh_one.astype(BF)
    d_lo = (dh_one - d_hi.astype(F32)).astype(BF)
    small[...] = jnp.where(
        iota((SMALL, C), 0) < STEM_ROW, nn(small_hot, dz), nn(small_hot, d_hi) + nn(small_hot, d_lo)
    )
    grad_a[...] = tn(normed, dpre)
    grad_b[...] = tn(dmixed, act)
    for which, ref in ((core, keep_ref), (1 - core, send_ref)):
        for x in range(X):
            grad = grad_a if x < 2 else grad_b
            for half in range(YL):
                cols = slice(C * half, C * (half + 1))
                parts = []
                for h in range(YH):
                    top = pl.multiple_of((2 * h + which) * SHARD + 24 * (x % 2), 8)
                    parts.append(grad[pl.ds(top, 24), cols])
                parts.append(small[24 * x : 24 * x + 24, :])
                ref[YL * x + half] = jnp.concatenate(parts, axis=0).astype(BF)


def output_kernel(h_one, act, wout, out_ref, rows_f):
    mixed = nt(act[...], wout[...]).astype(BF).astype(F32)
    for lane in LANES:
        rows_f[pl.ds(0, HALF, stride=2), :] = h_one[:HALF, lane] + mixed[:, lane]
        rows_f[pl.ds(1, HALF, stride=2), :] = h_one[HALF:, lane] + mixed[:, lane]
        out_ref[0, :, lane] = rows_f[...].astype(BF)


def middle_kernel(in_ref, out_ref):
    total = in_ref[0].astype(F32)
    for i in range(1, X * YL):
        total = total + in_ref[i].astype(F32)
    for z in range(Z):
        for h in range(YH):
            if z < 3:
                piece = total[24 * h + 8 * z : 24 * h + 8 * z + 8]
            elif z < 6:
                piece = total[96 + 8 * (z - 3) : 96 + 8 * (z - 3) + 8]
            else:
                piece = jnp.zeros((8, C), F32)
            out_ref[YH * z + h] = piece.astype(BF)


def last_kernel(in_ref, out_ref):
    total = in_ref[0].astype(F32)
    for i in range(1, Z * YH):
        total = total + in_ref[i].astype(F32)
    total = total.astype(BF)
    for i in range(Z * X):
        out_ref[i] = total


def grads_kernel(
    in_ref, left, pick, conv_ref, gemb_hbm, gconv_hbm, gin_hbm, gout_hbm,
    gemb_v, gin_v, gout_v, gconv_v, sums, back, sems,
):
    for x in range(X):
        for z in range(3, 6):
            top = 24 * x + 8 * (z - 3)
            sums[top : top + 8, :] = in_ref[X * z + x].astype(F32)
    small = sums[...].astype(BF)
    for k in range(TAPS):
        gconv_v[k] = tn(left[k], small)
    copies = [
        pltpu.make_async_copy(src, dst, sems.at[i])
        for i, (src, dst) in enumerate(
            ((gconv_v, gconv_hbm), (gin_v, gin_hbm), (gout_v, gout_hbm), (gemb_v, gemb_hbm))
        )
    ]
    copies[0].start()
    for k in range(TAPS):
        back[k] = nt(small, conv_ref[k])
    back[TAPS] = nn(small, pick[...])
    back[TAPS, 0:PAIRS, :] = back[TAPS, STEM_ROW : STEM_ROW + PAIRS, :] + sum(
        back[k, BASES * k : BASES * k + PAIRS, :] for k in range(TAPS)
    )
    for j in range(TAPS):
        rows = back[TAPS, BASES * j : BASES * (j + 1), :]
        for q, (k, tap) in enumerate(ENDS):
            if tap == j:
                rows = rows - back[k, END_ROW + BASES * q : END_ROW + BASES * (q + 1), :]
        gemb_v[j] = rows
    copies[3].start()
    for x in range(X):
        for z in range(3):
            top = 24 * (x % 2) + 8 * z
            (gin_v if x < 2 else gout_v)[top : top + 8, :] = in_ref[X * z + x].astype(F32)
    copies[1].start()
    copies[2].start()
    for copy in copies:
        copy.wait()


def call(body, outs, scratch, args, hbm=False, out_hbm=(), alias={}, flops=0):
    spec = pl.BlockSpec(memory_space=VMEM)
    far = pl.BlockSpec(memory_space=pltpu.HBM)
    if hbm:
        args = tuple(pltpu.with_memory_space_constraint(a, pltpu.HBM) for a in args)
    many = isinstance(outs, list)
    moved = sum(a.size * a.dtype.itemsize for a in args)
    return pl.pallas_call(
        body,
        out_shape=outs,
        in_specs=[far if hbm else spec] * len(args),
        out_specs=[far if i in out_hbm else spec for i in range(len(outs))] if many else spec,
        scratch_shapes=scratch,
        input_output_aliases=alias,
        compiler_params=pltpu.CompilerParams(vmem_limit_bytes=48 * 1024 * 1024),
        cost_estimate=pl.CostEstimate(flops=flops, bytes_accessed=moved, transcendentals=0),
        name=body.__name__,
    )(*args)


def array(*shape, dtype=BF):
    return jax.ShapeDtypeStruct(shape, dtype)


def exchange(pieces, axes):
    return lax.all_to_all(pieces, axes, 0, 0, tiled=True)


def local(bases, embed, conv_w, w_in, w_out, cotangent):
    packed = call(
        pack_kernel,
        array(YH * YL, 40, C),
        [
            VMEM((1, ROWS), jnp.int32),
            VMEM((TAPS, BASES, C), BF),
            VMEM((TAPS, SHARD, C), BF),
            VMEM((2, SHARD, C), BF),
            pltpu.SemaphoreType.DMA((5,)),
            VMEM((24, C), F32),
            VMEM((104, C), F32),
            VMEM((128, C), F32),
            VMEM((96, C), F32),
        ],
        (bases, embed, conv_w, w_in, w_out.T),
        hbm=True,
    )
    quarters = call(relay_kernel, array(X, 224, C), [], (exchange(packed, ("yh", "yl")),))
    swap = [(0, 1), (1, 0)]
    mine = exchange(quarters, "x")
    other = lax.ppermute(mine, "core", swap)
    win, wout, e_own, stem, dout, dmixed, left, pick = call(
        own_kernel,
        [
            array(C, F),
            array(C, F),
            array(128, C, dtype=F32),
            array(128, C),
            array(ROWS, C, dtype=F32),
            array(HALF, C),
            array(TAPS, SMALL, SHARD),
            array(C, SHARD),
        ],
        [VMEM((128, C), F32), VMEM((ROWS, 128), F32), VMEM((24, C), F32), VMEM((TAPS, SMALL, SHARD), F32)],
        (mine, embed, cotangent),
        flops=10**8,
    )
    keep, send, win, wout, e_own, h_one, act = call(
        step_kernel,
        [
            array(X * YL, 120, C),
            array(X * YL, 120, C),
            array(C, F),
            array(C, F),
            array(128, C, dtype=F32),
            array(ROWS, C, dtype=F32),
            array(HALF, F),
        ],
        [VMEM((C, F), F32), VMEM((C, F), F32), VMEM((SMALL, C), F32)],
        (other, bases, win, wout, e_own, stem, dout, dmixed),
        alias={2: 2, 3: 3, 4: 4},
        flops=10**9,
    )
    came = lax.ppermute(send, "core", swap)
    output = call(output_kernel, array(1, ROWS, C), [VMEM((ROWS, 128), F32)], (h_one, act, wout), flops=10**8)
    came, output = lax.optimization_barrier((came, output))
    pairs = (keep.astype(F32) + came.astype(F32)).astype(BF)
    pieces = call(middle_kernel, array(Z * YH, 8, C), [], (exchange(pairs, ("x", "yl")),))
    copies = call(last_kernel, array(Z * X, 8, C), [], (exchange(pieces, ("z", "yh")),))
    gathered = exchange(copies, ("z", "x"))
    g_embed, g_conv, g_in, g_out = call(
        grads_kernel,
        [
            array(TAPS, BASES, SHARD, dtype=F32),
            array(TAPS, SHARD, C, dtype=F32),
            array(SHARD, C, dtype=F32),
            array(SHARD, C, dtype=F32),
        ],
        [
            VMEM((TAPS, BASES, SHARD), F32),
            VMEM((SHARD, C), F32),
            VMEM((SHARD, C), F32),
            VMEM((TAPS, SHARD, C), F32),
            VMEM((SMALL, C), F32),
            VMEM((TAPS + 1, SMALL, SHARD), F32),
            pltpu.SemaphoreType.DMA((4,)),
        ],
        (gathered, left, pick, conv_w),
        out_hbm=(0, 1, 2, 3),
    )
    return output, g_embed, g_conv, g_in, g_out.T


def solution(mesh):
    mesh = Mesh(mesh.devices.reshape(Z, X, YH, CORE, YL), ("z", "x", "yh", "core", "yl"))
    seq = ("yh", "core")
    samples = ("z", "x", "yl")
    return jax.shard_map(
        local,
        mesh=mesh,
        in_specs=(
            P(samples, seq),
            P(),
            P(None, seq, None),
            P(seq, "yl"),
            P("yl", seq),
            P(samples, seq, None),
        ),
        out_specs=(
            P(samples, seq, None),
            P(None, None, seq),
            P(None, seq, None),
            P(seq, "yl"),
            P("yl", seq),
        ),
        check_vma=False,
    )
```

```python
import jax
import jax.numpy as jnp
from jax import lax
from jax.experimental import pallas as pl
from jax.experimental.pallas import tpu as pltpu
from jax.sharding import Mesh
from jax.sharding import PartitionSpec as P

Z, X, YH, CORE, YL = 8, 4, 4, 2, 2
TAPS = 5
BASES = 4
C = 384
F = 768
ROWS = 256
HALF = 128
LENGTH = 2048
SHARD = 48
PAIRS = TAPS * BASES
ENDS = [(0, 3), (0, 4), (1, 3), (1, 4), (3, 0), (3, 1), (4, 0), (4, 1)]
END_ROW = BASES * (2 * TAPS - 1)
STEM_ROW = END_ROW + BASES * len(ENDS)
SMALL = 96
BF = jnp.bfloat16
F32 = jnp.float32
VMEM = pltpu.VMEM
LANES = [slice(128 * i, 128 * (i + 1)) for i in range(C // 128)]
GELU_C = 0.7978845608028654
GELU_A = 0.044715


def dot(a, b, dims):
    return lax.dot_general(a, b, (dims, ((), ())), preferred_element_type=F32)


def nn(a, b):
    return dot(a, b, ((1,), (0,)))


def nt(a, b):
    return dot(a, b, ((1,), (1,)))


def tn(a, b):
    return dot(a, b, ((0,), (0,)))


def iota(shape, dim):
    return lax.broadcasted_iota(jnp.int32, shape, dim)


def gelu_both(x):
    x2 = x * x
    t = jnp.tanh(GELU_C * (x + GELU_A * (x * x2)))
    half = 0.5 * (1.0 + t)
    slope = half + 0.5 * x * (1.0 - t * t) * (GELU_C * (1.0 + 3.0 * GELU_A * x2))
    return x * half, slope


def where_am_i():
    x, yh, core, yl = (lax.axis_index(name) for name in ("x", "yh", "core", "yl"))
    return x, yh, core, yl, yh * CORE + core


def stack_embed(embed_ref, scratch, top):
    for j in range(TAPS):
        scratch[top + BASES * j : top + BASES * (j + 1), :] = embed_ref[j].astype(F32)


def picker(seq):
    return (iota((C, SHARD), 0) == iota((C, SHARD), 1) + seq * SHARD).astype(BF)


def pack_kernel(
    ids_hbm, embed_hbm, conv_hbm, win_hbm, wout_hbm, out_ref,
    ids_v, embed_v, conv_v, shard_v, sems, emb, esum, tail, shard_f,
):
    x, yh, core, yl, seq = where_am_i()
    copies = [
        pltpu.make_async_copy(src, dst, sems.at[i])
        for i, (src, dst) in enumerate(
            (
                (embed_hbm, embed_v),
                (conv_hbm, conv_v),
                (win_hbm, shard_v.at[0]),
                (wout_hbm, shard_v.at[1]),
                (ids_hbm, ids_v),
            )
        )
    ]
    for copy in copies:
        copy.start()
    emb[...] = jnp.zeros_like(emb)
    esum[...] = jnp.zeros_like(esum)
    tail[...] = jnp.zeros_like(tail)
    copies[0].wait()
    stack_embed(embed_v, emb, 0)
    mine = nn(emb[...].astype(BF), picker(seq)).astype(BF)
    copies[1].wait()
    for k in range(TAPS):
        esum[PAIRS * k : PAIRS * (k + 1), :] = nn(mine, conv_v[k])[:PAIRS]
    for q in range(X * YL):
        tail[16 * q : 16 * q + 13, :] = esum[13 * q : 13 * q + 13, :]
    part = tail[pl.ds(pl.multiple_of((YL * x + yl) * 16, 16), 16), :]
    for copy in copies[2:]:
        copy.wait()
    ids = jnp.concatenate([ids_v[...].astype(F32), jnp.zeros((1, C - ROWS), F32)], axis=1)
    part = jnp.where(iota((16, C), 0) == 15, ids, part)
    shard_f[0:48, :] = shard_v[0].astype(F32)
    shard_f[48:96, :] = shard_v[1].astype(F32)
    piece = shard_f[pl.ds(pl.multiple_of(24 * x, 8), 24), :]
    piece = jnp.concatenate([piece, part], axis=0).astype(BF)
    for d in range(YH * YL):
        out_ref[d] = piece


def relay_kernel(in_ref, out_ref):
    yl = where_am_i()[3]
    got = [in_ref[p].astype(F32) for p in range(YH * YL)]
    sums = [sum(got[YL * h + half][24:40] for h in range(YH)) for half in range(YL)]
    row = iota((16, C), 0)
    for h in range(YH):
        ids = in_ref[YL * h + yl].astype(F32)[39:40]
        sums[h // 2] = jnp.where(row == 13 + h % 2, ids, sums[h // 2])
    piece = jnp.concatenate([g[:24] for g in got] + sums, axis=0).astype(BF)
    for x in range(X):
        out_ref[x] = piece


def fill_weights(core, got, win, wout):
    for h in range(YH):
        top = pl.multiple_of((CORE * h + core) * SHARD, SHARD)
        for half in range(YL):
            cols = slice(C * half, C * (half + 1))
            p = 24 * (YL * h + half)
            for ref, first in ((win, 0), (wout, 2)):
                ref[pl.ds(top, SHARD), cols] = jnp.concatenate(
                    [got[first, p : p + 24, :], got[first + 1, p : p + 24, :]], axis=0
                )


def add_e(got, ebuf):
    for x in range(X):
        for half in range(YL):
            p = 192 + 16 * half
            q = 13 * (YL * x + half)
            ebuf[q : q + 13, :] = ebuf[q : q + 13, :] + got[x, p : p + 16, :].astype(F32)[:13]


def own_kernel(
    own, embed_ref, cot_ref, win, wout, ebuf, stem, dout, dmixed, left, pick_ref, embf, rows_f, emb, leftf
):
    x_mine, yh, core, yl, seq = where_am_i()
    pick = picker(seq)
    pick_ref[...] = pick
    emb[...] = jnp.zeros_like(emb)
    stack_embed(embed_ref, emb, 0)
    mine = nn(emb[...].astype(BF), pick)
    leftf[...] = jnp.zeros_like(leftf)
    for k in range(TAPS):
        leftf[k, BASES * k : BASES * k + PAIRS, :] = mine[:PAIRS]
    for q, (k, j) in enumerate(ENDS):
        leftf[k, END_ROW + BASES * q : END_ROW + BASES * (q + 1), :] = -mine[BASES * j : BASES * (j + 1)]
    left[...] = leftf[...].astype(BF)
    fill_weights(core, own, win, wout)
    ebuf[...] = jnp.zeros_like(ebuf)
    add_e(own, ebuf)
    embf[...] = jnp.zeros_like(embf)
    stack_embed(embed_ref, embf, TAPS * PAIRS)
    stem[...] = embf[...].astype(BF)
    for lane in LANES:
        rows_f[...] = cot_ref[0, :, lane].astype(F32)
        even = rows_f[pl.ds(0, HALF, stride=2), :]
        odd = rows_f[pl.ds(1, HALF, stride=2), :]
        dout[:HALF, lane] = even
        dout[HALF:, lane] = odd
        dmixed[:, lane] = (even + odd).astype(BF)


def step_kernel(
    oth, ids_ref, win_in, wout_in, ebuf_in, stem, dout, dmixed_ref,
    keep_ref, send_ref, win, wout, ebuf, h_out, act_out,
    grad_a, grad_b, small,
):
    x_mine, yh, core, yl, seq = where_am_i()
    fill_weights(1 - core, oth, win, wout)
    add_e(oth, ebuf)
    e_full = ebuf[...]
    e_hi = e_full.astype(BF)
    e_lo = (e_full - e_hi.astype(F32)).astype(BF)
    before = jnp.maximum(yh - (1 - core), 0)
    after = jnp.minimum(yh + core, YH - 1)
    near = oth[x_mine, 192:224, :].astype(F32)[:, :ROWS]
    row = iota((32, ROWS), 0)

    def ids_of(h):
        at = 16 * jnp.right_shift(h, 1) + 13 + jnp.bitwise_and(h, 1)
        line = jnp.sum(jnp.where(row == at, near, 0.0), axis=0, keepdims=True)
        return jnp.broadcast_to(line, (8, ROWS))

    id_prev = jnp.where(seq == 0, -1.0, ids_of(before)[:, 128:])
    id_next = jnp.where(seq == YH * CORE - 1, -1.0, ids_of(after)[:, :128])
    id_mid = jnp.broadcast_to(ids_ref[...].astype(F32), (8, ROWS))
    line = jnp.concatenate([id_prev, id_mid, id_next], axis=1)
    near_ids = [pltpu.roll(line, (4 - o) % 512, 1)[:, 128 : 128 + ROWS] for o in range(2 * TAPS - 1)]

    def matches(offset, base):
        rows = offset.shape[0]
        seen = jnp.full((rows, ROWS), -2.0, F32)
        for o in range(2 * TAPS - 1):
            seen = jnp.where(offset == o, jnp.concatenate([near_ids[o]] * (rows // 8), axis=0), seen)
        return seen == base.astype(F32)

    def outside(k):
        at = seq * ROWS + iota(k.shape, 1) + k - 2
        return (at < 0) | (at >= LENGTH)

    m = iota((HALF, ROWS), 0)
    k = sum((m >= PAIRS * q).astype(jnp.int32) for q in range(1, TAPS + 1))
    rest = m - PAIRS * k
    k = jnp.where(m >= PAIRS * TAPS, 2, k)
    hit = matches(k + jnp.right_shift(rest, 2), jnp.bitwise_and(rest, 3))
    hit = hit & jnp.logical_not(outside(k)) & (m < PAIRS * (TAPS + 1))
    onehot = jnp.where(hit, 1.0, 0.0).astype(BF)
    m = iota((SMALL, ROWS), 0)
    group = jnp.right_shift(m, 2)
    k = jnp.full((SMALL, ROWS), 2, jnp.int32)
    offset = jnp.where(m < END_ROW, group, group - STEM_ROW // BASES + 2)
    for q, (tap, j) in enumerate(ENDS):
        here = group == END_ROW // BASES + q
        k = jnp.where(here, tap, k)
        offset = jnp.where(here, tap + j, offset)
    ends = (m >= END_ROW) & (m < STEM_ROW)
    hit = matches(offset, jnp.bitwise_and(m, 3)) & (m < STEM_ROW + PAIRS)
    hit = hit & (jnp.logical_not(ends) | outside(k))
    small_hot = jnp.where(hit, 1.0, 0.0).astype(BF)
    src = iota((ROWS, ROWS), 0)
    dst = iota((ROWS, ROWS), 1)
    order = jnp.where(dst < HALF, 2 * dst, 2 * dst - (ROWS - 1))
    order = (src == order).astype(BF)
    onehot_t = nn(onehot, order).T.astype(BF)
    small_hot = nn(small_hot, order).astype(BF)
    z = nn(onehot_t, e_hi) + nn(onehot_t, e_lo)
    h_zero = nn(onehot_t, stem[...]).astype(BF).astype(F32)
    g_z, s_z = gelu_both(z)
    h_one = (h_zero + g_z).astype(BF).astype(F32)
    even, odd = h_one[:HALF], h_one[HALF:]
    pooled = ((even + odd) * 0.5).astype(BF).astype(F32)
    scale = lax.rsqrt(jnp.mean(pooled * pooled, axis=-1, keepdims=True) + 1e-06)
    normed = (pooled * scale).astype(BF)
    w_in = win[...]
    w_out = wout[...]
    pre = nn(normed, w_in)
    g_p, s_p = gelu_both(pre)
    act = g_p.astype(BF)
    h_out[...] = h_one
    act_out[...] = act
    dmixed = dmixed_ref[...]
    d_even, d_odd = dout[:HALF, :], dout[HALF:, :]
    dact = nn(dmixed, w_out)
    dpre = (dact * s_p).astype(BF)
    dnormed = nt(dpre, w_in)
    dpooled = scale * dnormed - pooled * (scale * scale * scale) * jnp.mean(
        dnormed * pooled, axis=-1, keepdims=True
    )
    add = dpooled * 0.5
    dh_one = jnp.concatenate([d_even + add, d_odd + add], axis=0)
    dz = (dh_one * s_z).astype(BF)
    d_hi = dh_one.astype(BF)
    d_lo = (dh_one - d_hi.astype(F32)).astype(BF)
    small[...] = jnp.where(
        iota((SMALL, C), 0) < STEM_ROW, nn(small_hot, dz), nn(small_hot, d_hi) + nn(small_hot, d_lo)
    )
    grad_a[...] = tn(normed, dpre)
    grad_b[...] = tn(dmixed, act)
    for which, ref in ((core, keep_ref), (1 - core, send_ref)):
        for x in range(X):
            grad = grad_a if x < 2 else grad_b
            for half in range(YL):
                cols = slice(C * half, C * (half + 1))
                parts = []
                for h in range(YH):
                    top = pl.multiple_of((2 * h + which) * SHARD + 24 * (x % 2), 8)
                    parts.append(grad[pl.ds(top, 24), cols])
                parts.append(small[24 * x : 24 * x + 24, :])
                ref[YL * x + half] = jnp.concatenate(parts, axis=0).astype(BF)


def output_kernel(h_one, act, wout, out_ref, rows_f):
    mixed = nt(act[...], wout[...]).astype(BF).astype(F32)
    for lane in LANES:
        rows_f[pl.ds(0, HALF, stride=2), :] = h_one[:HALF, lane] + mixed[:, lane]
        rows_f[pl.ds(1, HALF, stride=2), :] = h_one[HALF:, lane] + mixed[:, lane]
        out_ref[0, :, lane] = rows_f[...].astype(BF)


def middle_kernel(in_ref, out_ref):
    total = in_ref[0].astype(F32)
    for i in range(1, X * YL):
        total = total + in_ref[i].astype(F32)
    for z in range(Z):
        for h in range(YH):
            if z < 3:
                piece = total[24 * h + 8 * z : 24 * h + 8 * z + 8]
            elif z < 6:
                piece = total[96 + 8 * (z - 3) : 96 + 8 * (z - 3) + 8]
            else:
                piece = jnp.zeros((8, C), F32)
            out_ref[YH * z + h] = piece.astype(BF)


def last_kernel(in_ref, out_ref):
    total = in_ref[0].astype(F32)
    for i in range(1, Z * YH):
        total = total + in_ref[i].astype(F32)
    total = total.astype(BF)
    for i in range(Z * X):
        out_ref[i] = total


def grads_kernel(
    in_ref, left, pick, conv_ref, gemb_hbm, gconv_hbm, gin_hbm, gout_hbm,
    gemb_v, gin_v, gout_v, gconv_v, sums, back, sems,
):
    for x in range(X):
        for z in range(3, 6):
            top = 24 * x + 8 * (z - 3)
            sums[top : top + 8, :] = in_ref[Z * x + z].astype(F32)
    small = sums[...].astype(BF)
    for k in range(TAPS):
        gconv_v[k] = tn(left[k], small)
    copies = [
        pltpu.make_async_copy(src, dst, sems.at[i])
        for i, (src, dst) in enumerate(
            ((gconv_v, gconv_hbm), (gin_v, gin_hbm), (gout_v, gout_hbm), (gemb_v, gemb_hbm))
        )
    ]
    copies[0].start()
    for k in range(TAPS):
        back[k] = nt(small, conv_ref[k])
    back[TAPS] = nn(small, pick[...])
    back[TAPS, 0:PAIRS, :] = back[TAPS, STEM_ROW : STEM_ROW + PAIRS, :] + sum(
        back[k, BASES * k : BASES * k + PAIRS, :] for k in range(TAPS)
    )
    for j in range(TAPS):
        rows = back[TAPS, BASES * j : BASES * (j + 1), :]
        for q, (k, tap) in enumerate(ENDS):
            if tap == j:
                rows = rows - back[k, END_ROW + BASES * q : END_ROW + BASES * (q + 1), :]
        gemb_v[j] = rows
    copies[3].start()
    for x in range(X):
        for z in range(3):
            top = 24 * (x % 2) + 8 * z
            (gin_v if x < 2 else gout_v)[top : top + 8, :] = in_ref[Z * x + z].astype(F32)
    copies[1].start()
    copies[2].start()
    for copy in copies:
        copy.wait()


def call(body, outs, scratch, args, hbm=False, out_hbm=(), alias={}, flops=0):
    spec = pl.BlockSpec(memory_space=VMEM)
    far = pl.BlockSpec(memory_space=pltpu.HBM)
    if hbm:
        args = tuple(pltpu.with_memory_space_constraint(a, pltpu.HBM) for a in args)
    many = isinstance(outs, list)
    moved = sum(a.size * a.dtype.itemsize for a in args)
    return pl.pallas_call(
        body,
        out_shape=outs,
        in_specs=[far if hbm else spec] * len(args),
        out_specs=[far if i in out_hbm else spec for i in range(len(outs))] if many else spec,
        scratch_shapes=scratch,
        input_output_aliases=alias,
        compiler_params=pltpu.CompilerParams(vmem_limit_bytes=48 * 1024 * 1024),
        cost_estimate=pl.CostEstimate(flops=flops, bytes_accessed=moved, transcendentals=0),
        name=body.__name__,
    )(*args)


def array(*shape, dtype=BF):
    return jax.ShapeDtypeStruct(shape, dtype)


def exchange(pieces, axes):
    return lax.all_to_all(pieces, axes, 0, 0, tiled=True)


def local(bases, embed, conv_w, w_in, w_out, cotangent):
    packed = call(
        pack_kernel,
        array(YH * YL, 40, C),
        [
            VMEM((1, ROWS), jnp.int32),
            VMEM((TAPS, BASES, C), BF),
            VMEM((TAPS, SHARD, C), BF),
            VMEM((2, SHARD, C), BF),
            pltpu.SemaphoreType.DMA((5,)),
            VMEM((24, C), F32),
            VMEM((104, C), F32),
            VMEM((128, C), F32),
            VMEM((96, C), F32),
        ],
        (bases, embed, conv_w, w_in, w_out.T),
        hbm=True,
    )
    quarters = call(relay_kernel, array(X, 224, C), [], (exchange(packed, ("yh", "yl")),))
    swap = [(0, 1), (1, 0)]
    mine = exchange(quarters, "x")
    other = lax.ppermute(mine, "core", swap)
    win, wout, e_own, stem, dout, dmixed, left, pick = call(
        own_kernel,
        [
            array(C, F),
            array(C, F),
            array(128, C, dtype=F32),
            array(128, C),
            array(ROWS, C, dtype=F32),
            array(HALF, C),
            array(TAPS, SMALL, SHARD),
            array(C, SHARD),
        ],
        [VMEM((128, C), F32), VMEM((ROWS, 128), F32), VMEM((24, C), F32), VMEM((TAPS, SMALL, SHARD), F32)],
        (mine, embed, cotangent),
        flops=10**8,
    )
    keep, send, win, wout, e_own, h_one, act = call(
        step_kernel,
        [
            array(X * YL, 120, C),
            array(X * YL, 120, C),
            array(C, F),
            array(C, F),
            array(128, C, dtype=F32),
            array(ROWS, C, dtype=F32),
            array(HALF, F),
        ],
        [VMEM((C, F), F32), VMEM((C, F), F32), VMEM((SMALL, C), F32)],
        (other, bases, win, wout, e_own, stem, dout, dmixed),
        alias={2: 2, 3: 3, 4: 4},
        flops=10**9,
    )
    came = lax.ppermute(send, "core", swap)
    output = call(output_kernel, array(1, ROWS, C), [VMEM((ROWS, 128), F32)], (h_one, act, wout), flops=10**8)
    came, output = lax.optimization_barrier((came, output))
    pairs = (keep.astype(F32) + came.astype(F32)).astype(BF)
    pieces = call(middle_kernel, array(Z * YH, 8, C), [], (exchange(pairs, ("x", "yl")),))
    copies = call(last_kernel, array(Z * X, 8, C), [], (exchange(pieces, ("z", "yh")),))
    gathered = exchange(copies, ("x", "z"))
    g_embed, g_conv, g_in, g_out = call(
        grads_kernel,
        [
            array(TAPS, BASES, SHARD, dtype=F32),
            array(TAPS, SHARD, C, dtype=F32),
            array(SHARD, C, dtype=F32),
            array(SHARD, C, dtype=F32),
        ],
        [
            VMEM((TAPS, BASES, SHARD), F32),
            VMEM((SHARD, C), F32),
            VMEM((SHARD, C), F32),
            VMEM((TAPS, SHARD, C), F32),
            VMEM((SMALL, C), F32),
            VMEM((TAPS + 1, SMALL, SHARD), F32),
            pltpu.SemaphoreType.DMA((4,)),
        ],
        (gathered, left, pick, conv_w),
        out_hbm=(0, 1, 2, 3),
    )
    return output, g_embed, g_conv, g_in, g_out.T


def solution(mesh):
    mesh = Mesh(mesh.devices.reshape(Z, X, YH, CORE, YL), ("z", "x", "yh", "core", "yl"))
    seq = ("yh", "core")
    samples = ("z", "x", "yl")
    return jax.shard_map(
        local,
        mesh=mesh,
        in_specs=(
            P(samples, seq),
            P(),
            P(None, seq, None),
            P(seq, "yl"),
            P("yl", seq),
            P(samples, seq, None),
        ),
        out_specs=(
            P(samples, seq, None),
            P(None, None, seq),
            P(None, seq, None),
            P(seq, "yl"),
            P("yl", seq),
        ),
        check_vma=False,
    )
```

```python
import jax
import jax.numpy as jnp
from jax import lax
from jax.experimental import pallas as pl
from jax.experimental.pallas import tpu as pltpu
from jax.sharding import Mesh
from jax.sharding import PartitionSpec as P

Z, X, YH, CORE, YL = 8, 4, 4, 2, 2
TAPS = 5
BASES = 4
C = 384
F = 768
ROWS = 256
HALF = 128
LENGTH = 2048
SHARD = 48
PAIRS = TAPS * BASES
ENDS = [(0, 3), (0, 4), (1, 3), (1, 4), (3, 0), (3, 1), (4, 0), (4, 1)]
END_ROW = BASES * (2 * TAPS - 1)
STEM_ROW = END_ROW + BASES * len(ENDS)
SMALL = 96
BF = jnp.bfloat16
F32 = jnp.float32
VMEM = pltpu.VMEM
LANES = [slice(128 * i, 128 * (i + 1)) for i in range(C // 128)]
GELU_C = 0.7978845608028654
GELU_A = 0.044715


def dot(a, b, dims):
    return lax.dot_general(a, b, (dims, ((), ())), preferred_element_type=F32)


def nn(a, b):
    return dot(a, b, ((1,), (0,)))


def nt(a, b):
    return dot(a, b, ((1,), (1,)))


def tn(a, b):
    return dot(a, b, ((0,), (0,)))


def iota(shape, dim):
    return lax.broadcasted_iota(jnp.int32, shape, dim)


def gelu_both(x):
    x2 = x * x
    t = jnp.tanh(GELU_C * (x + GELU_A * (x * x2)))
    half = 0.5 * (1.0 + t)
    slope = half + 0.5 * x * (1.0 - t * t) * (GELU_C * (1.0 + 3.0 * GELU_A * x2))
    return x * half, slope


def where_am_i():
    x, yh, core, yl = (lax.axis_index(name) for name in ("x", "yh", "core", "yl"))
    return x, yh, core, yl, yh * CORE + core


def stack_embed(embed_ref, scratch, top):
    for j in range(TAPS):
        scratch[top + BASES * j : top + BASES * (j + 1), :] = embed_ref[j].astype(F32)


def picker(seq):
    return (iota((C, SHARD), 0) == iota((C, SHARD), 1) + seq * SHARD).astype(BF)


def pack_kernel(
    ids_hbm, embed_hbm, conv_hbm, win_hbm, wout_hbm, out_ref,
    ids_v, embed_v, conv_v, shard_v, sems, emb, esum, tail, shard_f,
):
    x, yh, core, yl, seq = where_am_i()
    copies = [
        pltpu.make_async_copy(src, dst, sems.at[i])
        for i, (src, dst) in enumerate(
            (
                (embed_hbm, embed_v),
                (conv_hbm, conv_v),
                (win_hbm, shard_v.at[0]),
                (wout_hbm, shard_v.at[1]),
                (ids_hbm, ids_v),
            )
        )
    ]
    for copy in copies:
        copy.start()
    emb[...] = jnp.zeros_like(emb)
    esum[...] = jnp.zeros_like(esum)
    tail[...] = jnp.zeros_like(tail)
    copies[0].wait()
    stack_embed(embed_v, emb, 0)
    mine = nn(emb[...].astype(BF), picker(seq)).astype(BF)
    copies[1].wait()
    for k in range(TAPS):
        esum[PAIRS * k : PAIRS * (k + 1), :] = nn(mine, conv_v[k])[:PAIRS]
    for q in range(X * YL):
        tail[16 * q : 16 * q + 13, :] = esum[13 * q : 13 * q + 13, :]
    part = tail[pl.ds(pl.multiple_of((YL * x + yl) * 16, 16), 16), :]
    for copy in copies[2:]:
        copy.wait()
    ids = jnp.concatenate([ids_v[...].astype(F32), jnp.zeros((1, C - ROWS), F32)], axis=1)
    part = jnp.where(iota((16, C), 0) == 15, ids, part)
    shard_f[0:48, :] = shard_v[0].astype(F32)
    shard_f[48:96, :] = shard_v[1].astype(F32)
    piece = shard_f[pl.ds(pl.multiple_of(24 * x, 8), 24), :]
    piece = jnp.concatenate([piece, part], axis=0).astype(BF)
    for d in range(YH * YL):
        out_ref[d] = piece


def relay_kernel(in_ref, out_ref):
    yl = where_am_i()[3]
    got = [in_ref[p].astype(F32) for p in range(YH * YL)]
    sums = [sum(got[YL * h + half][24:40] for h in range(YH)) for half in range(YL)]
    row = iota((16, C), 0)
    for h in range(YH):
        ids = in_ref[YL * h + yl].astype(F32)[39:40]
        sums[h // 2] = jnp.where(row == 13 + h % 2, ids, sums[h // 2])
    piece = jnp.concatenate([g[:24] for g in got] + sums, axis=0).astype(BF)
    for x in range(X):
        out_ref[x] = piece


def fill_weights(core, got, win, wout):
    for h in range(YH):
        top = pl.multiple_of((CORE * h + core) * SHARD, SHARD)
        for half in range(YL):
            cols = slice(C * half, C * (half + 1))
            p = 24 * (YL * h + half)
            for ref, first in ((win, 0), (wout, 2)):
                ref[pl.ds(top, SHARD), cols] = jnp.concatenate(
                    [got[first, p : p + 24, :], got[first + 1, p : p + 24, :]], axis=0
                )


def add_e(got, ebuf):
    for x in range(X):
        for half in range(YL):
            p = 192 + 16 * half
            q = 13 * (YL * x + half)
            ebuf[q : q + 13, :] = ebuf[q : q + 13, :] + got[x, p : p + 16, :].astype(F32)[:13]


def own_kernel(
    own, embed_ref, cot_ref, win, wout, ebuf, stem, dout, dmixed, left, pick_ref, embf, rows_f, emb, leftf
):
    x_mine, yh, core, yl, seq = where_am_i()
    pick = picker(seq)
    pick_ref[...] = pick
    emb[...] = jnp.zeros_like(emb)
    stack_embed(embed_ref, emb, 0)
    mine = nn(emb[...].astype(BF), pick)
    leftf[...] = jnp.zeros_like(leftf)
    for k in range(TAPS):
        leftf[k, BASES * k : BASES * k + PAIRS, :] = mine[:PAIRS]
    for q, (k, j) in enumerate(ENDS):
        leftf[k, END_ROW + BASES * q : END_ROW + BASES * (q + 1), :] = -mine[BASES * j : BASES * (j + 1)]
    left[...] = leftf[...].astype(BF)
    fill_weights(core, own, win, wout)
    ebuf[...] = jnp.zeros_like(ebuf)
    add_e(own, ebuf)
    embf[...] = jnp.zeros_like(embf)
    stack_embed(embed_ref, embf, TAPS * PAIRS)
    stem[...] = embf[...].astype(BF)
    for lane in LANES:
        rows_f[0:ROWS, :] = cot_ref[0, :, lane].astype(F32)
        even = rows_f[pl.ds(0, HALF, stride=2), :]
        odd = rows_f[pl.ds(1, HALF, stride=2), :]
        dout[:HALF, lane] = even
        dout[HALF:, lane] = odd
        dmixed[:, lane] = (even + odd).astype(BF)


def step_kernel(
    oth, ids_ref, win_in, wout_in, ebuf_in, stem, dout, dmixed_ref,
    keep_ref, send_ref, win, wout, ebuf, h_out, act_out,
    grad_a, grad_b, small,
):
    x_mine, yh, core, yl, seq = where_am_i()
    fill_weights(1 - core, oth, win, wout)
    add_e(oth, ebuf)
    e_full = ebuf[...]
    e_hi = e_full.astype(BF)
    e_lo = (e_full - e_hi.astype(F32)).astype(BF)
    before = jnp.maximum(yh - (1 - core), 0)
    after = jnp.minimum(yh + core, YH - 1)
    near = oth[x_mine, 192:224, :].astype(F32)[:, :ROWS]
    row = iota((32, ROWS), 0)

    def ids_of(h):
        at = 16 * jnp.right_shift(h, 1) + 13 + jnp.bitwise_and(h, 1)
        line = jnp.sum(jnp.where(row == at, near, 0.0), axis=0, keepdims=True)
        return jnp.broadcast_to(line, (8, ROWS))

    id_prev = jnp.where(seq == 0, -1.0, ids_of(before)[:, 128:])
    id_next = jnp.where(seq == YH * CORE - 1, -1.0, ids_of(after)[:, :128])
    id_mid = jnp.broadcast_to(ids_ref[...].astype(F32), (8, ROWS))
    line = jnp.concatenate([id_prev, id_mid, id_next], axis=1)
    near_ids = [pltpu.roll(line, (4 - o) % 512, 1)[:, 128 : 128 + ROWS] for o in range(2 * TAPS - 1)]

    def matches(offset, base):
        rows = offset.shape[0]
        seen = jnp.full((rows, ROWS), -2.0, F32)
        for o in range(2 * TAPS - 1):
            seen = jnp.where(offset == o, jnp.concatenate([near_ids[o]] * (rows // 8), axis=0), seen)
        return seen == base.astype(F32)

    def outside(k):
        at = seq * ROWS + iota(k.shape, 1) + k - 2
        return (at < 0) | (at >= LENGTH)

    m = iota((HALF, ROWS), 0)
    k = sum((m >= PAIRS * q).astype(jnp.int32) for q in range(1, TAPS + 1))
    rest = m - PAIRS * k
    k = jnp.where(m >= PAIRS * TAPS, 2, k)
    hit = matches(k + jnp.right_shift(rest, 2), jnp.bitwise_and(rest, 3))
    hit = hit & jnp.logical_not(outside(k)) & (m < PAIRS * (TAPS + 1))
    onehot = jnp.where(hit, 1.0, 0.0).astype(BF)
    m = iota((SMALL, ROWS), 0)
    group = jnp.right_shift(m, 2)
    k = jnp.full((SMALL, ROWS), 2, jnp.int32)
    offset = jnp.where(m < END_ROW, group, group - STEM_ROW // BASES + 2)
    for q, (tap, j) in enumerate(ENDS):
        here = group == END_ROW // BASES + q
        k = jnp.where(here, tap, k)
        offset = jnp.where(here, tap + j, offset)
    ends = (m >= END_ROW) & (m < STEM_ROW)
    hit = matches(offset, jnp.bitwise_and(m, 3)) & (m < STEM_ROW + PAIRS)
    hit = hit & (jnp.logical_not(ends) | outside(k))
    small_hot = jnp.where(hit, 1.0, 0.0).astype(BF)
    src = iota((ROWS, ROWS), 0)
    dst = iota((ROWS, ROWS), 1)
    order = jnp.where(dst < HALF, 2 * dst, 2 * dst - (ROWS - 1))
    order = (src == order).astype(BF)
    onehot_t = nn(onehot, order).T.astype(BF)
    small_hot = nn(small_hot, order).astype(BF)
    z = nn(onehot_t, e_hi) + nn(onehot_t, e_lo)
    h_zero = nn(onehot_t, stem[...]).astype(BF).astype(F32)
    g_z, s_z = gelu_both(z)
    h_one = (h_zero + g_z).astype(BF).astype(F32)
    even, odd = h_one[:HALF], h_one[HALF:]
    pooled = ((even + odd) * 0.5).astype(BF).astype(F32)
    scale = lax.rsqrt(jnp.mean(pooled * pooled, axis=-1, keepdims=True) + 1e-06)
    normed = (pooled * scale).astype(BF)
    w_in = win[...]
    w_out = wout[...]
    pre = nn(normed, w_in)
    g_p, s_p = gelu_both(pre)
    act = g_p.astype(BF)
    h_out[...] = h_one
    act_out[...] = act
    dmixed = dmixed_ref[...]
    d_even, d_odd = dout[:HALF, :], dout[HALF:, :]
    dact = nn(dmixed, w_out)
    dpre = (dact * s_p).astype(BF)
    dnormed = nt(dpre, w_in)
    dpooled = scale * dnormed - pooled * (scale * scale * scale) * jnp.mean(
        dnormed * pooled, axis=-1, keepdims=True
    )
    add = dpooled * 0.5
    dh_one = jnp.concatenate([d_even + add, d_odd + add], axis=0)
    dz = (dh_one * s_z).astype(BF)
    d_hi = dh_one.astype(BF)
    d_lo = (dh_one - d_hi.astype(F32)).astype(BF)
    small[...] = jnp.where(
        iota((SMALL, C), 0) < STEM_ROW, nn(small_hot, dz), nn(small_hot, d_hi) + nn(small_hot, d_lo)
    )
    grad_a[...] = tn(normed, dpre)
    grad_b[...] = tn(dmixed, act)
    for which, ref in ((core, keep_ref), (1 - core, send_ref)):
        for x in range(X):
            grad = grad_a if x < 2 else grad_b
            for half in range(YL):
                cols = slice(C * half, C * (half + 1))
                parts = []
                for h in range(YH):
                    top = pl.multiple_of((2 * h + which) * SHARD + 24 * (x % 2), 8)
                    parts.append(grad[pl.ds(top, 24), cols])
                parts.append(small[24 * x : 24 * x + 24, :])
                ref[YL * x + half] = jnp.concatenate(parts, axis=0).astype(BF)


def output_kernel(h_one, act, wout, out_ref, rows_f):
    mixed = nt(act[...], wout[...]).astype(BF).astype(F32)
    for lane in LANES:
        rows_f[pl.ds(0, HALF, stride=2), :] = h_one[:HALF, lane] + mixed[:, lane]
        rows_f[pl.ds(1, HALF, stride=2), :] = h_one[HALF:, lane] + mixed[:, lane]
        out_ref[0, :, lane] = rows_f[0:ROWS, :].astype(BF)


def middle_kernel(in_ref, out_ref):
    total = in_ref[0].astype(F32)
    for i in range(1, X * YL):
        total = total + in_ref[i].astype(F32)
    for z in range(Z):
        for h in range(YH):
            if z < 3:
                piece = total[24 * h + 8 * z : 24 * h + 8 * z + 8]
            elif z < 6:
                piece = total[96 + 8 * (z - 3) : 96 + 8 * (z - 3) + 8]
            else:
                piece = jnp.zeros((8, C), F32)
            out_ref[YH * z + h] = piece.astype(BF)


def last_kernel(in_ref, out_ref):
    total = in_ref[0].astype(F32)
    for i in range(1, Z * YH):
        total = total + in_ref[i].astype(F32)
    total = total.astype(BF)
    for i in range(Z * X):
        out_ref[i] = total


def grads_kernel(
    in_ref, left, pick, conv_ref, gemb_hbm, gconv_hbm, gin_hbm, gout_hbm,
    gemb_v, gin_v, gout_v, gconv_v, sums, back, sems,
):
    for x in range(X):
        for z in range(3, 6):
            top = 24 * x + 8 * (z - 3)
            sums[top : top + 8, :] = in_ref[Z * x + z].astype(F32)
    small = sums[...].astype(BF)
    for k in range(TAPS):
        gconv_v[k] = tn(left[k], small)
    copies = [
        pltpu.make_async_copy(src, dst, sems.at[i])
        for i, (src, dst) in enumerate(
            ((gconv_v, gconv_hbm), (gin_v, gin_hbm), (gout_v, gout_hbm), (gemb_v, gemb_hbm))
        )
    ]
    copies[0].start()
    for k in range(TAPS):
        back[k] = nt(small, conv_ref[k])
    back[TAPS] = nn(small, pick[...])
    back[TAPS, 0:PAIRS, :] = back[TAPS, STEM_ROW : STEM_ROW + PAIRS, :] + sum(
        back[k, BASES * k : BASES * k + PAIRS, :] for k in range(TAPS)
    )
    for j in range(TAPS):
        rows = back[TAPS, BASES * j : BASES * (j + 1), :]
        for q, (k, tap) in enumerate(ENDS):
            if tap == j:
                rows = rows - back[k, END_ROW + BASES * q : END_ROW + BASES * (q + 1), :]
        gemb_v[j] = rows
    copies[3].start()
    for x in range(X):
        for z in range(3):
            top = 24 * (x % 2) + 8 * z
            (gin_v if x < 2 else gout_v)[top : top + 8, :] = in_ref[Z * x + z].astype(F32)
    copies[1].start()
    copies[2].start()
    for copy in copies:
        copy.wait()


def call(body, outs, scratch, args, hbm=False, out_hbm=(), alias={}, flops=0):
    spec = pl.BlockSpec(memory_space=VMEM)
    far = pl.BlockSpec(memory_space=pltpu.HBM)
    if hbm:
        args = tuple(pltpu.with_memory_space_constraint(a, pltpu.HBM) for a in args)
    many = isinstance(outs, list)
    moved = sum(a.size * a.dtype.itemsize for a in args)
    return pl.pallas_call(
        body,
        out_shape=outs,
        in_specs=[far if hbm else spec] * len(args),
        out_specs=[far if i in out_hbm else spec for i in range(len(outs))] if many else spec,
        scratch_shapes=scratch,
        input_output_aliases=alias,
        compiler_params=pltpu.CompilerParams(vmem_limit_bytes=48 * 1024 * 1024),
        cost_estimate=pl.CostEstimate(flops=flops, bytes_accessed=moved, transcendentals=0),
        name=body.__name__,
    )(*args)


def array(*shape, dtype=BF):
    return jax.ShapeDtypeStruct(shape, dtype)


def exchange(pieces, axes):
    return lax.all_to_all(pieces, axes, 0, 0, tiled=True)


def local(bases, embed, conv_w, w_in, w_out, cotangent):
    packed = call(
        pack_kernel,
        array(YH * YL, 40, C),
        [
            VMEM((1, ROWS), jnp.int32),
            VMEM((TAPS, BASES, C), BF),
            VMEM((TAPS, SHARD, C), BF),
            VMEM((2, SHARD, C), BF),
            pltpu.SemaphoreType.DMA((5,)),
            VMEM((24, C), F32),
            VMEM((112, C), F32),
            VMEM((128, C), F32),
            VMEM((96, C), F32),
        ],
        (bases, embed, conv_w, w_in, w_out.T),
        hbm=True,
    )
    quarters = call(relay_kernel, array(X, 224, C), [], (exchange(packed, ("yh", "yl")),))
    swap = [(0, 1), (1, 0)]
    mine = exchange(quarters, "x")
    other = lax.ppermute(mine, "core", swap)
    win, wout, e_own, stem, dout, dmixed, left, pick = call(
        own_kernel,
        [
            array(C, F),
            array(C, F),
            array(128, C, dtype=F32),
            array(128, C),
            array(ROWS, C, dtype=F32),
            array(HALF, C),
            array(TAPS, SMALL, SHARD),
            array(C, SHARD),
        ],
        [VMEM((128, C), F32), VMEM((ROWS + 8, 128), F32), VMEM((24, C), F32), VMEM((TAPS, SMALL, SHARD), F32)],
        (mine, embed, cotangent),
        flops=10**8,
    )
    keep, send, win, wout, e_own, h_one, act = call(
        step_kernel,
        [
            array(X * YL, 120, C),
            array(X * YL, 120, C),
            array(C, F),
            array(C, F),
            array(128, C, dtype=F32),
            array(ROWS, C, dtype=F32),
            array(HALF, F),
        ],
        [VMEM((C, F), F32), VMEM((C, F), F32), VMEM((SMALL, C), F32)],
        (other, bases, win, wout, e_own, stem, dout, dmixed),
        alias={2: 2, 3: 3, 4: 4},
        flops=10**9,
    )
    came = lax.ppermute(send, "core", swap)
    output = call(output_kernel, array(1, ROWS, C), [VMEM((ROWS + 8, 128), F32)], (h_one, act, wout), flops=10**8)
    came, output = lax.optimization_barrier((came, output))
    pairs = (keep.astype(F32) + came.astype(F32)).astype(BF)
    pieces = call(middle_kernel, array(Z * YH, 8, C), [], (exchange(pairs, ("x", "yl")),))
    copies = call(last_kernel, array(Z * X, 8, C), [], (exchange(pieces, ("z", "yh")),))
    gathered = exchange(copies, ("x", "z"))
    g_embed, g_conv, g_in, g_out = call(
        grads_kernel,
        [
            array(TAPS, BASES, SHARD, dtype=F32),
            array(TAPS, SHARD, C, dtype=F32),
            array(SHARD, C, dtype=F32),
            array(SHARD, C, dtype=F32),
        ],
        [
            VMEM((TAPS, BASES, SHARD), F32),
            VMEM((SHARD, C), F32),
            VMEM((SHARD, C), F32),
            VMEM((TAPS, SHARD, C), F32),
            VMEM((SMALL, C), F32),
            VMEM((TAPS + 1, SMALL, SHARD), F32),
            pltpu.SemaphoreType.DMA((4,)),
        ],
        (gathered, left, pick, conv_w),
        out_hbm=(0, 1, 2, 3),
    )
    return output, g_embed, g_conv, g_in, g_out.T


def solution(mesh):
    mesh = Mesh(mesh.devices.reshape(Z, X, YH, CORE, YL), ("z", "x", "yh", "core", "yl"))
    seq = ("yh", "core")
    samples = ("z", "x", "yl")
    return jax.shard_map(
        local,
        mesh=mesh,
        in_specs=(
            P(samples, seq),
            P(),
            P(None, seq, None),
            P(seq, "yl"),
            P("yl", seq),
            P(samples, seq, None),
        ),
        out_specs=(
            P(samples, seq, None),
            P(None, None, seq),
            P(None, seq, None),
            P(seq, "yl"),
            P("yl", seq),
        ),
        check_vma=False,
    )
```

```python
import jax
import jax.numpy as jnp
from jax import lax
from jax.experimental import pallas as pl
from jax.experimental.pallas import tpu as pltpu
from jax.sharding import Mesh
from jax.sharding import PartitionSpec as P

Z, X, YH, CORE, YL = 8, 4, 4, 2, 2
TAPS = 5
BASES = 4
C = 384
F = 768
ROWS = 256
HALF = 128
LENGTH = 2048
SHARD = 48
PAIRS = TAPS * BASES
ENDS = [(0, 3), (0, 4), (1, 3), (1, 4), (3, 0), (3, 1), (4, 0), (4, 1)]
END_ROW = BASES * (2 * TAPS - 1)
STEM_ROW = END_ROW + BASES * len(ENDS)
SMALL = 96
BF = jnp.bfloat16
F32 = jnp.float32
VMEM = pltpu.VMEM
LANES = [slice(128 * i, 128 * (i + 1)) for i in range(C // 128)]
GELU_C = 0.7978845608028654
GELU_A = 0.044715


def dot(a, b, dims):
    return lax.dot_general(a, b, (dims, ((), ())), preferred_element_type=F32)


def nn(a, b):
    return dot(a, b, ((1,), (0,)))


def nt(a, b):
    return dot(a, b, ((1,), (1,)))


def tn(a, b):
    return dot(a, b, ((0,), (0,)))


def iota(shape, dim):
    return lax.broadcasted_iota(jnp.int32, shape, dim)


def gelu_both(x):
    x2 = x * x
    t = jnp.tanh(GELU_C * (x + GELU_A * (x * x2)))
    half = 0.5 * (1.0 + t)
    slope = half + 0.5 * x * (1.0 - t * t) * (GELU_C * (1.0 + 3.0 * GELU_A * x2))
    return x * half, slope


def where_am_i():
    x, yh, core, yl = (lax.axis_index(name) for name in ("x", "yh", "core", "yl"))
    return x, yh, core, yl, yh * CORE + core


def stack_embed(embed_ref, scratch, top):
    for j in range(TAPS):
        scratch[top + BASES * j : top + BASES * (j + 1), :] = embed_ref[j].astype(F32)


def picker(seq):
    return (iota((C, SHARD), 0) == iota((C, SHARD), 1) + seq * SHARD).astype(BF)


def pack_kernel(
    ids_hbm, embed_hbm, conv_hbm, win_hbm, wout_hbm, out_ref,
    ids_v, embed_v, conv_v, shard_v, sems, emb, esum, tail, shard_f,
):
    x, yh, core, yl, seq = where_am_i()
    copies = [
        pltpu.make_async_copy(src, dst, sems.at[i])
        for i, (src, dst) in enumerate(
            (
                (embed_hbm, embed_v),
                (conv_hbm, conv_v),
                (win_hbm, shard_v.at[0]),
                (wout_hbm, shard_v.at[1]),
                (ids_hbm, ids_v),
            )
        )
    ]
    for copy in copies:
        copy.start()
    emb[...] = jnp.zeros_like(emb)
    esum[...] = jnp.zeros_like(esum)
    tail[...] = jnp.zeros_like(tail)
    copies[0].wait()
    stack_embed(embed_v, emb, 0)
    mine = nn(emb[...].astype(BF), picker(seq)).astype(BF)
    copies[1].wait()
    for k in range(TAPS):
        esum[PAIRS * k : PAIRS * (k + 1), :] = nn(mine, conv_v[k])[:PAIRS]
    for q in range(X * YL):
        tail[16 * q : 16 * q + 13, :] = esum[13 * q : 13 * q + 13, :]
    part = tail[pl.ds(pl.multiple_of((YL * x + yl) * 16, 16), 16), :]
    for copy in copies[2:]:
        copy.wait()
    ids = jnp.concatenate([ids_v[...].astype(F32), jnp.zeros((1, C - ROWS), F32)], axis=1)
    part = jnp.where(iota((16, C), 0) == 15, ids, part)
    shard_f[0:48, :] = shard_v[0].astype(F32)
    shard_f[48:96, :] = shard_v[1].astype(F32)
    piece = shard_f[pl.ds(pl.multiple_of(24 * x, 8), 24), :]
    piece = jnp.concatenate([piece, part], axis=0).astype(BF)
    for d in range(YH * YL):
        out_ref[d] = piece


def relay_kernel(in_ref, out_ref):
    yl = where_am_i()[3]
    got = [in_ref[p].astype(F32) for p in range(YH * YL)]
    sums = [sum(got[YL * h + half][24:40] for h in range(YH)) for half in range(YL)]
    row = iota((16, C), 0)
    for h in range(YH):
        ids = in_ref[YL * h + yl].astype(F32)[39:40]
        sums[h // 2] = jnp.where(row == 13 + h % 2, ids, sums[h // 2])
    piece = jnp.concatenate([g[:24] for g in got] + sums, axis=0).astype(BF)
    for x in range(X):
        out_ref[x] = piece


def fill_weights(core, got, win, wout):
    for h in range(YH):
        top = pl.multiple_of((CORE * h + core) * SHARD, SHARD)
        for half in range(YL):
            cols = slice(C * half, C * (half + 1))
            p = 24 * (YL * h + half)
            for ref, first in ((win, 0), (wout, 2)):
                ref[pl.ds(top, SHARD), cols] = jnp.concatenate(
                    [got[first, p : p + 24, :], got[first + 1, p : p + 24, :]], axis=0
                )


def add_e(got, ebuf):
    for x in range(X):
        for half in range(YL):
            p = 192 + 16 * half
            q = 13 * (YL * x + half)
            ebuf[q : q + 13, :] = ebuf[q : q + 13, :] + got[x, p : p + 16, :].astype(F32)[:13]


def own_kernel(
    own, embed_ref, cot_ref, win, wout, ebuf, stem, dout, dmixed, left, pick_ref, embf, rows_f, emb, leftf
):
    x_mine, yh, core, yl, seq = where_am_i()
    pick = picker(seq)
    pick_ref[...] = pick
    emb[...] = jnp.zeros_like(emb)
    stack_embed(embed_ref, emb, 0)
    mine = nn(emb[...].astype(BF), pick)
    leftf[...] = jnp.zeros_like(leftf)
    for k in range(TAPS):
        leftf[k, BASES * k : BASES * k + PAIRS, :] = mine[:PAIRS]
    for q, (k, j) in enumerate(ENDS):
        leftf[k, END_ROW + BASES * q : END_ROW + BASES * (q + 1), :] = -mine[BASES * j : BASES * (j + 1)]
    left[...] = leftf[...].astype(BF)
    fill_weights(core, own, win, wout)
    ebuf[...] = jnp.zeros_like(ebuf)
    add_e(own, ebuf)
    embf[...] = jnp.zeros_like(embf)
    stack_embed(embed_ref, embf, TAPS * PAIRS)
    stem[...] = embf[...].astype(BF)
    for lane in LANES:
        rows_f[0:ROWS, :] = cot_ref[0, :, lane].astype(F32)
        even = rows_f[pl.ds(0, HALF, stride=2), :]
        odd = rows_f[pl.ds(1, HALF, stride=2), :]
        dout[:HALF, lane] = even
        dout[HALF:, lane] = odd
        dmixed[:, lane] = (even + odd).astype(BF)


def step_kernel(
    oth, ids_ref, win_in, wout_in, ebuf_in, stem, dout, dmixed_ref,
    keep_ref, send_ref, win, wout, ebuf, h_out, act_out,
    grad_a, grad_b, small,
):
    x_mine, yh, core, yl, seq = where_am_i()
    fill_weights(1 - core, oth, win, wout)
    add_e(oth, ebuf)
    e_full = ebuf[...]
    e_hi = e_full.astype(BF)
    e_lo = (e_full - e_hi.astype(F32)).astype(BF)
    before = jnp.maximum(yh - (1 - core), 0)
    after = jnp.minimum(yh + core, YH - 1)
    near = oth[x_mine, 192:224, :].astype(F32)[:, :ROWS]
    row = iota((32, ROWS), 0)

    def ids_of(h):
        at = 16 * jnp.right_shift(h, 1) + 13 + jnp.bitwise_and(h, 1)
        line = jnp.sum(jnp.where(row == at, near, 0.0), axis=0, keepdims=True)
        return jnp.broadcast_to(line, (8, ROWS))

    id_prev = jnp.where(seq == 0, -1.0, ids_of(before)[:, 128:])
    id_next = jnp.where(seq == YH * CORE - 1, -1.0, ids_of(after)[:, :128])
    id_mid = jnp.broadcast_to(ids_ref[...].astype(F32), (8, ROWS))
    line = jnp.concatenate([id_prev, id_mid, id_next], axis=1)
    near_ids = [pltpu.roll(line, (4 - o) % 512, 1)[:, 128 : 128 + ROWS] for o in range(2 * TAPS - 1)]

    def matches(offset, base):
        rows = offset.shape[0]
        seen = jnp.full((rows, ROWS), -2.0, F32)
        for o in range(2 * TAPS - 1):
            seen = jnp.where(offset == o, jnp.concatenate([near_ids[o]] * (rows // 8), axis=0), seen)
        return seen == base.astype(F32)

    def outside(k):
        at = seq * ROWS + iota(k.shape, 1) + k - 2
        return (at < 0) | (at >= LENGTH)

    m = iota((HALF, ROWS), 0)
    k = sum((m >= PAIRS * q).astype(jnp.int32) for q in range(1, TAPS + 1))
    rest = m - PAIRS * k
    k = jnp.where(m >= PAIRS * TAPS, 2, k)
    hit = matches(k + jnp.right_shift(rest, 2), jnp.bitwise_and(rest, 3))
    hit = hit & jnp.logical_not(outside(k)) & (m < PAIRS * (TAPS + 1))
    onehot = jnp.where(hit, 1.0, 0.0).astype(BF)
    m = iota((SMALL, ROWS), 0)
    group = jnp.right_shift(m, 2)
    k = jnp.full((SMALL, ROWS), 2, jnp.int32)
    offset = jnp.where(m < END_ROW, group, group - STEM_ROW // BASES + 2)
    for q, (tap, j) in enumerate(ENDS):
        here = group == END_ROW // BASES + q
        k = jnp.where(here, tap, k)
        offset = jnp.where(here, tap + j, offset)
    ends = (m >= END_ROW) & (m < STEM_ROW)
    hit = matches(offset, jnp.bitwise_and(m, 3)) & (m < STEM_ROW + PAIRS)
    hit = hit & (jnp.logical_not(ends) | outside(k))
    small_hot = jnp.where(hit, 1.0, 0.0).astype(BF)
    src = iota((ROWS, ROWS), 0)
    dst = iota((ROWS, ROWS), 1)
    order = jnp.where(dst < HALF, 2 * dst, 2 * dst - (ROWS - 1))
    order = (src == order).astype(BF)
    onehot_t = nn(onehot, order).T.astype(BF)
    small_hot = nn(small_hot, order).astype(BF)
    z = nn(onehot_t, e_hi) + nn(onehot_t, e_lo)
    h_zero = nn(onehot_t, stem[...]).astype(BF).astype(F32)
    g_z, s_z = gelu_both(z)
    h_one = (h_zero + g_z).astype(BF).astype(F32)
    even, odd = h_one[:HALF], h_one[HALF:]
    pooled = ((even + odd) * 0.5).astype(BF).astype(F32)
    scale = lax.rsqrt(jnp.mean(pooled * pooled, axis=-1, keepdims=True) + 1e-06)
    normed = (pooled * scale).astype(BF)
    w_in = win[...]
    w_out = wout[...]
    pre = nn(normed, w_in)
    g_p, s_p = gelu_both(pre)
    act = g_p.astype(BF)
    h_out[...] = h_one
    act_out[...] = act
    dmixed = dmixed_ref[...]
    d_even, d_odd = dout[:HALF, :], dout[HALF:, :]
    dact = nn(dmixed, w_out)
    dpre = (dact * s_p).astype(BF)
    dnormed = nt(dpre, w_in)
    dpooled = scale * dnormed - pooled * (scale * scale * scale) * jnp.mean(
        dnormed * pooled, axis=-1, keepdims=True
    )
    add = dpooled * 0.5
    dh_one = jnp.concatenate([d_even + add, d_odd + add], axis=0)
    dz = (dh_one * s_z).astype(BF)
    d_hi = dh_one.astype(BF)
    d_lo = (dh_one - d_hi.astype(F32)).astype(BF)
    small[...] = jnp.where(
        iota((SMALL, C), 0) < STEM_ROW, nn(small_hot, dz), nn(small_hot, d_hi) + nn(small_hot, d_lo)
    )
    grad_a[...] = tn(normed, dpre)
    grad_b[...] = tn(dmixed, act)
    for which, ref in ((core, keep_ref), (1 - core, send_ref)):
        for x in range(X):
            grad = grad_a if x < 2 else grad_b
            for half in range(YL):
                cols = slice(C * half, C * (half + 1))
                parts = []
                for h in range(YH):
                    top = pl.multiple_of((2 * h + which) * SHARD + 24 * (x % 2), 8)
                    parts.append(grad[pl.ds(top, 24), cols])
                parts.append(small[24 * x : 24 * x + 24, :])
                ref[YL * x + half] = jnp.concatenate(parts, axis=0).astype(BF)


def output_kernel(h_one, act, wout, out_ref, rows_f):
    mixed = nt(act[...], wout[...]).astype(BF).astype(F32)
    for lane in LANES:
        rows_f[pl.ds(0, HALF, stride=2), :] = h_one[:HALF, lane] + mixed[:, lane]
        rows_f[pl.ds(1, HALF, stride=2), :] = h_one[HALF:, lane] + mixed[:, lane]
        out_ref[0, :, lane] = rows_f[0:ROWS, :].astype(BF)


def middle_kernel(in_ref, out_ref):
    total = in_ref[0].astype(F32)
    for i in range(1, X * YL):
        total = total + in_ref[i].astype(F32)
    for z in range(Z):
        for h in range(YH):
            if z < 3:
                piece = total[24 * h + 8 * z : 24 * h + 8 * z + 8]
            elif z < 6:
                piece = total[96 + 8 * (z - 3) : 96 + 8 * (z - 3) + 8]
            else:
                piece = jnp.zeros((8, C), F32)
            out_ref[YH * z + h] = piece.astype(BF)


def last_kernel(in_ref, out_ref):
    total = in_ref[0].astype(F32)
    for i in range(1, Z * YH):
        total = total + in_ref[i].astype(F32)
    total = total.astype(BF)
    for i in range(Z * X):
        out_ref[i] = total


def grads_kernel(
    in_ref, left, pick, conv_ref, gemb_hbm, gconv_hbm, gin_hbm, gout_hbm,
    gemb_v, gin_v, gout_v, gconv_v, sums, back, sems,
):
    for x in range(X):
        for z in range(3):
            top = 24 * (x % 2) + 8 * z
            (gin_v if x < 2 else gout_v)[top : top + 8, :] = in_ref[Z * x + z].astype(F32)
    pairs = [(gin_v, gin_hbm), (gout_v, gout_hbm)]
    pairs += [(gconv_v.at[k], gconv_hbm.at[k]) for k in range(TAPS)] + [(gemb_v, gemb_hbm)]
    copies = [pltpu.make_async_copy(src, dst, sems.at[i]) for i, (src, dst) in enumerate(pairs)]
    copies[0].start()
    copies[1].start()
    for x in range(X):
        for z in range(3, 6):
            top = 24 * x + 8 * (z - 3)
            sums[top : top + 8, :] = in_ref[Z * x + z].astype(F32)
    small = sums[...].astype(BF)
    for k in range(TAPS):
        gconv_v[k] = tn(left[k], small)
        copies[2 + k].start()
    for k in range(TAPS):
        back[k] = nt(small, conv_ref[k])
    back[TAPS] = nn(small, pick[...])
    back[TAPS, 0:PAIRS, :] = back[TAPS, STEM_ROW : STEM_ROW + PAIRS, :] + sum(
        back[k, BASES * k : BASES * k + PAIRS, :] for k in range(TAPS)
    )
    for j in range(TAPS):
        rows = back[TAPS, BASES * j : BASES * (j + 1), :]
        for q, (k, tap) in enumerate(ENDS):
            if tap == j:
                rows = rows - back[k, END_ROW + BASES * q : END_ROW + BASES * (q + 1), :]
        gemb_v[j] = rows
    copies[-1].start()
    for copy in copies:
        copy.wait()


def call(body, outs, scratch, args, hbm=False, out_hbm=(), alias={}, flops=0):
    spec = pl.BlockSpec(memory_space=VMEM)
    far = pl.BlockSpec(memory_space=pltpu.HBM)
    if hbm:
        args = tuple(pltpu.with_memory_space_constraint(a, pltpu.HBM) for a in args)
    many = isinstance(outs, list)
    moved = sum(a.size * a.dtype.itemsize for a in args)
    return pl.pallas_call(
        body,
        out_shape=outs,
        in_specs=[far if hbm else spec] * len(args),
        out_specs=[far if i in out_hbm else spec for i in range(len(outs))] if many else spec,
        scratch_shapes=scratch,
        input_output_aliases=alias,
        compiler_params=pltpu.CompilerParams(vmem_limit_bytes=48 * 1024 * 1024),
        cost_estimate=pl.CostEstimate(flops=flops, bytes_accessed=moved, transcendentals=0),
        name=body.__name__,
    )(*args)


def array(*shape, dtype=BF):
    return jax.ShapeDtypeStruct(shape, dtype)


def exchange(pieces, axes):
    return lax.all_to_all(pieces, axes, 0, 0, tiled=True)


def local(bases, embed, conv_w, w_in, w_out, cotangent):
    packed = call(
        pack_kernel,
        array(YH * YL, 40, C),
        [
            VMEM((1, ROWS), jnp.int32),
            VMEM((TAPS, BASES, C), BF),
            VMEM((TAPS, SHARD, C), BF),
            VMEM((2, SHARD, C), BF),
            pltpu.SemaphoreType.DMA((5,)),
            VMEM((24, C), F32),
            VMEM((112, C), F32),
            VMEM((128, C), F32),
            VMEM((96, C), F32),
        ],
        (bases, embed, conv_w, w_in, w_out.T),
        hbm=True,
    )
    quarters = call(relay_kernel, array(X, 224, C), [], (exchange(packed, ("yh", "yl")),))
    swap = [(0, 1), (1, 0)]
    mine = exchange(quarters, "x")
    other = lax.ppermute(mine, "core", swap)
    win, wout, e_own, stem, dout, dmixed, left, pick = call(
        own_kernel,
        [
            array(C, F),
            array(C, F),
            array(128, C, dtype=F32),
            array(128, C),
            array(ROWS, C, dtype=F32),
            array(HALF, C),
            array(TAPS, SMALL, SHARD),
            array(C, SHARD),
        ],
        [VMEM((128, C), F32), VMEM((ROWS + 8, 128), F32), VMEM((24, C), F32), VMEM((TAPS, SMALL, SHARD), F32)],
        (mine, embed, cotangent),
        flops=10**8,
    )
    keep, send, win, wout, e_own, h_one, act = call(
        step_kernel,
        [
            array(X * YL, 120, C),
            array(X * YL, 120, C),
            array(C, F),
            array(C, F),
            array(128, C, dtype=F32),
            array(ROWS, C, dtype=F32),
            array(HALF, F),
        ],
        [VMEM((C, F), F32), VMEM((C, F), F32), VMEM((SMALL, C), F32)],
        (other, bases, win, wout, e_own, stem, dout, dmixed),
        alias={2: 2, 3: 3, 4: 4},
        flops=10**9,
    )
    came = lax.ppermute(send, "core", swap)
    output = call(output_kernel, array(1, ROWS, C), [VMEM((ROWS + 8, 128), F32)], (h_one, act, wout), flops=10**8)
    came, output = lax.optimization_barrier((came, output))
    pairs = (keep.astype(F32) + came.astype(F32)).astype(BF)
    pieces = call(middle_kernel, array(Z * YH, 8, C), [], (exchange(pairs, ("x", "yl")),))
    copies = call(last_kernel, array(Z * X, 8, C), [], (exchange(pieces, ("z", "yh")),))
    gathered = exchange(copies, ("x", "z"))
    g_embed, g_conv, g_in, g_out = call(
        grads_kernel,
        [
            array(TAPS, BASES, SHARD, dtype=F32),
            array(TAPS, SHARD, C, dtype=F32),
            array(SHARD, C, dtype=F32),
            array(SHARD, C, dtype=F32),
        ],
        [
            VMEM((TAPS, BASES, SHARD), F32),
            VMEM((SHARD, C), F32),
            VMEM((SHARD, C), F32),
            VMEM((TAPS, SHARD, C), F32),
            VMEM((SMALL, C), F32),
            VMEM((TAPS + 1, SMALL, SHARD), F32),
            pltpu.SemaphoreType.DMA((8,)),
        ],
        (gathered, left, pick, conv_w),
        out_hbm=(0, 1, 2, 3),
    )
    return output, g_embed, g_conv, g_in, g_out.T


def solution(mesh):
    mesh = Mesh(mesh.devices.reshape(Z, X, YH, CORE, YL), ("z", "x", "yh", "core", "yl"))
    seq = ("yh", "core")
    samples = ("z", "x", "yl")
    return jax.shard_map(
        local,
        mesh=mesh,
        in_specs=(
            P(samples, seq),
            P(),
            P(None, seq, None),
            P(seq, "yl"),
            P("yl", seq),
            P(samples, seq, None),
        ),
        out_specs=(
            P(samples, seq, None),
            P(None, None, seq),
            P(None, seq, None),
            P(seq, "yl"),
            P("yl", seq),
        ),
        check_vma=False,
    )
```

```python
import jax
import jax.numpy as jnp
from jax import lax
from jax.experimental import pallas as pl
from jax.experimental.pallas import tpu as pltpu
from jax.sharding import Mesh
from jax.sharding import PartitionSpec as P

Z, X, YH, CORE, YL = 8, 4, 4, 2, 2
TAPS = 5
BASES = 4
C = 384
F = 768
ROWS = 256
HALF = 128
LENGTH = 2048
SHARD = 48
PAIRS = TAPS * BASES
ENDS = [(0, 3), (0, 4), (1, 3), (1, 4), (3, 0), (3, 1), (4, 0), (4, 1)]
END_ROW = BASES * (2 * TAPS - 1)
STEM_ROW = END_ROW + BASES * len(ENDS)
SMALL = 96
BF = jnp.bfloat16
F32 = jnp.float32
VMEM = pltpu.VMEM
LANES = [slice(128 * i, 128 * (i + 1)) for i in range(C // 128)]
GELU_C = 0.7978845608028654
GELU_A = 0.044715


def dot(a, b, dims):
    return lax.dot_general(a, b, (dims, ((), ())), preferred_element_type=F32)


def nn(a, b):
    return dot(a, b, ((1,), (0,)))


def nt(a, b):
    return dot(a, b, ((1,), (1,)))


def tn(a, b):
    return dot(a, b, ((0,), (0,)))


def iota(shape, dim):
    return lax.broadcasted_iota(jnp.int32, shape, dim)


def gelu_both(x):
    x2 = x * x
    t = jnp.tanh(GELU_C * (x + GELU_A * (x * x2)))
    half = 0.5 * (1.0 + t)
    slope = half + 0.5 * x * (1.0 - t * t) * (GELU_C * (1.0 + 3.0 * GELU_A * x2))
    return x * half, slope


def where_am_i():
    x, yh, core, yl = (lax.axis_index(name) for name in ("x", "yh", "core", "yl"))
    return x, yh, core, yl, yh * CORE + core


def stack_embed(embed_ref, scratch, top):
    for j in range(TAPS):
        scratch[top + BASES * j : top + BASES * (j + 1), :] = embed_ref[j].astype(F32)


def picker(seq):
    return (iota((C, SHARD), 0) == iota((C, SHARD), 1) + seq * SHARD).astype(BF)


def pack_kernel(
    ids_hbm, embed_hbm, conv_hbm, win_hbm, wout_hbm, out_ref,
    ids_v, embed_v, conv_v, shard_v, sems, emb, esum, tail, shard_f,
):
    x, yh, core, yl, seq = where_am_i()
    copies = [
        pltpu.make_async_copy(src, dst, sems.at[i])
        for i, (src, dst) in enumerate(
            (
                (embed_hbm, embed_v),
                (conv_hbm, conv_v),
                (win_hbm, shard_v.at[0]),
                (wout_hbm, shard_v.at[1]),
                (ids_hbm, ids_v),
            )
        )
    ]
    for copy in copies:
        copy.start()
    emb[...] = jnp.zeros_like(emb)
    esum[...] = jnp.zeros_like(esum)
    tail[...] = jnp.zeros_like(tail)
    copies[0].wait()
    stack_embed(embed_v, emb, 0)
    mine = nn(emb[...].astype(BF), picker(seq)).astype(BF)
    for copy in copies[2:]:
        copy.wait()
    shard_f[0:48, :] = shard_v[0].astype(F32)
    shard_f[48:96, :] = shard_v[1].astype(F32)
    piece = shard_f[pl.ds(pl.multiple_of(24 * x, 8), 24), :]
    copies[1].wait()
    for k in range(TAPS):
        esum[PAIRS * k : PAIRS * (k + 1), :] = nn(mine, conv_v[k])[:PAIRS]
    for q in range(X * YL):
        tail[16 * q : 16 * q + 13, :] = esum[13 * q : 13 * q + 13, :]
    part = tail[pl.ds(pl.multiple_of((YL * x + yl) * 16, 16), 16), :]
    ids = jnp.concatenate([ids_v[...].astype(F32), jnp.zeros((1, C - ROWS), F32)], axis=1)
    part = jnp.where(iota((16, C), 0) == 15, ids, part)
    piece = jnp.concatenate([piece, part], axis=0).astype(BF)
    for d in range(YH * YL):
        out_ref[d] = piece


def relay_kernel(in_ref, out_ref):
    yl = where_am_i()[3]
    got = [in_ref[p].astype(F32) for p in range(YH * YL)]
    sums = [sum(got[YL * h + half][24:40] for h in range(YH)) for half in range(YL)]
    row = iota((16, C), 0)
    for h in range(YH):
        ids = in_ref[YL * h + yl].astype(F32)[39:40]
        sums[h // 2] = jnp.where(row == 13 + h % 2, ids, sums[h // 2])
    piece = jnp.concatenate([g[:24] for g in got] + sums, axis=0).astype(BF)
    for x in range(X):
        out_ref[x] = piece


def fill_weights(core, got, win, wout):
    for h in range(YH):
        top = pl.multiple_of((CORE * h + core) * SHARD, SHARD)
        for half in range(YL):
            cols = slice(C * half, C * (half + 1))
            p = 24 * (YL * h + half)
            for ref, first in ((win, 0), (wout, 2)):
                ref[pl.ds(top, SHARD), cols] = jnp.concatenate(
                    [got[first, p : p + 24, :], got[first + 1, p : p + 24, :]], axis=0
                )


def add_e(got, ebuf):
    for x in range(X):
        for half in range(YL):
            p = 192 + 16 * half
            q = 13 * (YL * x + half)
            ebuf[q : q + 13, :] = ebuf[q : q + 13, :] + got[x, p : p + 16, :].astype(F32)[:13]


def own_kernel(
    own, embed_ref, cot_ref, win, wout, ebuf, stem, dout, dmixed, left, pick_ref, embf, rows_f, emb, leftf
):
    x_mine, yh, core, yl, seq = where_am_i()
    pick = picker(seq)
    pick_ref[...] = pick
    emb[...] = jnp.zeros_like(emb)
    stack_embed(embed_ref, emb, 0)
    mine = nn(emb[...].astype(BF), pick)
    leftf[...] = jnp.zeros_like(leftf)
    for k in range(TAPS):
        leftf[k, BASES * k : BASES * k + PAIRS, :] = mine[:PAIRS]
    for q, (k, j) in enumerate(ENDS):
        leftf[k, END_ROW + BASES * q : END_ROW + BASES * (q + 1), :] = -mine[BASES * j : BASES * (j + 1)]
    left[...] = leftf[...].astype(BF)
    fill_weights(core, own, win, wout)
    ebuf[...] = jnp.zeros_like(ebuf)
    add_e(own, ebuf)
    embf[...] = jnp.zeros_like(embf)
    stack_embed(embed_ref, embf, TAPS * PAIRS)
    stem[...] = embf[...].astype(BF)
    for lane in LANES:
        rows_f[0:ROWS, :] = cot_ref[0, :, lane].astype(F32)
        even = rows_f[pl.ds(0, HALF, stride=2), :]
        odd = rows_f[pl.ds(1, HALF, stride=2), :]
        dout[:HALF, lane] = even
        dout[HALF:, lane] = odd
        dmixed[:, lane] = (even + odd).astype(BF)


def step_kernel(
    oth, ids_ref, win_in, wout_in, ebuf_in, stem, dout, dmixed_ref,
    keep_ref, send_ref, win, wout, ebuf, h_out, act_out,
    grad_a, grad_b, small,
):
    x_mine, yh, core, yl, seq = where_am_i()
    fill_weights(1 - core, oth, win, wout)
    add_e(oth, ebuf)
    e_full = ebuf[...]
    e_hi = e_full.astype(BF)
    e_lo = (e_full - e_hi.astype(F32)).astype(BF)
    before = jnp.maximum(yh - (1 - core), 0)
    after = jnp.minimum(yh + core, YH - 1)
    near = oth[x_mine, 192:224, :].astype(F32)[:, :ROWS]
    row = iota((32, ROWS), 0)

    def ids_of(h):
        at = 16 * jnp.right_shift(h, 1) + 13 + jnp.bitwise_and(h, 1)
        line = jnp.sum(jnp.where(row == at, near, 0.0), axis=0, keepdims=True)
        return jnp.broadcast_to(line, (8, ROWS))

    id_prev = jnp.where(seq == 0, -1.0, ids_of(before)[:, 128:])
    id_next = jnp.where(seq == YH * CORE - 1, -1.0, ids_of(after)[:, :128])
    id_mid = jnp.broadcast_to(ids_ref[...].astype(F32), (8, ROWS))
    line = jnp.concatenate([id_prev, id_mid, id_next], axis=1)
    near_ids = [pltpu.roll(line, (4 - o) % 512, 1)[:, 128 : 128 + ROWS] for o in range(2 * TAPS - 1)]

    def matches(offset, base):
        rows = offset.shape[0]
        seen = jnp.full((rows, ROWS), -2.0, F32)
        for o in range(2 * TAPS - 1):
            seen = jnp.where(offset == o, jnp.concatenate([near_ids[o]] * (rows // 8), axis=0), seen)
        return seen == base.astype(F32)

    def outside(k):
        at = seq * ROWS + iota(k.shape, 1) + k - 2
        return (at < 0) | (at >= LENGTH)

    m = iota((HALF, ROWS), 0)
    k = sum((m >= PAIRS * q).astype(jnp.int32) for q in range(1, TAPS + 1))
    rest = m - PAIRS * k
    k = jnp.where(m >= PAIRS * TAPS, 2, k)
    hit = matches(k + jnp.right_shift(rest, 2), jnp.bitwise_and(rest, 3))
    hit = hit & jnp.logical_not(outside(k)) & (m < PAIRS * (TAPS + 1))
    onehot = jnp.where(hit, 1.0, 0.0).astype(BF)
    m = iota((SMALL, ROWS), 0)
    group = jnp.right_shift(m, 2)
    k = jnp.full((SMALL, ROWS), 2, jnp.int32)
    offset = jnp.where(m < END_ROW, group, group - STEM_ROW // BASES + 2)
    for q, (tap, j) in enumerate(ENDS):
        here = group == END_ROW // BASES + q
        k = jnp.where(here, tap, k)
        offset = jnp.where(here, tap + j, offset)
    ends = (m >= END_ROW) & (m < STEM_ROW)
    hit = matches(offset, jnp.bitwise_and(m, 3)) & (m < STEM_ROW + PAIRS)
    hit = hit & (jnp.logical_not(ends) | outside(k))
    small_hot = jnp.where(hit, 1.0, 0.0).astype(BF)
    src = iota((ROWS, ROWS), 0)
    dst = iota((ROWS, ROWS), 1)
    order = jnp.where(dst < HALF, 2 * dst, 2 * dst - (ROWS - 1))
    order = (src == order).astype(BF)
    onehot_t = nn(onehot, order).T.astype(BF)
    small_hot = nn(small_hot, order).astype(BF)
    z = nn(onehot_t, e_hi) + nn(onehot_t, e_lo)
    h_zero = nn(onehot_t, stem[...]).astype(BF).astype(F32)
    g_z, s_z = gelu_both(z)
    h_one = (h_zero + g_z).astype(BF).astype(F32)
    even, odd = h_one[:HALF], h_one[HALF:]
    pooled = ((even + odd) * 0.5).astype(BF).astype(F32)
    scale = lax.rsqrt(jnp.mean(pooled * pooled, axis=-1, keepdims=True) + 1e-06)
    normed = (pooled * scale).astype(BF)
    w_in = win[...]
    w_out = wout[...]
    pre = nn(normed, w_in)
    g_p, s_p = gelu_both(pre)
    act = g_p.astype(BF)
    h_out[...] = h_one
    act_out[...] = act
    dmixed = dmixed_ref[...]
    d_even, d_odd = dout[:HALF, :], dout[HALF:, :]
    dact = nn(dmixed, w_out)
    dpre = (dact * s_p).astype(BF)
    dnormed = nt(dpre, w_in)
    dpooled = scale * dnormed - pooled * (scale * scale * scale) * jnp.mean(
        dnormed * pooled, axis=-1, keepdims=True
    )
    add = dpooled * 0.5
    dh_one = jnp.concatenate([d_even + add, d_odd + add], axis=0)
    dz = (dh_one * s_z).astype(BF)
    d_hi = dh_one.astype(BF)
    d_lo = (dh_one - d_hi.astype(F32)).astype(BF)
    small[...] = jnp.where(
        iota((SMALL, C), 0) < STEM_ROW, nn(small_hot, dz), nn(small_hot, d_hi) + nn(small_hot, d_lo)
    )
    grad_a[...] = tn(normed, dpre)
    grad_b[...] = tn(dmixed, act)
    for which, ref in ((core, keep_ref), (1 - core, send_ref)):
        for x in range(X):
            grad = grad_a if x < 2 else grad_b
            for half in range(YL):
                cols = slice(C * half, C * (half + 1))
                parts = []
                for h in range(YH):
                    top = pl.multiple_of((2 * h + which) * SHARD + 24 * (x % 2), 8)
                    parts.append(grad[pl.ds(top, 24), cols])
                parts.append(small[24 * x : 24 * x + 24, :])
                ref[YL * x + half] = jnp.concatenate(parts, axis=0).astype(BF)


def output_kernel(h_one, act, wout, out_ref, rows_f):
    mixed = nt(act[...], wout[...]).astype(BF).astype(F32)
    for lane in LANES:
        rows_f[pl.ds(0, HALF, stride=2), :] = h_one[:HALF, lane] + mixed[:, lane]
        rows_f[pl.ds(1, HALF, stride=2), :] = h_one[HALF:, lane] + mixed[:, lane]
        out_ref[0, :, lane] = rows_f[0:ROWS, :].astype(BF)


def middle_kernel(in_ref, out_ref):
    total = in_ref[0].astype(F32)
    for i in range(1, X * YL):
        total = total + in_ref[i].astype(F32)
    for z in range(Z):
        for h in range(YH):
            if z < 3:
                piece = total[24 * h + 8 * z : 24 * h + 8 * z + 8]
            elif z < 6:
                piece = total[96 + 8 * (z - 3) : 96 + 8 * (z - 3) + 8]
            else:
                piece = jnp.zeros((8, C), F32)
            out_ref[YH * z + h] = piece.astype(BF)


def last_kernel(in_ref, out_ref):
    total = in_ref[0].astype(F32)
    for i in range(1, Z * YH):
        total = total + in_ref[i].astype(F32)
    total = total.astype(BF)
    for i in range(Z * X):
        out_ref[i] = total


def grads_kernel(
    in_ref, left, pick, conv_ref, gemb_hbm, gconv_hbm, gin_hbm, gout_hbm,
    gemb_v, gin_v, gout_v, gconv_v, sums, back, sems,
):
    for x in range(X):
        for z in range(3, 6):
            top = 24 * x + 8 * (z - 3)
            sums[top : top + 8, :] = in_ref[Z * x + z].astype(F32)
    small = sums[...].astype(BF)
    for k in range(TAPS):
        gconv_v[k] = tn(left[k], small)
    copies = [
        pltpu.make_async_copy(src, dst, sems.at[i])
        for i, (src, dst) in enumerate(
            ((gconv_v, gconv_hbm), (gin_v, gin_hbm), (gout_v, gout_hbm), (gemb_v, gemb_hbm))
        )
    ]
    copies[0].start()
    for k in range(TAPS):
        back[k] = nt(small, conv_ref[k])
    back[TAPS] = nn(small, pick[...])
    back[TAPS, 0:PAIRS, :] = back[TAPS, STEM_ROW : STEM_ROW + PAIRS, :] + sum(
        back[k, BASES * k : BASES * k + PAIRS, :] for k in range(TAPS)
    )
    for j in range(TAPS):
        rows = back[TAPS, BASES * j : BASES * (j + 1), :]
        for q, (k, tap) in enumerate(ENDS):
            if tap == j:
                rows = rows - back[k, END_ROW + BASES * q : END_ROW + BASES * (q + 1), :]
        gemb_v[j] = rows
    copies[3].start()
    for x in range(X):
        for z in range(3):
            top = 24 * (x % 2) + 8 * z
            (gin_v if x < 2 else gout_v)[top : top + 8, :] = in_ref[Z * x + z].astype(F32)
    copies[1].start()
    copies[2].start()
    for copy in copies:
        copy.wait()


def call(body, outs, scratch, args, hbm=False, out_hbm=(), alias={}, flops=0):
    spec = pl.BlockSpec(memory_space=VMEM)
    far = pl.BlockSpec(memory_space=pltpu.HBM)
    if hbm:
        args = tuple(pltpu.with_memory_space_constraint(a, pltpu.HBM) for a in args)
    many = isinstance(outs, list)
    moved = sum(a.size * a.dtype.itemsize for a in args)
    return pl.pallas_call(
        body,
        out_shape=outs,
        in_specs=[far if hbm else spec] * len(args),
        out_specs=[far if i in out_hbm else spec for i in range(len(outs))] if many else spec,
        scratch_shapes=scratch,
        input_output_aliases=alias,
        compiler_params=pltpu.CompilerParams(vmem_limit_bytes=48 * 1024 * 1024),
        cost_estimate=pl.CostEstimate(flops=flops, bytes_accessed=moved, transcendentals=0),
        name=body.__name__,
    )(*args)


def array(*shape, dtype=BF):
    return jax.ShapeDtypeStruct(shape, dtype)


def exchange(pieces, axes):
    return lax.all_to_all(pieces, axes, 0, 0, tiled=True)


def local(bases, embed, conv_w, w_in, w_out, cotangent):
    packed = call(
        pack_kernel,
        array(YH * YL, 40, C),
        [
            VMEM((1, ROWS), jnp.int32),
            VMEM((TAPS, BASES, C), BF),
            VMEM((TAPS, SHARD, C), BF),
            VMEM((2, SHARD, C), BF),
            pltpu.SemaphoreType.DMA((5,)),
            VMEM((24, C), F32),
            VMEM((112, C), F32),
            VMEM((128, C), F32),
            VMEM((96, C), F32),
        ],
        (bases, embed, conv_w, w_in, w_out.T),
        hbm=True,
    )
    quarters = call(relay_kernel, array(X, 224, C), [], (exchange(packed, ("yh", "yl")),))
    swap = [(0, 1), (1, 0)]
    mine = exchange(quarters, "x")
    other = lax.ppermute(mine, "core", swap)
    win, wout, e_own, stem, dout, dmixed, left, pick = call(
        own_kernel,
        [
            array(C, F),
            array(C, F),
            array(128, C, dtype=F32),
            array(128, C),
            array(ROWS, C, dtype=F32),
            array(HALF, C),
            array(TAPS, SMALL, SHARD),
            array(C, SHARD),
        ],
        [VMEM((128, C), F32), VMEM((ROWS + 8, 128), F32), VMEM((24, C), F32), VMEM((TAPS, SMALL, SHARD), F32)],
        (mine, embed, cotangent),
        flops=10**8,
    )
    keep, send, win, wout, e_own, h_one, act = call(
        step_kernel,
        [
            array(X * YL, 120, C),
            array(X * YL, 120, C),
            array(C, F),
            array(C, F),
            array(128, C, dtype=F32),
            array(ROWS, C, dtype=F32),
            array(HALF, F),
        ],
        [VMEM((C, F), F32), VMEM((C, F), F32), VMEM((SMALL, C), F32)],
        (other, bases, win, wout, e_own, stem, dout, dmixed),
        alias={2: 2, 3: 3, 4: 4},
        flops=10**9,
    )
    came = lax.ppermute(send, "core", swap)
    output = call(output_kernel, array(1, ROWS, C), [VMEM((ROWS + 8, 128), F32)], (h_one, act, wout), flops=10**8)
    came, output = lax.optimization_barrier((came, output))
    pairs = (keep.astype(F32) + came.astype(F32)).astype(BF)
    pieces = call(middle_kernel, array(Z * YH, 8, C), [], (exchange(pairs, ("x", "yl")),))
    copies = call(last_kernel, array(Z * X, 8, C), [], (exchange(pieces, ("z", "yh")),))
    gathered = exchange(copies, ("x", "z"))
    g_embed, g_conv, g_in, g_out = call(
        grads_kernel,
        [
            array(TAPS, BASES, SHARD, dtype=F32),
            array(TAPS, SHARD, C, dtype=F32),
            array(SHARD, C, dtype=F32),
            array(SHARD, C, dtype=F32),
        ],
        [
            VMEM((TAPS, BASES, SHARD), F32),
            VMEM((SHARD, C), F32),
            VMEM((SHARD, C), F32),
            VMEM((TAPS, SHARD, C), F32),
            VMEM((SMALL, C), F32),
            VMEM((TAPS + 1, SMALL, SHARD), F32),
            pltpu.SemaphoreType.DMA((4,)),
        ],
        (gathered, left, pick, conv_w),
        out_hbm=(0, 1, 2, 3),
    )
    return output, g_embed, g_conv, g_in, g_out.T


def solution(mesh):
    mesh = Mesh(mesh.devices.reshape(Z, X, YH, CORE, YL), ("z", "x", "yh", "core", "yl"))
    seq = ("yh", "core")
    samples = ("z", "x", "yl")
    return jax.shard_map(
        local,
        mesh=mesh,
        in_specs=(
            P(samples, seq),
            P(),
            P(None, seq, None),
            P(seq, "yl"),
            P("yl", seq),
            P(samples, seq, None),
        ),
        out_specs=(
            P(samples, seq, None),
            P(None, None, seq),
            P(None, seq, None),
            P(seq, "yl"),
            P("yl", seq),
        ),
        check_vma=False,
    )
```
